32 devices in a mesh: scene: 2 (over y), pulse: 4 (over z), range: 2 (over x), rep: 2 (over core).
Axes of the slice: x: 2, y: 2, z: 4, core: 2. Of those that a mesh axis runs over, the one named last changes fastest.
Arguments:
- echo: bfloat16 [8, 64, 2, 6144], P(('scene', 'pulse'), 'rep', None, 'range'), parts along dimension 0, may hold values from -6 to 6
- chirp: bfloat16 [2, 512], replicated, may hold values from -0.1875 to 0.1875
- beam_one: int32 [2, 128], replicated, may hold values from 0 to 63, as said below
- shift_one: int32 [2, 128], replicated, may hold values from -28 to 28
- frac_one: float32 [2, 128], replicated, may hold values from 0 to 1
- base_one: float32 [2, 128], replicated, may hold values from -3.140625 to 3.140625
- beam_two: int32 [2, 256], replicated, may hold values from 0 to 127, as said below
- shift_two: int32 [2, 256], replicated, may hold values from -28 to 28
- frac_two: float32 [2, 256], replicated, may hold values from 0 to 1
- base_two: float32 [2, 256], replicated, may hold values from -3.140625 to 3.140625
Outputs:
- image: bfloat16 [2, 8, 32, 2, 6144], P('rep', ('scene', 'pulse'), None, None, 'range'), parts along dimension 1
The draws below stay inside these ranges and needn't reach their ends.
There are 2 independent parts, one for each index of `scene`. The reference program is written for one: setup_inputs(seed, part) draws one part's arguments, and reference() takes and returns one part's arrays. A program takes and returns all parts, laid end to end along the dimension named above; an argument that names none is the same for every part. Nothing has to cross between parts.
Inputs may be any that keep to these rules, and one draw needn't show every extreme that they name: beam_one[c, p] differs from p // 2 by at most 1 and lies in the same aligned block of 8 child beams as p // 2; the first and last parent beams read child beams 0 and 63. beam_two[c, p] differs from p // 2 by at most 1 and lies in the same aligned block of 16 child beams as p // 2; the first and last parent beams read child beams 0 and 127.
All inputs are finite; a program needn't handle non-finite values.
Results may differ from the reference program's by a relative error of at most 0.012.
Values may be sent and summed in bfloat16 or wider, within the bound.
No kernel may reach another device: no remote copies, remote signals or barrier semaphores. Data moves between devices by JAX's collectives and lax.ppermute only.
A program may use at most 64 MiB of HBM per device.

```python
import jax
import jax.numpy as jnp
from jax import lax

BD = 32
CH = 512
OMAX = 28
HALO = 32
SUBS = 4
B0 = 64
B1 = 128
B2 = 256
RANGE = 6144
N_PULSE = 4
N_REP = 2


def child_table(key, parent_count, half_count):
    parents = jnp.arange(parent_count).astype(jnp.int32)
    centre = parents // 2
    lowest = centre // half_count * half_count
    offsets = jax.random.randint(key, (2, parent_count), -1, 2).astype(jnp.int32)
    edges = (parents == 0) | (parents == parent_count - 1)
    offsets = jnp.where(edges[None, :], 0, offsets)
    return jnp.clip(centre[None, :] + offsets, lowest[None, :], lowest[None, :] + half_count - 1).astype(jnp.int32)


def draw_beam_one(key, part):
    return child_table(jax.random.fold_in(key, 11), B1, BD // 4)


def draw_beam_two(key, part):
    return child_table(jax.random.fold_in(key, 23), B2, BD // 2)


def touch_ends(values, stream_key, least, top_value):
    index_at = [jax.random.randint(jax.random.fold_in(stream_key, axis), (), 0, length) for axis, length in enumerate(values.shape)]
    main_axis = values.shape.index(max(values.shape))
    beside = index_at[:main_axis] + [(index_at[main_axis] + 1) % values.shape[main_axis]] + index_at[main_axis + 1:]
    return values.at[tuple(index_at)].set(least).at[tuple(beside)].set(top_value)


def block_scale(own_key, dims, shards, smallest, high):
    factor_of = 1.0
    for position, blocks in shards:
        heights = jax.random.uniform(jax.random.fold_in(jax.random.fold_in(own_key, 6), position), (blocks,), jnp.float32, smallest / len(shards), high / len(shards))
        factor_of = factor_of * jnp.repeat(jnp.exp(heights), dims[position] // blocks).reshape((-1,) + (1,) * (len(dims) - 1 - position))
    return factor_of


def bell_draw(own_key, extent, scale, reach, shards=(), dtype=jnp.bfloat16):
    factor_of = block_scale(own_key, extent, shards, -0.22, 0.18) if shards else 1.0
    entries = jax.random.normal(own_key, extent, jnp.float32) * scale * factor_of
    return jnp.minimum(jnp.maximum(entries, -reach), reach).astype(dtype)


def setup_inputs(seed: int = 0, part: int = 0) -> dict:
    streams_of = jax.random.split(jax.random.key(seed), 11)
    own_keys = jax.random.split(jax.random.fold_in(streams_of[10], part), 11)
    return {
        "echo": bell_draw(own_keys[0], (SUBS, B0, 2, RANGE), 1.0, 6.0, ((0, 4), (1, 2), (3, 2))),
        "chirp": bell_draw(streams_of[1], (2, CH), (2 * CH) ** -0.5, 0.1875),
        "beam_one": draw_beam_one(jax.random.fold_in(streams_of[10], 71), part),
        "shift_one": touch_ends(jax.random.randint(streams_of[3], (2, B1), 0 - OMAX, OMAX + 1), jax.random.fold_in(streams_of[3], 1), 0 - OMAX, OMAX).astype(jnp.int32),
        "frac_one": jnp.clip(jax.random.uniform(streams_of[4], (2, B1), jnp.float32, 0.0, 1.0), 0.0, 1.0),
        "base_one": jnp.clip(jax.random.uniform(streams_of[5], (2, B1), jnp.float32, -3.140625, 3.140625), -3.140625, 3.140625),
        "beam_two": draw_beam_two(jax.random.fold_in(streams_of[10], 71), part),
        "shift_two": touch_ends(jax.random.randint(streams_of[7], (2, B2), 0 - OMAX, OMAX + 1), jax.random.fold_in(streams_of[7], 1), 0 - OMAX, OMAX).astype(jnp.int32),
        "frac_two": jnp.clip(jax.random.uniform(streams_of[8], (2, B2), jnp.float32, 0.0, 1.0), 0.0, 1.0),
        "base_two": jnp.clip(jax.random.uniform(streams_of[9], (2, B2), jnp.float32, -3.140625, 3.140625), -3.140625, 3.140625),
    }


def correlate_all(echo, chirp):
    real_part = chirp[0].astype(jnp.float32)
    imag_part = chirp[1].astype(jnp.float32)
    kernel = jnp.stack([jnp.stack([real_part, imag_part]), jnp.stack([-imag_part, real_part])])

    def one_subaperture(subimage):
        signal = subimage.astype(jnp.float32)
        result = lax.conv_general_dilated(signal, kernel, (1,), [(0, CH - 1)], dimension_numbers=("NCH", "OIH", "NCH"), precision=lax.Precision.HIGHEST)
        return result.astype(jnp.bfloat16)

    return lax.map(one_subaperture, echo)


def tap_table(frac_table):
    spread = (jnp.arange(8).astype(jnp.float32) - 3.0)[None, None, :] - frac_table[..., None]
    return jnp.sinc(spread) * (0.54 + 0.46 * jnp.cos(jnp.pi * spread / 4.0))


def merge_level(images, beam_table, shift_table, frac_table, base_table):
    pair_count = images.shape[0] // 2
    parent_count = beam_table.shape[1]
    bin_total = images.shape[3]
    tap_weights = tap_table(frac_table)
    range_ramp = jnp.arange(bin_total).astype(jnp.float32) / bin_total - 0.5
    seg_len = bin_total + 7

    def slide(line_data, offset_start):
        return lax.dynamic_slice_in_dim(line_data, offset_start, seg_len, 1)

    def one_pair(pair_index):
        merged = jnp.zeros((parent_count, 2, bin_total), jnp.float32)
        for child in range(2):
            child_image = lax.dynamic_index_in_dim(images, 2 * pair_index + child, 0, keepdims=False)
            chosen = jnp.take(child_image, beam_table[child], axis=0)
            padded = jnp.pad(chosen, ((0, 0), (0, 0), (HALO, HALO)))
            starts = (HALO - 3 + shift_table[child]).astype(jnp.int32)
            segments = jax.vmap(slide)(padded, starts)
            interpolated = jnp.zeros((parent_count, 2, bin_total), jnp.float32)
            for tap_index in range(8):
                interpolated = interpolated + tap_weights[child, :, tap_index, None, None] * segments[:, :, tap_index:tap_index + bin_total].astype(jnp.float32)
            phase_angle = base_table[child][:, None] + 0.5 * (shift_table[child].astype(jnp.float32) + frac_table[child])[:, None] * range_ramp[None, :]
            cosine = jnp.cos(phase_angle)
            sine_part = jnp.sin(phase_angle)
            rotated = jnp.stack([interpolated[:, 0] * cosine - interpolated[:, 1] * sine_part, interpolated[:, 0] * sine_part + interpolated[:, 1] * cosine], axis=1)
            merged = merged + rotated
        return merged.astype(jnp.bfloat16)

    return lax.map(one_pair, jnp.arange(pair_count).astype(jnp.int32))


def reference(echo, chirp, beam_one, shift_one, frac_one, base_one, beam_two, shift_two, frac_two, base_two):
    compressed = correlate_all(echo, chirp)
    level_one = merge_level(compressed, beam_one, shift_one, frac_one, base_one)
    level_two = merge_level(level_one, beam_two, shift_two, frac_two, base_two)
    grouped = level_two.reshape(N_PULSE // 4, N_REP, 2, 2, BD, 2, RANGE)
    return grouped.transpose(1, 0, 3, 2, 4, 5, 6).reshape(N_REP, N_PULSE, BD, 2, RANGE)
```

```python
import jax
import jax.numpy as jnp
from jax import lax
from jax.experimental import pallas as pl
from jax.experimental.pallas import tpu as pltpu
from jax.sharding import PartitionSpec as P

LEFT = 128
STEP = 128
ROWS = 56
COLS = 64
GROUPS = 16
RIM = 32
WIDE = GROUPS * ROWS
SPANS = COLS // GROUPS
CHUNKS = ROWS // 8
PER = 8 + 2 * CHUNKS


def exchange(parts, lane):
    parts = list(parts)
    step = 1
    while step < len(parts):
        low = (lane & step) == 0
        for first in range(len(parts)):
            if first & step:
                continue
            a, b = parts[first], parts[first + step]
            parts[first] = jnp.where(low, a, pltpu.roll(b, step, 1))
            parts[first + step] = jnp.where(low, pltpu.roll(a, 128 - step, 1), b)
        step *= 2
    return parts


def store_rimmed(ref, index, chunk, value):
    row = 8 * chunk
    ref[index, pl.ds(RIM + row, 8), :] = value
    if row >= ROWS - RIM:
        ref[index, pl.ds(row - (ROWS - RIM), 8), :] = pltpu.roll(value, 1, 1)
    if row < RIM:
        ref[index, pl.ds(RIM + ROWS + row, 8), :] = pltpu.roll(value, 127, 1)


def merged(images, index_ref, float_ref, turn_ref, entry, sign, roots):
    total = [None] * CHUNKS
    for child in range(2):
        place = entry + child
        image = index_ref[2 * place] + roots[child]
        start = index_ref[2 * place + 1]
        value = None
        for tap in range(8):
            term = images[image, pl.ds(start + tap, ROWS), :] * float_ref[PER * place + tap]
            value = term if value is None else value + term
        cos_row, sin_row = turn_ref[place, 0], turn_ref[place, 1]
        cos_signed, sin_signed = cos_row * sign, sin_row * sign
        for chunk in range(CHUNKS):
            c = float_ref[PER * place + 8 + chunk]
            s = float_ref[PER * place + 8 + CHUNKS + chunk]
            part = value[8 * chunk : 8 * chunk + 8]
            cosine = cos_row * c - sin_row * s
            sine = sin_signed * c + cos_signed * s
            term = part * cosine + pltpu.roll(part, COLS, 1) * sine
            total[chunk] = term if total[chunk] is None else total[chunk] + term
    return total


def whole_kernel(
    index_ref, float_ref, chirp_ref, a0, a1, a2, a3, turn_ref, out_ref,
    band_ref, source, columns, compressed, level_one, level_two,
):
    bins = out_ref.shape[2]
    span = band_ref.shape[1]
    lanes = lax.broadcasted_iota(jnp.int32, (8, 128), 1)
    rows = lax.broadcasted_iota(jnp.int32, (8, 128), 0)
    column = lanes & (COLS - 1)
    sign = jnp.where(lanes < COLS, -1.0, 1.0)
    first_bin, bin_total = index_ref[512], index_ref[513]
    place = column * ROWS + rows + (first_bin - LEFT)

    def inside(chunk, value):
        spot = place + 8 * chunk
        return jnp.where((spot >= 0) & (spot < bin_total), value, 0.0)

    for part in range(2):
        band = jnp.broadcast_to(chirp_ref[part : part + 1, :], (STEP, span))
        band = pltpu.roll(band, 0, 1, stride=1, stride_axis=0)
        band_ref[pl.ds(STEP * part, STEP), :] = band.astype(jnp.bfloat16)
    held = a0.shape[2]
    for pair, (near, far) in enumerate(((a0, a1), (a2, a3))):
        for comp in range(2):
            both = jnp.concatenate(
                [near[comp].astype(jnp.float32), far[comp].astype(jnp.float32)], axis=0
            ).astype(jnp.bfloat16)
            source[pair * 2 + comp, :, pl.ds(0, held)] = both
    if source.shape[2] > held:
        source[:, :, pl.ds(held, source.shape[2] - held)] = jnp.zeros(
            (4, 16, source.shape[2] - held), jnp.bfloat16
        )
    blocks = WIDE // STEP
    for pair in range(2):
        windows = jnp.concatenate(
            [
                source[pair * 2 + comp, :, pl.ds(WIDE * u + STEP * block, span)]
                for block in range(blocks)
                for comp in range(2)
                for u in range(SPANS)
            ],
            axis=0,
        )
        product = lax.dot_general(
            band_ref[...], windows, (((1,), (1,)), ((), ())), preferred_element_type=jnp.float32
        )
        wide_sign = jnp.where(lax.broadcasted_iota(jnp.int32, (STEP, 128), 1) < COLS, 1.0, -1.0)
        for block in range(blocks):
            plain = product[:STEP, 128 * block : 128 * block + 128]
            crossed = product[STEP:, 128 * block : 128 * block + 128]
            columns[pl.ds(STEP * block, STEP), :] = plain + wide_sign * pltpu.roll(crossed, COLS, 1)
        for chunk in range(CHUNKS):
            parts = [columns[pl.ds(ROWS * g + 8 * chunk, 8), :] for g in range(GROUPS)]
            for image, value in enumerate(exchange(parts, lanes)):
                store_rimmed(compressed, 16 * pair + image, chunk, inside(chunk, value))

    def one(step, carry):
        for pair in range(2):
            total = merged(
                compressed, index_ref, float_ref, turn_ref, 2 * step, sign, (16 * pair, 16 * pair)
            )
            for chunk in range(CHUNKS):
                store_rimmed(level_one, 16 * pair + step, chunk, inside(chunk, total[chunk]))
        return carry

    lax.fori_loop(0, 16, one, 0)

    for half in range(2):

        def two(step, carry):
            total = merged(
                level_one, index_ref, float_ref, turn_ref, 32 + 32 * half + 2 * step, sign, (0, 0)
            )
            for chunk in range(CHUNKS):
                level_two[step, pl.ds(8 * chunk, 8), :] = total[chunk]
            return carry

        lax.fori_loop(0, 16, two, 0)
        for chunk in range(CHUNKS):
            parts = [level_two[image, pl.ds(8 * chunk, 8), :] for image in range(GROUPS)]
            for g, value in enumerate(exchange(parts, lanes)):
                columns[pl.ds(ROWS * g + 8 * chunk, 8), :] = value
        for block in range(blocks):
            turned = columns[pl.ds(STEP * block, STEP), :].T.astype(jnp.bfloat16)
            for comp in range(2):
                for u in range(SPANS):
                    left = WIDE * u + STEP * block - LEFT
                    if 0 <= left < bins:
                        row = (comp * SPANS + u) * 16
                        out_ref[comp, pl.ds(16 * half, 16), pl.ds(left, 128)] = turned[row : row + 16]


def tables(beam, shift, frac, base, width, first_parent, first_child, swap, stride, first_bin, bin_total):
    def mine(table):
        return lax.dynamic_slice_in_dim(table, first_parent, width, 1).T

    beam, shift, frac, base = mine(beam), mine(shift), mine(frac), mine(base)
    spread = (jnp.arange(8).astype(jnp.float32) - 3.0) - frac[..., None]
    taps = jnp.sinc(spread) * (0.54 + 0.46 * jnp.cos(jnp.pi * spread / 4.0))
    slope = 0.5 * (shift.astype(jnp.float32) + frac)
    chunk_angle = slope[..., None] * (8.0 * jnp.arange(CHUNKS).astype(jnp.float32) / bin_total)
    floats = jnp.concatenate([taps, jnp.cos(chunk_angle), jnp.sin(chunk_angle)], axis=2)
    image = beam - first_child + (jnp.arange(2)[None, :] ^ swap) * stride
    indices = jnp.stack([image, shift + (RIM - 3)], axis=2)
    spot = (jnp.arange(128) % COLS)[None, :] * ROWS + jnp.arange(8)[:, None] + (first_bin - LEFT)
    ramp = spot.astype(jnp.float32) / bin_total - 0.5
    angle = base[..., None, None] + slope[..., None, None] * ramp
    turns = jnp.stack([jnp.cos(angle), jnp.sin(angle)], axis=2)
    return indices.reshape(-1), floats.reshape(-1), turns.reshape(2 * width, 2, 8, 128)


def neighbours(head, tail, axis):
    count = lax.axis_size(axis)
    index = lax.axis_index(axis)
    even = index % 2 == 0
    near = [(i, i ^ 1) for i in range(count) if i ^ 1 < count]
    far = [(i + 1, i + 2) for i in range(0, count - 2, 2)]
    far = far + [(b, a) for a, b in far]
    first = lax.ppermute(jnp.where(even, tail, head), axis, near)
    second = lax.ppermute(jnp.where(even, head, tail), axis, far) if far else jnp.zeros_like(first)
    return jnp.where(even, second, first), jnp.where(even, first, second)


def body(
    echo, chirp, beam_one, shift_one, frac_one, base_one, beam_two, shift_two, frac_two, base_two
):
    signal = echo[0]
    beams, _, bins = signal.shape
    taps = chirp.shape[1]
    span = STEP + taps
    bin_total = bins * lax.axis_size("range")
    first_bin = lax.axis_index("range") * bins
    pulse = lax.axis_index("pulse")
    low, high = pulse % 2, pulse // 2 % 2
    own = 4 * lax.axis_index("rep") + 2 * low + high

    head = signal[:, :, :span]
    tail = signal[:, :, bins - span :]
    from_left, from_right = neighbours(head, tail, "range")
    wide = jnp.concatenate([from_left[:, :, span - LEFT :], signal, from_right], axis=2)
    wide = wide.reshape(4, beams // 4, 2, wide.shape[2]).transpose(0, 2, 1, 3)

    def block_of(index):
        return lax.dynamic_index_in_dim(wide, 2 * (index % 2) + index // 2 % 2, 0, keepdims=False)

    parts = [block_of(pulse)]
    for mask in (1, 2, 3):
        route = [(i, i ^ mask) for i in range(lax.axis_size("pulse"))]
        parts.append(lax.ppermute(block_of(pulse ^ mask), "pulse", route))

    one = tables(
        beam_one, shift_one, frac_one, base_one, 16, 16 * own, 8 * own, low, 8, first_bin, bin_total
    )
    two = tables(
        beam_two, shift_two, frac_two, base_two, 32, 32 * own, 16 * own, high, 16, first_bin, bin_total
    )
    edges = jnp.stack([first_bin, jnp.asarray(bin_total)]).astype(jnp.int32)
    pad = jnp.zeros((512 - one[0].size - two[0].size,), jnp.int32)
    indices = jnp.concatenate([one[0], two[0], pad, edges])
    floats = jnp.concatenate([one[1], two[1]])
    turns = jnp.concatenate([one[2], two[2]])
    chirp_row = jnp.pad(chirp.astype(jnp.float32), ((0, 0), (0, STEP)))

    full = SPANS * WIDE + span - STEP
    vmem = pl.BlockSpec(memory_space=pltpu.VMEM)
    smem = pl.BlockSpec(memory_space=pltpu.SMEM)
    image = pl.pallas_call(
        whole_kernel,
        out_shape=jax.ShapeDtypeStruct((2, 32, bins), jnp.bfloat16),
        in_specs=[smem, smem] + [vmem] * 6,
        out_specs=vmem,
        scratch_shapes=[
            pltpu.VMEM((2 * STEP, span), jnp.bfloat16),
            pltpu.VMEM((4, 16, full), jnp.bfloat16),
            pltpu.VMEM((WIDE, 128), jnp.float32),
            pltpu.VMEM((32, ROWS + 2 * RIM, 128), jnp.float32),
            pltpu.VMEM((32, ROWS + 2 * RIM, 128), jnp.float32),
            pltpu.VMEM((16, ROWS, 128), jnp.float32),
        ],
        name="backproject",
    )(indices, floats, chirp_row, *parts, turns)
    return image.transpose(1, 0, 2)[None, None]


def solution(mesh):
    in_specs = (P(("scene", "pulse"), "rep", None, "range"),) + (P(),) * 9
    out_specs = P("rep", ("scene", "pulse"), None, None, "range")
    return jax.shard_map(body, mesh=mesh, in_specs=in_specs, out_specs=out_specs, check_vma=False)
```

```python
import jax
import jax.numpy as jnp
from jax import lax
from jax.experimental import pallas as pl
from jax.experimental.pallas import tpu as pltpu
from jax.sharding import PartitionSpec as P

LEFT = 128
STEP = 128
ROWS = 56
COLS = 64
GROUPS = 16
RIM = 32
WIDE = GROUPS * ROWS
SPANS = COLS // GROUPS
CHUNKS = ROWS // 8
BLOCKS = WIDE // STEP
ONE, TWO = 16, 32
TALL = ROWS + 2 * RIM
TOGETHER = 4


def position():
    rep, pulse = lax.axis_index("rep"), lax.axis_index("pulse")
    low, high = pulse % 2, pulse // 2 % 2
    return 4 * rep + 2 * low + high, low, high


def lane_ids(shape):
    return lax.broadcasted_iota(jnp.int32, shape, len(shape) - 1)


def row_ids(shape):
    return lax.broadcasted_iota(jnp.int32, shape, len(shape) - 2)


def exchange(parts):
    parts = list(parts)
    lane = lane_ids(parts[0].shape)
    step = 1
    while step < len(parts):
        low = (lane & step) == 0
        for first in range(len(parts)):
            if first & step:
                continue
            a, b = parts[first], parts[first + step]
            parts[first] = jnp.where(low, a, pltpu.roll(b, step, 1))
            parts[first + step] = jnp.where(low, pltpu.roll(a, 128 - step, 1), b)
        step *= 2
    return parts


def store_rimmed(ref, index, chunk, value):
    row = 8 * chunk
    ref[index, pl.ds(RIM + row, 8), :] = value
    if row >= ROWS - RIM:
        ref[index, pl.ds(row - (ROWS - RIM), 8), :] = pltpu.roll(value, 1, 1)
    if row < RIM:
        ref[index, pl.ds(RIM + ROWS + row, 8), :] = pltpu.roll(value, 127, 1)


def inside_test(bins):
    first_bin = lax.axis_index("range") * bins
    bin_total = bins * lax.axis_size("range")
    shape = (8, 128)
    place = (lane_ids(shape) & (COLS - 1)) * ROWS + row_ids(shape) + (first_bin - LEFT)

    def inside(chunk, value):
        spot = place + 8 * chunk
        return jnp.where((spot >= 0) & (spot < bin_total), value, 0.0)

    return inside


def prep_kernel(bins):
    def kernel(
        chirp_ref, shift_one, frac_one, base_one, shift_two, frac_two, base_two,
        band_ref, taps_ref, turn_ref,
    ):
        own, _, _ = position()
        first_bin = lax.axis_index("range") * bins
        bin_total = bins * lax.axis_size("range")
        span = band_ref.shape[0]
        for part in range(2):
            row = chirp_ref[part : part + 1, :].astype(jnp.float32)
            row = jnp.concatenate([row, jnp.zeros((1, STEP), jnp.float32)], axis=1)
            band = pltpu.roll(jnp.broadcast_to(row, (STEP, span)), 0, 1, stride=1, stride_axis=0)
            for block in range(span // 128):
                turned = band[:, 128 * block : 128 * block + 128].T
                band_ref[pl.ds(128 * block, 128), pl.ds(STEP * part, STEP)] = turned.astype(
                    jnp.bfloat16
                )

        shape = (8, 128)
        lane = lane_ids(shape)

        def packed(first, second):
            total = jnp.zeros(shape, jnp.float32)
            at = 0
            for ref, width in ((first, ONE), (second, TWO)):
                offset = own * width
                for child in range(2):
                    row = ref[child : child + 1, 0:128].astype(jnp.float32)
                    for block in range(1, ref.shape[1] // 128):
                        other = ref[child : child + 1, 128 * block : 128 * block + 128]
                        row = jnp.where(offset // 128 == block, other.astype(jnp.float32), row)
                    row = pltpu.roll(
                        jnp.broadcast_to(row, shape), (at + 256 - offset % 128) % 128, 1
                    )
                    total = jnp.where((lane >= at) & (lane < at + width), row, total)
                    at += width
            return total

        frac = packed(frac_one, frac_two)
        base = packed(base_one, base_two)
        slope = 0.5 * (packed(shift_one, shift_two) + frac)
        row = row_ids(shape).astype(jnp.float32)
        spread = (row - 3.0) - frac
        turned = jnp.pi * spread
        still = turned == 0.0
        safe = jnp.where(still, 1.0, turned)
        weights = jnp.where(still, 1.0, jnp.sin(safe) / safe) * (
            0.54 + 0.46 * jnp.cos(jnp.pi * spread / 4.0)
        )
        count = taps_ref.shape[0]
        square = (128, 128)
        base_rows = jnp.broadcast_to(base[0:1], square).T[:count]
        slope_rows = jnp.broadcast_to(slope[0:1], square).T[:count]
        wide = lane_ids((count, 128))
        spot = (wide & (COLS - 1)) * ROWS + (first_bin - LEFT)
        angle = base_rows + slope_rows * (spot.astype(jnp.float32) / bin_total - 0.5)
        cos_col, sin_col = jnp.cos(angle), jnp.sin(angle)
        sign = jnp.where(lane < COLS, -1.0, 1.0)
        fine = [slope * ((row + 8.0 * chunk) / bin_total) for chunk in range(CHUNKS)]
        cos_row = [jnp.cos(a) for a in fine]
        sin_row = [jnp.sin(a) for a in fine]
        for place in range(count):
            taps_ref[place] = jnp.broadcast_to(weights[:, place : place + 1], shape)
            c = jnp.broadcast_to(cos_col[place : place + 1], shape)
            s = jnp.broadcast_to(sin_col[place : place + 1], shape)
            c_signed, s_signed = c * sign, s * sign
            for chunk in range(CHUNKS):
                cb = jnp.broadcast_to(cos_row[chunk][:, place : place + 1], shape)
                sb = jnp.broadcast_to(sin_row[chunk][:, place : place + 1], shape)
                turn_ref[place, 0, pl.ds(8 * chunk, 8), :] = c * cb - s * sb
                turn_ref[place, 1, pl.ds(8 * chunk, 8), :] = s_signed * cb + c_signed * sb

    return kernel


def compress_pair(near, near_rim, far, far_rim, band_ref, source, columns, images, inside):
    held = near.shape[2]
    rim = near_rim.shape[2]

    def both(first, second, comp):
        return jnp.concatenate(
            [first[comp].astype(jnp.float32), second[comp].astype(jnp.float32)], axis=0
        ).astype(jnp.bfloat16)

    for comp in range(2):
        sides = both(near_rim, far_rim, comp)
        source[comp, :, pl.ds(0, LEFT)] = sides[:, :LEFT]
        source[comp, :, pl.ds(LEFT, held)] = both(near, far, comp)
        source[comp, :, pl.ds(LEFT + held, rim - LEFT)] = sides[:, LEFT:]
        rest = source.shape[2] - held - rim
        if rest:
            source[comp, :, pl.ds(held + rim, rest)] = jnp.zeros((16, rest), jnp.bfloat16)
    span = band_ref.shape[0]
    windows = jnp.concatenate(
        [
            source[comp, :, pl.ds(WIDE * u + STEP * block, span)]
            for block in range(BLOCKS)
            for comp in range(2)
            for u in range(SPANS)
        ],
        axis=0,
    )
    product = jnp.dot(windows, band_ref[...], preferred_element_type=jnp.float32)
    half = 16 * SPANS
    for block in range(BLOCKS):
        top = product[128 * block : 128 * block + half]
        low = product[128 * block + half : 128 * block + 128]
        result = jnp.concatenate(
            [top[:, :STEP] + low[:, STEP:], low[:, :STEP] - top[:, STEP:]], axis=0
        )
        columns[pl.ds(STEP * block, STEP), :] = result.astype(jnp.bfloat16).T.astype(jnp.float32)
    for chunk in range(0, CHUNKS, 2):
        size = min(2, CHUNKS - chunk) * 8
        parts = [columns[pl.ds(ROWS * g + 8 * chunk, size), :] for g in range(GROUPS)]
        parts = exchange([part.astype(jnp.bfloat16) for part in parts])
        for image, part in enumerate(parts):
            part = part.astype(jnp.float32)
            for extra in range(size // 8):
                value = inside(chunk + extra, part[8 * extra : 8 * extra + 8])
                store_rimmed(images, image, chunk + extra, value)


def merged(images, beam_ref, shift_ref, taps_ref, turn_ref, parent, first_parent, first_child,
           swap, stride, width, at):
    total = [None] * CHUNKS
    for child in range(2):
        place = at + child * width + parent
        image = beam_ref[child, first_parent + parent] - first_child + (child ^ swap) * stride
        start = shift_ref[child, first_parent + parent] + (RIM - 3)
        value = None
        for tap in range(8):
            term = images[image, pl.ds(start + tap, ROWS), :] * taps_ref[place, pl.ds(tap, 1), :]
            value = term if value is None else value + term
        for chunk in range(CHUNKS):
            part = value[8 * chunk : 8 * chunk + 8]
            term = (
                part * turn_ref[place, 0, pl.ds(8 * chunk, 8), :]
                + pltpu.roll(part, COLS, 1) * turn_ref[place, 1, pl.ds(8 * chunk, 8), :]
            )
            total[chunk] = term if total[chunk] is None else total[chunk] + term
    return total


def merge_one(images, beam_ref, shift_ref, taps_ref, turn_ref, result, inside):
    own, low, _ = position()

    def step(index, carry):
        for extra in range(TOGETHER):
            parent = TOGETHER * index + extra
            total = merged(
                images, beam_ref, shift_ref, taps_ref, turn_ref, parent, ONE * own, 8 * own, low, 8,
                ONE, 0,
            )
            for chunk in range(CHUNKS):
                store_rimmed(result, parent, chunk, inside(chunk, total[chunk]))
        return carry

    lax.fori_loop(0, ONE // TOGETHER, step, 0)


def first_kernel(bins):
    def kernel(
        beam_ref, shift_ref, a0, r0, a1, r1, band_ref, taps_ref, turn_ref, out_ref,
        source, columns, images,
    ):
        inside = inside_test(bins)
        compress_pair(a0, r0, a1, r1, band_ref, source, columns, images, inside)
        merge_one(images, beam_ref, shift_ref, taps_ref, turn_ref, out_ref, inside)

    return kernel


def second_kernel(bins):
    def kernel(
        beam_one, shift_one, beam_two, shift_two, a2, r2, a3, r3, band_ref, taps_ref, turn_ref,
        done_ref, out_ref, source, columns, images, level_one, level_two,
    ):
        inside = inside_test(bins)
        level_one[pl.ds(0, ONE)] = done_ref[...]
        compress_pair(a2, r2, a3, r3, band_ref, source, columns, images, inside)
        merge_one(
            images, beam_one, shift_one, taps_ref, turn_ref, level_one.at[pl.ds(ONE, ONE)], inside
        )
        own, _, high = position()
        for half in range(2):

            def step(index, carry):
                for extra in range(TOGETHER):
                    parent = TOGETHER * index + extra
                    total = merged(
                        level_one, beam_two, shift_two, taps_ref, turn_ref, parent + 16 * half,
                        TWO * own, ONE * own, high, ONE, TWO, 2 * ONE,
                    )
                    for chunk in range(CHUNKS):
                        level_two[parent, pl.ds(8 * chunk, 8), :] = total[chunk]
                return carry

            lax.fori_loop(0, 16 // TOGETHER, step, 0)
            for chunk in range(0, CHUNKS, 2):
                size = min(2, CHUNKS - chunk) * 8
                parts = [level_two[image, pl.ds(8 * chunk, size), :] for image in range(GROUPS)]
                parts = exchange([part.astype(jnp.bfloat16) for part in parts])
                for g, part in enumerate(parts):
                    columns[pl.ds(ROWS * g + 8 * chunk, size), :] = part.astype(jnp.float32)
            for block in range(BLOCKS):
                turned = columns[pl.ds(STEP * block, STEP), :].astype(jnp.bfloat16).T
                for comp in range(2):
                    for u in range(SPANS):
                        left = WIDE * u + STEP * block - LEFT
                        if 0 <= left < bins:
                            row = (comp * SPANS + u) * 16
                            out_ref[comp, pl.ds(16 * half, 16), pl.ds(left, 128)] = turned[
                                row : row + 16
                            ]

    return kernel


def neighbours(head, tail, axis):
    count = lax.axis_size(axis)
    even = lax.axis_index(axis) % 2 == 0
    near = [(i, i ^ 1) for i in range(count) if i ^ 1 < count]
    far = [(i + 1, i + 2) for i in range(0, count - 2, 2)]
    far = far + [(b, a) for a, b in far]
    first = lax.ppermute(jnp.where(even, tail, head), axis, near)
    second = lax.ppermute(jnp.where(even, head, tail), axis, far) if far else jnp.zeros_like(first)
    return jnp.where(even, second, first), jnp.where(even, first, second)


def body(
    echo, chirp, beam_one, shift_one, frac_one, base_one, beam_two, shift_two, frac_two, base_two
):
    signal = echo[0]
    beams, _, bins = signal.shape
    span = STEP + chirp.shape[1]
    pulse = lax.axis_index("pulse")

    signal = signal.reshape(4, beams // 4, 2, bins).transpose(0, 2, 1, 3)

    def routed(array):
        def block_of(index):
            return lax.dynamic_index_in_dim(array, 2 * (index % 2) + index // 2 % 2, 0, keepdims=False)

        parts = [block_of(pulse)]
        for mask in (1, 2, 3):
            route = [(i, i ^ mask) for i in range(lax.axis_size("pulse"))]
            parts.append(lax.ppermute(block_of(pulse ^ mask), "pulse", route))
        return parts

    parts = routed(signal)
    from_left, from_right = neighbours(
        signal[:, :, :, :span], signal[:, :, :, bins - span :], "range"
    )
    rims = routed(jnp.concatenate([from_left[:, :, :, span - LEFT :], from_right], axis=3))

    vmem = pl.BlockSpec(memory_space=pltpu.VMEM)
    smem = pl.BlockSpec(memory_space=pltpu.SMEM)
    params = pltpu.CompilerParams(vmem_limit_bytes=24 << 20)
    count = 2 * (ONE + TWO)
    band, taps, turns = pl.pallas_call(
        prep_kernel(bins),
        out_shape=(
            jax.ShapeDtypeStruct((span, 2 * STEP), jnp.bfloat16),
            jax.ShapeDtypeStruct((count, 8, 128), jnp.float32),
            jax.ShapeDtypeStruct((count, 2, ROWS, 128), jnp.float32),
        ),
        in_specs=[vmem] * 7,
        out_specs=(vmem,) * 3,
        compiler_params=params,
        name="prepare",
    )(chirp, shift_one, frac_one, base_one, shift_two, frac_two, base_two)

    scratch = [
        pltpu.VMEM((2, 16, SPANS * WIDE + span - STEP), jnp.bfloat16),
        pltpu.VMEM((WIDE, 128), jnp.float32),
        pltpu.VMEM((16, TALL, 128), jnp.float32),
    ]
    done = pl.pallas_call(
        first_kernel(bins),
        out_shape=jax.ShapeDtypeStruct((ONE, TALL, 128), jnp.float32),
        in_specs=[smem] * 2 + [vmem] * 7,
        out_specs=vmem,
        scratch_shapes=scratch,
        compiler_params=params,
        name="first_pair",
    )(beam_one, shift_one, parts[0], rims[0], parts[1], rims[1], band, taps, turns)
    image = pl.pallas_call(
        second_kernel(bins),
        out_shape=jax.ShapeDtypeStruct((2, 2 * 16, bins), jnp.bfloat16),
        in_specs=[smem] * 4 + [vmem] * 8,
        out_specs=vmem,
        scratch_shapes=scratch
        + [
            pltpu.VMEM((2 * ONE, TALL, 128), jnp.float32),
            pltpu.VMEM((16, ROWS, 128), jnp.float32),
        ],
        compiler_params=params,
        name="second_pair",
    )(
        beam_one, shift_one, beam_two, shift_two, parts[2], rims[2], parts[3], rims[3], band, taps,
        turns, done,
    )
    return image.transpose(1, 0, 2)[None, None]


def solution(mesh):
    in_specs = (P(("scene", "pulse"), "rep", None, "range"),) + (P(),) * 9
    out_specs = P("rep", ("scene", "pulse"), None, None, "range")
    return jax.shard_map(body, mesh=mesh, in_specs=in_specs, out_specs=out_specs, check_vma=False)
```

```python
import jax
import jax.numpy as jnp
from jax import lax
from jax.experimental import pallas as pl
from jax.experimental.pallas import tpu as pltpu
from jax.sharding import PartitionSpec as P

LEFT = 128
STEP = 128
ROWS = 56
COLS = 64
GROUPS = 16
RIM = 32
WIDE = GROUPS * ROWS
SPANS = COLS // GROUPS
CHUNKS = ROWS // 8
BLOCKS = WIDE // STEP
ONE, TWO = 16, 32
TALL = ROWS + 2 * RIM
TOGETHER = 4


def position():
    rep, pulse = lax.axis_index("rep"), lax.axis_index("pulse")
    low, high = pulse % 2, pulse // 2 % 2
    return 4 * rep + 2 * low + high, low, high


def lane_ids(shape):
    return lax.broadcasted_iota(jnp.int32, shape, len(shape) - 1)


def row_ids(shape):
    return lax.broadcasted_iota(jnp.int32, shape, len(shape) - 2)


def exchange(parts):
    parts = list(parts)
    lane = lane_ids(parts[0].shape)
    step = 1
    while step < len(parts):
        low = (lane & step) == 0
        for first in range(len(parts)):
            if first & step:
                continue
            a, b = parts[first], parts[first + step]
            parts[first] = jnp.where(low, a, pltpu.roll(b, step, 1))
            parts[first + step] = jnp.where(low, pltpu.roll(a, 128 - step, 1), b)
        step *= 2
    return parts


def store_rimmed(ref, index, chunk, value):
    row = 8 * chunk
    ref[index, pl.ds(RIM + row, 8), :] = value
    if row >= ROWS - RIM:
        ref[index, pl.ds(row - (ROWS - RIM), 8), :] = pltpu.roll(value, 1, 1)
    if row < RIM:
        ref[index, pl.ds(RIM + ROWS + row, 8), :] = pltpu.roll(value, 127, 1)


def inside_test(bins):
    first_bin = lax.axis_index("range") * bins
    bin_total = bins * lax.axis_size("range")
    shape = (8, 128)
    place = (lane_ids(shape) & (COLS - 1)) * ROWS + row_ids(shape) + (first_bin - LEFT)

    def inside(chunk, value):
        spot = place + 8 * chunk
        return jnp.where((spot >= 0) & (spot < bin_total), value, 0.0)

    return inside


def fetch(sources, targets, sems):
    copies = [
        pltpu.make_async_copy(source, target, sems.at[index])
        for index, (source, target) in enumerate(zip(sources, targets))
    ]
    for copy in copies:
        copy.start()
    for copy in copies:
        copy.wait()


def prep_kernel(bins):
    def kernel(*refs):
        far, (band_ref, taps_ref, turn_ref) = refs[:7], refs[7:10]
        chirp_ref, shift_one, frac_one, base_one, shift_two, frac_two, base_two = refs[10:17]
        fetch(far, refs[10:17], refs[17])
        own, _, _ = position()
        first_bin = lax.axis_index("range") * bins
        bin_total = bins * lax.axis_size("range")
        span = band_ref.shape[0]
        for part in range(2):
            row = chirp_ref[part : part + 1, :].astype(jnp.float32)
            row = jnp.concatenate([row, jnp.zeros((1, STEP), jnp.float32)], axis=1)
            band = pltpu.roll(jnp.broadcast_to(row, (STEP, span)), 0, 1, stride=1, stride_axis=0)
            for block in range(span // 128):
                turned = band[:, 128 * block : 128 * block + 128].T
                band_ref[pl.ds(128 * block, 128), pl.ds(STEP * part, STEP)] = turned.astype(
                    jnp.bfloat16
                )

        shape = (8, 128)
        lane = lane_ids(shape)

        def packed(first, second):
            total = jnp.zeros(shape, jnp.float32)
            at = 0
            for ref, width in ((first, ONE), (second, TWO)):
                offset = own * width
                for child in range(2):
                    row = ref[child : child + 1, 0:128].astype(jnp.float32)
                    for block in range(1, ref.shape[1] // 128):
                        other = ref[child : child + 1, 128 * block : 128 * block + 128]
                        row = jnp.where(offset // 128 == block, other.astype(jnp.float32), row)
                    row = pltpu.roll(
                        jnp.broadcast_to(row, shape), (at + 256 - offset % 128) % 128, 1
                    )
                    total = jnp.where((lane >= at) & (lane < at + width), row, total)
                    at += width
            return total

        frac = packed(frac_one, frac_two)
        base = packed(base_one, base_two)
        slope = 0.5 * (packed(shift_one, shift_two) + frac)
        row = row_ids(shape).astype(jnp.float32)
        spread = (row - 3.0) - frac
        turned = jnp.pi * spread
        still = turned == 0.0
        safe = jnp.where(still, 1.0, turned)
        weights = jnp.where(still, 1.0, jnp.sin(safe) / safe) * (
            0.54 + 0.46 * jnp.cos(jnp.pi * spread / 4.0)
        )
        count = taps_ref.shape[0]
        square = (128, 128)
        base_rows = jnp.broadcast_to(base[0:1], square).T[:count]
        slope_rows = jnp.broadcast_to(slope[0:1], square).T[:count]
        wide = lane_ids((count, 128))
        spot = (wide & (COLS - 1)) * ROWS + (first_bin - LEFT)
        angle = base_rows + slope_rows * (spot.astype(jnp.float32) / bin_total - 0.5)
        cos_col, sin_col = jnp.cos(angle), jnp.sin(angle)
        sign = jnp.where(lane < COLS, -1.0, 1.0)
        fine = [slope * ((row + 8.0 * chunk) / bin_total) for chunk in range(CHUNKS)]
        cos_row = [jnp.cos(a) for a in fine]
        sin_row = [jnp.sin(a) for a in fine]
        for place in range(count):
            taps_ref[place] = jnp.broadcast_to(weights[:, place : place + 1], shape)
            c = jnp.broadcast_to(cos_col[place : place + 1], shape)
            s = jnp.broadcast_to(sin_col[place : place + 1], shape)
            c_signed, s_signed = c * sign, s * sign
            for chunk in range(CHUNKS):
                cb = jnp.broadcast_to(cos_row[chunk][:, place : place + 1], shape)
                sb = jnp.broadcast_to(sin_row[chunk][:, place : place + 1], shape)
                turn_ref[place, 0, pl.ds(8 * chunk, 8), :] = c * cb - s * sb
                turn_ref[place, 1, pl.ds(8 * chunk, 8), :] = s_signed * cb + c_signed * sb

    return kernel


def compress_pair(near, near_rim, far, far_rim, band_ref, source, columns, images, inside):
    held = near.shape[2]
    rim = near_rim.shape[2]

    def both(first, second, comp):
        return jnp.concatenate(
            [first[comp].astype(jnp.float32), second[comp].astype(jnp.float32)], axis=0
        ).astype(jnp.bfloat16)

    for comp in range(2):
        sides = both(near_rim, far_rim, comp)
        source[comp, :, pl.ds(0, LEFT)] = sides[:, :LEFT]
        source[comp, :, pl.ds(LEFT, held)] = both(near, far, comp)
        source[comp, :, pl.ds(LEFT + held, rim - LEFT)] = sides[:, LEFT:]
        rest = source.shape[2] - held - rim
        if rest:
            source[comp, :, pl.ds(held + rim, rest)] = jnp.zeros((16, rest), jnp.bfloat16)
    span = band_ref.shape[0]
    windows = jnp.concatenate(
        [
            source[comp, :, pl.ds(WIDE * u + STEP * block, span)]
            for block in range(BLOCKS)
            for comp in range(2)
            for u in range(SPANS)
        ],
        axis=0,
    )
    product = jnp.dot(windows, band_ref[...], preferred_element_type=jnp.float32)
    half = 16 * SPANS
    for block in range(BLOCKS):
        top = product[128 * block : 128 * block + half]
        low = product[128 * block + half : 128 * block + 128]
        result = jnp.concatenate(
            [top[:, :STEP] + low[:, STEP:], low[:, :STEP] - top[:, STEP:]], axis=0
        )
        columns[pl.ds(STEP * block, STEP), :] = result.astype(jnp.bfloat16).T.astype(jnp.float32)
    for chunk in range(0, CHUNKS, 2):
        size = min(2, CHUNKS - chunk) * 8
        parts = [columns[pl.ds(ROWS * g + 8 * chunk, size), :] for g in range(GROUPS)]
        parts = exchange([part.astype(jnp.bfloat16) for part in parts])
        for image, part in enumerate(parts):
            part = part.astype(jnp.float32)
            for extra in range(size // 8):
                value = inside(chunk + extra, part[8 * extra : 8 * extra + 8])
                store_rimmed(images, image, chunk + extra, value)


def merged(images, beam_ref, shift_ref, taps_ref, turn_ref, parent, first_parent, first_child,
           swap, stride, width, at):
    total = [None] * CHUNKS
    for child in range(2):
        place = at + child * width + parent
        image = beam_ref[child, first_parent + parent] - first_child + (child ^ swap) * stride
        start = shift_ref[child, first_parent + parent] + (RIM - 3)
        value = None
        for tap in range(8):
            term = images[image, pl.ds(start + tap, ROWS), :] * taps_ref[place, pl.ds(tap, 1), :]
            value = term if value is None else value + term
        for chunk in range(CHUNKS):
            part = value[8 * chunk : 8 * chunk + 8]
            term = (
                part * turn_ref[place, 0, pl.ds(8 * chunk, 8), :]
                + pltpu.roll(part, COLS, 1) * turn_ref[place, 1, pl.ds(8 * chunk, 8), :]
            )
            total[chunk] = term if total[chunk] is None else total[chunk] + term
    return total


def merge_one(images, beam_ref, shift_ref, taps_ref, turn_ref, result, inside):
    own, low, _ = position()

    def step(index, carry):
        for extra in range(TOGETHER):
            parent = TOGETHER * index + extra
            total = merged(
                images, beam_ref, shift_ref, taps_ref, turn_ref, parent, ONE * own, 8 * own, low, 8,
                ONE, 0,
            )
            for chunk in range(CHUNKS):
                store_rimmed(result, parent, chunk, inside(chunk, total[chunk]))
        return carry

    lax.fori_loop(0, ONE // TOGETHER, step, 0)


def first_kernel(bins):
    def kernel(
        far_beam, far_shift, a0, r0, a1, r1, band_ref, taps_ref, turn_ref, out_ref,
        source, columns, images, beam_ref, shift_ref, sems,
    ):
        inside = inside_test(bins)
        fetch((far_beam, far_shift), (beam_ref, shift_ref), sems)
        compress_pair(a0, r0, a1, r1, band_ref, source, columns, images, inside)
        merge_one(images, beam_ref, shift_ref, taps_ref, turn_ref, out_ref, inside)

    return kernel


def second_kernel(bins):
    def kernel(
        far_beam_one, far_shift_one, far_beam_two, far_shift_two, a2, r2, a3, r3, band_ref,
        taps_ref, turn_ref, done_ref, out_ref, source, columns, images, level_one, level_two,
        beam_one, shift_one, beam_two, shift_two, sems,
    ):
        inside = inside_test(bins)
        fetch(
            (far_beam_one, far_shift_one, far_beam_two, far_shift_two),
            (beam_one, shift_one, beam_two, shift_two), sems,
        )
        level_one[pl.ds(0, ONE)] = done_ref[...]
        compress_pair(a2, r2, a3, r3, band_ref, source, columns, images, inside)
        merge_one(
            images, beam_one, shift_one, taps_ref, turn_ref, level_one.at[pl.ds(ONE, ONE)], inside
        )
        own, _, high = position()
        for half in range(2):

            def step(index, carry):
                for extra in range(TOGETHER):
                    parent = TOGETHER * index + extra
                    total = merged(
                        level_one, beam_two, shift_two, taps_ref, turn_ref, parent + 16 * half,
                        TWO * own, ONE * own, high, ONE, TWO, 2 * ONE,
                    )
                    for chunk in range(CHUNKS):
                        level_two[parent, pl.ds(8 * chunk, 8), :] = total[chunk]
                return carry

            lax.fori_loop(0, 16 // TOGETHER, step, 0)
            for chunk in range(0, CHUNKS, 2):
                size = min(2, CHUNKS - chunk) * 8
                parts = [level_two[image, pl.ds(8 * chunk, size), :] for image in range(GROUPS)]
                parts = exchange([part.astype(jnp.bfloat16) for part in parts])
                for g, part in enumerate(parts):
                    columns[pl.ds(ROWS * g + 8 * chunk, size), :] = part.astype(jnp.float32)
            for block in range(BLOCKS):
                turned = columns[pl.ds(STEP * block, STEP), :].astype(jnp.bfloat16).T
                for comp in range(2):
                    for u in range(SPANS):
                        left = WIDE * u + STEP * block - LEFT
                        if 0 <= left < bins:
                            row = (comp * SPANS + u) * 16
                            out_ref[comp, pl.ds(16 * half, 16), pl.ds(left, 128)] = turned[
                                row : row + 16
                            ]

    return kernel


def neighbours(head, tail, axis):
    count = lax.axis_size(axis)
    even = lax.axis_index(axis) % 2 == 0
    near = [(i, i ^ 1) for i in range(count) if i ^ 1 < count]
    far = [(i + 1, i + 2) for i in range(0, count - 2, 2)]
    far = far + [(b, a) for a, b in far]
    first = lax.ppermute(jnp.where(even, tail, head), axis, near)
    second = lax.ppermute(jnp.where(even, head, tail), axis, far) if far else jnp.zeros_like(first)
    return jnp.where(even, second, first), jnp.where(even, first, second)


def body(
    echo, chirp, beam_one, shift_one, frac_one, base_one, beam_two, shift_two, frac_two, base_two
):
    signal = echo[0]
    beams, _, bins = signal.shape
    span = STEP + chirp.shape[1]
    pulse = lax.axis_index("pulse")

    signal = signal.reshape(4, beams // 4, 2, bins).transpose(0, 2, 1, 3)
    small = (
        chirp, beam_one, shift_one, frac_one, base_one, beam_two, shift_two, frac_two, base_two
    )
    chirp, beam_one, shift_one, frac_one, base_one, beam_two, shift_two, frac_two, base_two = (
        pltpu.with_memory_space_constraint(array, pltpu.HBM) for array in small
    )

    def routed(array):
        def block_of(index):
            return lax.dynamic_index_in_dim(array, 2 * (index % 2) + index // 2 % 2, 0, keepdims=False)

        parts = [block_of(pulse)]
        for mask in (1, 2, 3):
            route = [(i, i ^ mask) for i in range(lax.axis_size("pulse"))]
            parts.append(lax.ppermute(block_of(pulse ^ mask), "pulse", route))
        return parts

    parts = routed(signal)
    from_left, from_right = neighbours(
        signal[:, :, :, :span], signal[:, :, :, bins - span :], "range"
    )
    rims = routed(jnp.concatenate([from_left[:, :, :, span - LEFT :], from_right], axis=3))

    vmem = pl.BlockSpec(memory_space=pltpu.VMEM)
    far = pl.BlockSpec(memory_space=pltpu.HBM)

    def held(space, *arrays):
        return [space(a.shape, a.dtype) for a in arrays] + [
            pltpu.SemaphoreType.DMA((len(arrays),))
        ]

    params = pltpu.CompilerParams(vmem_limit_bytes=24 << 20)
    count = 2 * (ONE + TWO)
    band, taps, turns = pl.pallas_call(
        prep_kernel(bins),
        out_shape=(
            jax.ShapeDtypeStruct((span, 2 * STEP), jnp.bfloat16),
            jax.ShapeDtypeStruct((count, 8, 128), jnp.float32),
            jax.ShapeDtypeStruct((count, 2, ROWS, 128), jnp.float32),
        ),
        in_specs=[far] * 7,
        out_specs=(vmem,) * 3,
        scratch_shapes=held(
            pltpu.VMEM, chirp, shift_one, frac_one, base_one, shift_two, frac_two, base_two
        ),
        compiler_params=params,
        name="prepare",
    )(chirp, shift_one, frac_one, base_one, shift_two, frac_two, base_two)

    scratch = [
        pltpu.VMEM((2, 16, SPANS * WIDE + span - STEP), jnp.bfloat16),
        pltpu.VMEM((WIDE, 128), jnp.float32),
        pltpu.VMEM((16, TALL, 128), jnp.float32),
    ]
    done = pl.pallas_call(
        first_kernel(bins),
        out_shape=jax.ShapeDtypeStruct((ONE, TALL, 128), jnp.float32),
        in_specs=[far] * 2 + [vmem] * 7,
        out_specs=vmem,
        scratch_shapes=scratch + held(pltpu.SMEM, beam_one, shift_one),
        compiler_params=params,
        name="first_pair",
    )(beam_one, shift_one, parts[0], rims[0], parts[1], rims[1], band, taps, turns)
    image = pl.pallas_call(
        second_kernel(bins),
        out_shape=jax.ShapeDtypeStruct((2, 2 * 16, bins), jnp.bfloat16),
        in_specs=[far] * 4 + [vmem] * 8,
        out_specs=vmem,
        scratch_shapes=scratch
        + [
            pltpu.VMEM((2 * ONE, TALL, 128), jnp.float32),
            pltpu.VMEM((16, ROWS, 128), jnp.float32),
        ]
        + held(pltpu.SMEM, beam_one, shift_one, beam_two, shift_two),
        compiler_params=params,
        name="second_pair",
    )(
        beam_one, shift_one, beam_two, shift_two, parts[2], rims[2], parts[3], rims[3], band, taps,
        turns, done,
    )
    return image.transpose(1, 0, 2)[None, None]


def solution(mesh):
    in_specs = (P(("scene", "pulse"), "rep", None, "range"),) + (P(),) * 9
    out_specs = P("rep", ("scene", "pulse"), None, None, "range")
    return jax.shard_map(body, mesh=mesh, in_specs=in_specs, out_specs=out_specs, check_vma=False)
```

```python
import jax
import jax.numpy as jnp
from jax import lax
from jax.experimental import pallas as pl
from jax.experimental.pallas import tpu as pltpu
from jax.sharding import PartitionSpec as P

LEFT = 128
STEP = 128
ROWS = 56
COLS = 64
GROUPS = 16
RIM = 32
WIDE = GROUPS * ROWS
SPANS = COLS // GROUPS
CHUNKS = ROWS // 8
BLOCKS = WIDE // STEP
ONE, TWO = 16, 32
TALL = ROWS + 2 * RIM
TOGETHER = 8


def position():
    rep, pulse = lax.axis_index("rep"), lax.axis_index("pulse")
    low, high = pulse % 2, pulse // 2 % 2
    return 4 * rep + 2 * low + high, low, high


def lane_ids(shape):
    return lax.broadcasted_iota(jnp.int32, shape, len(shape) - 1)


def row_ids(shape):
    return lax.broadcasted_iota(jnp.int32, shape, len(shape) - 2)


def exchange(parts):
    parts = list(parts)
    lane = lane_ids(parts[0].shape)
    step = 1
    while step < len(parts):
        low = (lane & step) == 0
        for first in range(len(parts)):
            if first & step:
                continue
            a, b = parts[first], parts[first + step]
            parts[first] = jnp.where(low, a, pltpu.roll(b, step, 1))
            parts[first + step] = jnp.where(low, pltpu.roll(a, 128 - step, 1), b)
        step *= 2
    return parts


def store_rimmed(ref, index, chunk, value):
    row = 8 * chunk
    ref[index, pl.ds(RIM + row, 8), :] = value
    if row >= ROWS - RIM:
        ref[index, pl.ds(row - (ROWS - RIM), 8), :] = pltpu.roll(value, 1, 1)
    if row < RIM:
        ref[index, pl.ds(RIM + ROWS + row, 8), :] = pltpu.roll(value, 127, 1)


def inside_test(bins):
    first_bin = lax.axis_index("range") * bins
    bin_total = bins * lax.axis_size("range")
    shape = (8, 128)
    place = (lane_ids(shape) & (COLS - 1)) * ROWS + row_ids(shape) + (first_bin - LEFT)

    def inside(chunk, value):
        spot = place + 8 * chunk
        return jnp.where((spot >= 0) & (spot < bin_total), value, 0.0)

    return inside


def fetch(sources, targets, sems):
    copies = [
        pltpu.make_async_copy(source, target, sems.at[index])
        for index, (source, target) in enumerate(zip(sources, targets))
    ]
    for copy in copies:
        copy.start()
    for copy in copies:
        copy.wait()


def prep_kernel(bins):
    def kernel(*refs):
        far, (band_ref, taps_ref, turn_ref) = refs[:7], refs[7:10]
        chirp_ref, shift_one, frac_one, base_one, shift_two, frac_two, base_two = refs[10:17]
        fetch(far, refs[10:17], refs[17])
        own, _, _ = position()
        first_bin = lax.axis_index("range") * bins
        bin_total = bins * lax.axis_size("range")
        span = band_ref.shape[0]
        for part in range(2):
            row = chirp_ref[part : part + 1, :].astype(jnp.float32)
            row = jnp.concatenate([row, jnp.zeros((1, STEP), jnp.float32)], axis=1)
            band = pltpu.roll(jnp.broadcast_to(row, (STEP, span)), 0, 1, stride=1, stride_axis=0)
            for block in range(span // 128):
                turned = band[:, 128 * block : 128 * block + 128].T
                band_ref[pl.ds(128 * block, 128), pl.ds(STEP * part, STEP)] = turned.astype(
                    jnp.bfloat16
                )

        shape = (8, 128)
        lane = lane_ids(shape)

        def packed(first, second):
            total = jnp.zeros(shape, jnp.float32)
            at = 0
            for ref, width in ((first, ONE), (second, TWO)):
                offset = own * width
                for child in range(2):
                    row = ref[child : child + 1, 0:128].astype(jnp.float32)
                    for block in range(1, ref.shape[1] // 128):
                        other = ref[child : child + 1, 128 * block : 128 * block + 128]
                        row = jnp.where(offset // 128 == block, other.astype(jnp.float32), row)
                    row = pltpu.roll(
                        jnp.broadcast_to(row, shape), (at + 256 - offset % 128) % 128, 1
                    )
                    total = jnp.where((lane >= at) & (lane < at + width), row, total)
                    at += width
            return total

        frac = packed(frac_one, frac_two)
        base = packed(base_one, base_two)
        slope = 0.5 * (packed(shift_one, shift_two) + frac)
        row = row_ids(shape).astype(jnp.float32)
        spread = (row - 3.0) - frac
        turned = jnp.pi * spread
        still = turned == 0.0
        safe = jnp.where(still, 1.0, turned)
        weights = jnp.where(still, 1.0, jnp.sin(safe) / safe) * (
            0.54 + 0.46 * jnp.cos(jnp.pi * spread / 4.0)
        )
        count = taps_ref.shape[0]
        square = (128, 128)
        base_rows = jnp.broadcast_to(base[0:1], square).T[:count]
        slope_rows = jnp.broadcast_to(slope[0:1], square).T[:count]
        wide = lane_ids((count, 128))
        spot = (wide & (COLS - 1)) * ROWS + (first_bin - LEFT)
        angle = base_rows + slope_rows * (spot.astype(jnp.float32) / bin_total - 0.5)
        cos_col, sin_col = jnp.cos(angle), jnp.sin(angle)
        sign = jnp.where(lane < COLS, -1.0, 1.0)
        fine, coarse = slope * (row / bin_total), slope * (8.0 / bin_total)
        cos_fine, sin_fine = jnp.cos(fine), jnp.sin(fine)
        cos_coarse, sin_coarse = jnp.cos(coarse), jnp.sin(coarse)
        for place in range(count):

            def spread_out(table):
                return jnp.broadcast_to(table[:, place : place + 1], shape)

            taps_ref[place] = spread_out(weights)
            cos_all = jnp.broadcast_to(cos_col[place : place + 1], shape)
            sin_all = jnp.broadcast_to(sin_col[place : place + 1], shape) * sign
            cos_step, sin_step = spread_out(cos_fine), spread_out(sin_fine) * sign
            cos_next, sin_next = spread_out(cos_coarse), spread_out(sin_coarse) * sign
            for chunk in range(CHUNKS):
                cos_all, sin_all = (
                    cos_all * cos_step - sin_all * sin_step,
                    sin_all * cos_step + cos_all * sin_step,
                )
                turn_ref[place, 0, pl.ds(8 * chunk, 8), :] = cos_all
                turn_ref[place, 1, pl.ds(8 * chunk, 8), :] = sin_all
                cos_step, sin_step = cos_next, sin_next

    return kernel


def compress_pair(near, near_rim, far, far_rim, band_ref, source, columns, images, inside):
    held = near.shape[2]
    rim = near_rim.shape[-1]

    def both(first, second, comp):
        return jnp.concatenate(
            [first[comp].astype(jnp.float32), second[comp].astype(jnp.float32)], axis=0
        ).astype(jnp.bfloat16)

    for comp in range(2):
        sides = both(near_rim, far_rim, comp)
        source[comp, :, pl.ds(0, LEFT)] = sides[:, :LEFT]
        source[comp, :, pl.ds(LEFT, held)] = both(near, far, comp)
        source[comp, :, pl.ds(LEFT + held, rim - LEFT)] = sides[:, LEFT:]
        rest = source.shape[2] - held - rim
        if rest:
            source[comp, :, pl.ds(held + rim, rest)] = jnp.zeros((16, rest), jnp.bfloat16)
    span = band_ref.shape[0]
    windows = jnp.concatenate(
        [
            source[comp, :, pl.ds(WIDE * u + STEP * block, span)]
            for block in range(BLOCKS)
            for comp in range(2)
            for u in range(SPANS)
        ],
        axis=0,
    )
    product = jnp.dot(windows, band_ref[...], preferred_element_type=jnp.float32)
    half = 16 * SPANS
    for block in range(BLOCKS):
        top = product[128 * block : 128 * block + half]
        low = product[128 * block + half : 128 * block + 128]
        result = jnp.concatenate(
            [top[:, :STEP] + low[:, STEP:], low[:, :STEP] - top[:, STEP:]], axis=0
        )
        columns[pl.ds(STEP * block, STEP), :] = result.astype(jnp.bfloat16).T.astype(jnp.float32)
    for chunk in range(0, CHUNKS, 2):
        size = min(2, CHUNKS - chunk) * 8
        parts = [columns[pl.ds(ROWS * g + 8 * chunk, size), :] for g in range(GROUPS)]
        parts = exchange([part.astype(jnp.bfloat16) for part in parts])
        for image, part in enumerate(parts):
            part = part.astype(jnp.float32)
            for extra in range(size // 8):
                value = inside(chunk + extra, part[8 * extra : 8 * extra + 8])
                store_rimmed(images, image, chunk + extra, value)


def merged(images, beam_ref, shift_ref, taps_ref, turn_ref, parent, first_parent, first_child,
           swap, stride, width, at):
    total = [None] * CHUNKS
    for child in range(2):
        place = at + child * width + parent
        image = beam_ref[child, first_parent + parent] - first_child + (child ^ swap) * stride
        start = shift_ref[child, first_parent + parent] + (RIM - 3)
        value = None
        for tap in range(8):
            term = images[image, pl.ds(start + tap, ROWS), :] * taps_ref[place, pl.ds(tap, 1), :]
            value = term if value is None else value + term
        for chunk in range(CHUNKS):
            part = value[8 * chunk : 8 * chunk + 8]
            term = (
                part * turn_ref[place, 0, pl.ds(8 * chunk, 8), :]
                + pltpu.roll(part, COLS, 1) * turn_ref[place, 1, pl.ds(8 * chunk, 8), :]
            )
            total[chunk] = term if total[chunk] is None else total[chunk] + term
    return total


def merge_one(images, beam_ref, shift_ref, taps_ref, turn_ref, result, inside):
    own, low, _ = position()

    def step(index, carry):
        for extra in range(TOGETHER):
            parent = TOGETHER * index + extra
            total = merged(
                images, beam_ref, shift_ref, taps_ref, turn_ref, parent, ONE * own, 8 * own, low, 8,
                ONE, 0,
            )
            for chunk in range(CHUNKS):
                store_rimmed(result, parent, chunk, inside(chunk, total[chunk]))
        return carry

    lax.fori_loop(0, ONE // TOGETHER, step, 0)


def first_kernel(bins):
    def kernel(
        far_beam, far_shift, a0, r0, a1, rims, band_ref, taps_ref, turn_ref, out_ref,
        source, columns, images, beam_ref, shift_ref, sems,
    ):
        inside = inside_test(bins)
        fetch((far_beam, far_shift), (beam_ref, shift_ref), sems)
        compress_pair(a0, r0, a1, rims.at[0], band_ref, source, columns, images, inside)
        merge_one(images, beam_ref, shift_ref, taps_ref, turn_ref, out_ref, inside)

    return kernel


def second_kernel(bins):
    def kernel(
        far_beam_one, far_shift_one, far_beam_two, far_shift_two, a2, r2, a3, rims, band_ref,
        taps_ref, turn_ref, done_ref, out_ref, source, columns, images, level_one, level_two,
        beam_one, shift_one, beam_two, shift_two, sems,
    ):
        inside = inside_test(bins)
        fetch(
            (far_beam_one, far_shift_one, far_beam_two, far_shift_two),
            (beam_one, shift_one, beam_two, shift_two), sems,
        )
        level_one[pl.ds(0, ONE)] = done_ref[...]
        compress_pair(a2, r2.at[0], a3, rims.at[1], band_ref, source, columns, images, inside)
        merge_one(
            images, beam_one, shift_one, taps_ref, turn_ref, level_one.at[pl.ds(ONE, ONE)], inside
        )
        own, _, high = position()
        for half in range(2):

            def step(index, carry):
                for extra in range(TOGETHER):
                    parent = TOGETHER * index + extra
                    total = merged(
                        level_one, beam_two, shift_two, taps_ref, turn_ref, parent + 16 * half,
                        TWO * own, ONE * own, high, ONE, TWO, 2 * ONE,
                    )
                    for chunk in range(CHUNKS):
                        level_two[parent, pl.ds(8 * chunk, 8), :] = total[chunk]
                return carry

            lax.fori_loop(0, 16 // TOGETHER, step, 0)
            for chunk in range(0, CHUNKS, 2):
                size = min(2, CHUNKS - chunk) * 8
                parts = [level_two[image, pl.ds(8 * chunk, size), :] for image in range(GROUPS)]
                parts = exchange([part.astype(jnp.bfloat16) for part in parts])
                for g, part in enumerate(parts):
                    columns[pl.ds(ROWS * g + 8 * chunk, size), :] = part.astype(jnp.float32)
            for block in range(BLOCKS):
                turned = columns[pl.ds(STEP * block, STEP), :].astype(jnp.bfloat16).T
                for comp in range(2):
                    for u in range(SPANS):
                        left = WIDE * u + STEP * block - LEFT
                        if 0 <= left < bins:
                            row = (comp * SPANS + u) * 16
                            out_ref[comp, pl.ds(16 * half, 16), pl.ds(left, 128)] = turned[
                                row : row + 16
                            ]

    return kernel


def neighbours(head, tail, axis):
    count = lax.axis_size(axis)
    even = lax.axis_index(axis) % 2 == 0
    near = [(i, i ^ 1) for i in range(count) if i ^ 1 < count]
    far = [(i + 1, i + 2) for i in range(0, count - 2, 2)]
    far = far + [(b, a) for a, b in far]
    first = lax.ppermute(jnp.where(even, tail, head), axis, near)
    second = lax.ppermute(jnp.where(even, head, tail), axis, far) if far else jnp.zeros_like(first)
    return jnp.where(even, second, first), jnp.where(even, first, second)


def body(
    echo, chirp, beam_one, shift_one, frac_one, base_one, beam_two, shift_two, frac_two, base_two
):
    signal = echo[0]
    beams, _, bins = signal.shape
    span = STEP + chirp.shape[1]
    pulse = lax.axis_index("pulse")

    signal = signal.reshape(4, beams // 4, 2, bins).transpose(0, 2, 1, 3)
    small = (
        chirp, beam_one, shift_one, frac_one, base_one, beam_two, shift_two, frac_two, base_two
    )
    chirp, beam_one, shift_one, frac_one, base_one, beam_two, shift_two, frac_two, base_two = (
        pltpu.with_memory_space_constraint(array, pltpu.HBM) for array in small
    )

    def block_of(array, mask):
        index = pulse ^ mask
        return lax.dynamic_index_in_dim(array, 2 * (index % 2) + index // 2 % 2, 0, keepdims=False)

    def sent(array, mask):
        count = lax.axis_size("pulse")
        return lax.ppermute(array, "pulse", [(i, i ^ mask) for i in range(count)])

    parts = [block_of(signal, 0)]
    parts += [sent(block_of(signal, mask), mask) for mask in (1, 2, 3)]
    from_left, from_right = neighbours(
        signal[:, :, :, :span], signal[:, :, :, bins - span :], "range"
    )
    rims = jnp.concatenate([from_left[:, :, :, span - LEFT :], from_right], axis=3)
    far_rims = sent(jnp.stack([block_of(rims, 2), block_of(rims, 3)]), 2)
    near_rims = sent(jnp.stack([block_of(rims, 1), far_rims[1]]), 1)

    vmem = pl.BlockSpec(memory_space=pltpu.VMEM)
    far = pl.BlockSpec(memory_space=pltpu.HBM)

    def held(space, *arrays):
        return [space(a.shape, a.dtype) for a in arrays] + [
            pltpu.SemaphoreType.DMA((len(arrays),))
        ]

    params = pltpu.CompilerParams(vmem_limit_bytes=24 << 20)
    count = 2 * (ONE + TWO)
    band, taps, turns = pl.pallas_call(
        prep_kernel(bins),
        out_shape=(
            jax.ShapeDtypeStruct((span, 2 * STEP), jnp.bfloat16),
            jax.ShapeDtypeStruct((count, 8, 128), jnp.float32),
            jax.ShapeDtypeStruct((count, 2, ROWS, 128), jnp.float32),
        ),
        in_specs=[far] * 7,
        out_specs=(vmem,) * 3,
        scratch_shapes=held(
            pltpu.VMEM, chirp, shift_one, frac_one, base_one, shift_two, frac_two, base_two
        ),
        compiler_params=params,
        name="prepare",
    )(chirp, shift_one, frac_one, base_one, shift_two, frac_two, base_two)

    scratch = [
        pltpu.VMEM((2, 16, SPANS * WIDE + span - STEP), jnp.bfloat16),
        pltpu.VMEM((WIDE, 128), jnp.float32),
        pltpu.VMEM((16, TALL, 128), jnp.float32),
    ]
    done = pl.pallas_call(
        first_kernel(bins),
        out_shape=jax.ShapeDtypeStruct((ONE, TALL, 128), jnp.float32),
        in_specs=[far] * 2 + [vmem] * 7,
        out_specs=vmem,
        scratch_shapes=scratch + held(pltpu.SMEM, beam_one, shift_one),
        compiler_params=params,
        name="first_pair",
    )(beam_one, shift_one, parts[0], block_of(rims, 0), parts[1], near_rims, band, taps, turns)
    image = pl.pallas_call(
        second_kernel(bins),
        out_shape=jax.ShapeDtypeStruct((2, 2 * 16, bins), jnp.bfloat16),
        in_specs=[far] * 4 + [vmem] * 8,
        out_specs=vmem,
        scratch_shapes=scratch
        + [
            pltpu.VMEM((2 * ONE, TALL, 128), jnp.float32),
            pltpu.VMEM((16, ROWS, 128), jnp.float32),
        ]
        + held(pltpu.SMEM, beam_one, shift_one, beam_two, shift_two),
        compiler_params=params,
        name="second_pair",
    )(
        beam_one, shift_one, beam_two, shift_two, parts[2], far_rims, parts[3], near_rims, band, taps,
        turns, done,
    )
    return image.transpose(1, 0, 2)[None, None]


def solution(mesh):
    in_specs = (P(("scene", "pulse"), "rep", None, "range"),) + (P(),) * 9
    out_specs = P("rep", ("scene", "pulse"), None, None, "range")

    return jax.shard_map(body, mesh=mesh, in_specs=in_specs, out_specs=out_specs, check_vma=False)
```

```python
import jax
import jax.numpy as jnp
from jax import lax
from jax.experimental import pallas as pl
from jax.experimental.pallas import tpu as pltpu
from jax.sharding import PartitionSpec as P

LEFT = 128
STEP = 128
ROWS = 56
COLS = 64
GROUPS = 16
RIM = 32
WIDE = GROUPS * ROWS
SPANS = COLS // GROUPS
CHUNKS = ROWS // 8
BLOCKS = WIDE // STEP
ONE, TWO = 16, 32
TALL = ROWS + 2 * RIM
TOGETHER = 8


def position():
    rep, pulse = lax.axis_index("rep"), lax.axis_index("pulse")
    low, high = pulse % 2, pulse // 2 % 2
    return 4 * rep + 2 * low + high, low, high


def lane_ids(shape):
    return lax.broadcasted_iota(jnp.int32, shape, len(shape) - 1)


def row_ids(shape):
    return lax.broadcasted_iota(jnp.int32, shape, len(shape) - 2)


def exchange(parts):
    parts = list(parts)
    lane = lane_ids(parts[0].shape)
    step = 1
    while step < len(parts):
        low = (lane & step) == 0
        for first in range(len(parts)):
            if first & step:
                continue
            a, b = parts[first], parts[first + step]
            parts[first] = jnp.where(low, a, pltpu.roll(b, step, 1))
            parts[first + step] = jnp.where(low, pltpu.roll(a, 128 - step, 1), b)
        step *= 2
    return parts


def store_rimmed(ref, index, chunk, value):
    row = 8 * chunk
    ref[index, pl.ds(RIM + row, 8), :] = value
    if row >= ROWS - RIM:
        ref[index, pl.ds(row - (ROWS - RIM), 8), :] = pltpu.roll(value, 1, 1)
    if row < RIM:
        ref[index, pl.ds(RIM + ROWS + row, 8), :] = pltpu.roll(value, 127, 1)


def inside_test(bins):
    first_bin = lax.axis_index("range") * bins
    bin_total = bins * lax.axis_size("range")
    shape = (8, 128)
    place = (lane_ids(shape) & (COLS - 1)) * ROWS + row_ids(shape) + (first_bin - LEFT)

    def inside(chunk, value):
        spot = place + 8 * chunk
        return jnp.where((spot >= 0) & (spot < bin_total), value, 0.0)

    return inside


def fetch(sources, targets, sems):
    copies = [
        pltpu.make_async_copy(source, target, sems.at[index])
        for index, (source, target) in enumerate(zip(sources, targets))
    ]
    for copy in copies:
        copy.start()
    for copy in copies:
        copy.wait()


def prep_kernel(bins):
    def kernel(*refs):
        far, (band_ref, taps_ref, turn_ref) = refs[:7], refs[7:10]
        chirp_ref, shift_one, frac_one, base_one, shift_two, frac_two, base_two = refs[10:17]
        fetch(far, refs[10:17], refs[17])
        own, _, _ = position()
        first_bin = lax.axis_index("range") * bins
        bin_total = bins * lax.axis_size("range")
        span = band_ref.shape[0]
        for part in range(2):
            row = chirp_ref[part : part + 1, :].astype(jnp.float32)
            row = jnp.concatenate([row, jnp.zeros((1, STEP), jnp.float32)], axis=1)
            band = pltpu.roll(jnp.broadcast_to(row, (STEP, span)), 0, 1, stride=1, stride_axis=0)
            for block in range(span // 128):
                turned = band[:, 128 * block : 128 * block + 128].T
                band_ref[pl.ds(128 * block, 128), pl.ds(STEP * part, STEP)] = turned.astype(
                    jnp.bfloat16
                )

        shape = (8, 128)
        lane = lane_ids(shape)

        def packed(first, second):
            total = jnp.zeros(shape, jnp.float32)
            at = 0
            for ref, width in ((first, ONE), (second, TWO)):
                offset = own * width
                for child in range(2):
                    row = ref[child : child + 1, 0:128].astype(jnp.float32)
                    for block in range(1, ref.shape[1] // 128):
                        other = ref[child : child + 1, 128 * block : 128 * block + 128]
                        row = jnp.where(offset // 128 == block, other.astype(jnp.float32), row)
                    row = pltpu.roll(
                        jnp.broadcast_to(row, shape), (at + 256 - offset % 128) % 128, 1
                    )
                    total = jnp.where((lane >= at) & (lane < at + width), row, total)
                    at += width
            return total

        frac = packed(frac_one, frac_two)
        base = packed(base_one, base_two)
        slope = 0.5 * (packed(shift_one, shift_two) + frac)
        row = row_ids(shape).astype(jnp.float32)
        spread = (row - 3.0) - frac
        turned = jnp.pi * spread
        still = turned == 0.0
        safe = jnp.where(still, 1.0, turned)
        weights = jnp.where(still, 1.0, jnp.sin(safe) / safe) * (
            0.54 + 0.46 * jnp.cos(jnp.pi * spread / 4.0)
        )
        count = taps_ref.shape[0]
        square = (128, 128)
        base_rows = jnp.broadcast_to(base[0:1], square).T[:count]
        slope_rows = jnp.broadcast_to(slope[0:1], square).T[:count]
        wide = lane_ids((count, 128))
        spot = (wide & (COLS - 1)) * ROWS + (first_bin - LEFT)
        angle = base_rows + slope_rows * (spot.astype(jnp.float32) / bin_total - 0.5)
        cos_col, sin_col = jnp.cos(angle), jnp.sin(angle)
        sign = jnp.where(lane < COLS, -1.0, 1.0)
        fine, coarse = slope * (row / bin_total), slope * (8.0 / bin_total)
        cos_fine, sin_fine = jnp.cos(fine), jnp.sin(fine)
        cos_coarse, sin_coarse = jnp.cos(coarse), jnp.sin(coarse)
        for place in range(count):

            def spread_out(table):
                return jnp.broadcast_to(table[:, place : place + 1], shape)

            taps_ref[place] = spread_out(weights)
            cos_all = jnp.broadcast_to(cos_col[place : place + 1], shape)
            sin_all = jnp.broadcast_to(sin_col[place : place + 1], shape) * sign
            cos_step, sin_step = spread_out(cos_fine), spread_out(sin_fine) * sign
            cos_next, sin_next = spread_out(cos_coarse), spread_out(sin_coarse) * sign
            for chunk in range(CHUNKS):
                cos_all, sin_all = (
                    cos_all * cos_step - sin_all * sin_step,
                    sin_all * cos_step + cos_all * sin_step,
                )
                turn_ref[place, 0, pl.ds(8 * chunk, 8), :] = cos_all
                turn_ref[place, 1, pl.ds(8 * chunk, 8), :] = sin_all
                cos_step, sin_step = cos_next, sin_next

    return kernel


def compress_pair(near, far, bins, band_ref, source, columns, images, inside):
    rest = source.shape[2] - LEFT - bins
    wide = near[0].shape[2] - LEFT - bins

    def piece(held, comp, at, size):
        if len(held) == 1:
            return held[0][comp, :, pl.ds(at, size)]
        main, rim = held
        if at == LEFT:
            return main[comp]
        return rim[comp, :, pl.ds(min(at, LEFT), size)]

    for comp in range(2):
        for at, size in ((0, LEFT), (LEFT, bins), (LEFT + bins, wide)):
            sides = [piece(held, comp, at, size).astype(jnp.float32) for held in (near, far)]
            source[comp, :, pl.ds(at, size)] = jnp.concatenate(sides, axis=0).astype(jnp.bfloat16)
        if rest > wide:
            source[comp, :, pl.ds(LEFT + bins + wide, rest - wide)] = jnp.zeros(
                (16, rest - wide), jnp.bfloat16
            )
    span = band_ref.shape[0]
    windows = jnp.concatenate(
        [
            source[comp, :, pl.ds(WIDE * u + STEP * block, span)]
            for block in range(BLOCKS)
            for comp in range(2)
            for u in range(SPANS)
        ],
        axis=0,
    )
    product = jnp.dot(windows, band_ref[...], preferred_element_type=jnp.float32)
    half = 16 * SPANS
    for block in range(BLOCKS):
        top = product[128 * block : 128 * block + half]
        low = product[128 * block + half : 128 * block + 128]
        result = jnp.concatenate(
            [top[:, :STEP] + low[:, STEP:], low[:, :STEP] - top[:, STEP:]], axis=0
        )
        columns[pl.ds(STEP * block, STEP), :] = result.astype(jnp.bfloat16).T.astype(jnp.float32)
    for chunk in range(0, CHUNKS, 2):
        size = min(2, CHUNKS - chunk) * 8
        parts = [columns[pl.ds(ROWS * g + 8 * chunk, size), :] for g in range(GROUPS)]
        parts = exchange([part.astype(jnp.bfloat16) for part in parts])
        for image, part in enumerate(parts):
            part = part.astype(jnp.float32)
            for extra in range(size // 8):
                value = inside(chunk + extra, part[8 * extra : 8 * extra + 8])
                store_rimmed(images, image, chunk + extra, value)


def merged(images, beam_ref, shift_ref, taps_ref, turn_ref, parent, first_parent, first_child,
           swap, stride, width, at):
    total = [None] * CHUNKS
    for child in range(2):
        place = at + child * width + parent
        image = beam_ref[child, first_parent + parent] - first_child + (child ^ swap) * stride
        start = shift_ref[child, first_parent + parent] + (RIM - 3)
        value = None
        for tap in range(8):
            term = images[image, pl.ds(start + tap, ROWS), :] * taps_ref[place, pl.ds(tap, 1), :]
            value = term if value is None else value + term
        for chunk in range(CHUNKS):
            part = value[8 * chunk : 8 * chunk + 8]
            term = (
                part * turn_ref[place, 0, pl.ds(8 * chunk, 8), :]
                + pltpu.roll(part, COLS, 1) * turn_ref[place, 1, pl.ds(8 * chunk, 8), :]
            )
            total[chunk] = term if total[chunk] is None else total[chunk] + term
    return total


def merge_one(images, beam_ref, shift_ref, taps_ref, turn_ref, result, inside):
    own, low, _ = position()

    def step(index, carry):
        for extra in range(TOGETHER):
            parent = TOGETHER * index + extra
            total = merged(
                images, beam_ref, shift_ref, taps_ref, turn_ref, parent, ONE * own, 8 * own, low, 8,
                ONE, 0,
            )
            for chunk in range(CHUNKS):
                store_rimmed(result, parent, chunk, inside(chunk, total[chunk]))
        return carry

    lax.fori_loop(0, ONE // TOGETHER, step, 0)


def first_kernel(bins):
    def kernel(
        far_beam, far_shift, a0, a1, band_ref, taps_ref, turn_ref, out_ref,
        source, columns, images, beam_ref, shift_ref, sems,
    ):
        inside = inside_test(bins)
        fetch((far_beam, far_shift), (beam_ref, shift_ref), sems)
        compress_pair((a0,), (a1,), bins, band_ref, source, columns, images, inside)
        merge_one(images, beam_ref, shift_ref, taps_ref, turn_ref, out_ref, inside)

    return kernel


def second_kernel(bins):
    def kernel(
        far_beam_one, far_shift_one, far_beam_two, far_shift_two, a2, a3, r3, band_ref,
        taps_ref, turn_ref, done_ref, out_ref, source, columns, images, level_one, level_two,
        beam_one, shift_one, beam_two, shift_two, sems,
    ):
        inside = inside_test(bins)
        fetch(
            (far_beam_one, far_shift_one, far_beam_two, far_shift_two),
            (beam_one, shift_one, beam_two, shift_two), sems,
        )
        level_one[pl.ds(0, ONE)] = done_ref[...]
        compress_pair((a2,), (a3, r3), bins, band_ref, source, columns, images, inside)
        merge_one(
            images, beam_one, shift_one, taps_ref, turn_ref, level_one.at[pl.ds(ONE, ONE)], inside
        )
        own, _, high = position()
        for half in range(2):

            def step(index, carry):
                for extra in range(TOGETHER):
                    parent = TOGETHER * index + extra
                    total = merged(
                        level_one, beam_two, shift_two, taps_ref, turn_ref, parent + 16 * half,
                        TWO * own, ONE * own, high, ONE, TWO, 2 * ONE,
                    )
                    for chunk in range(CHUNKS):
                        level_two[parent, pl.ds(8 * chunk, 8), :] = total[chunk]
                return carry

            lax.fori_loop(0, 16 // TOGETHER, step, 0)
            for chunk in range(0, CHUNKS, 2):
                size = min(2, CHUNKS - chunk) * 8
                parts = [level_two[image, pl.ds(8 * chunk, size), :] for image in range(GROUPS)]
                parts = exchange([part.astype(jnp.bfloat16) for part in parts])
                for g, part in enumerate(parts):
                    columns[pl.ds(ROWS * g + 8 * chunk, size), :] = part.astype(jnp.float32)
            for block in range(BLOCKS):
                turned = columns[pl.ds(STEP * block, STEP), :].astype(jnp.bfloat16).T
                for comp in range(2):
                    for u in range(SPANS):
                        left = WIDE * u + STEP * block - LEFT
                        if 0 <= left < bins:
                            row = (comp * SPANS + u) * 16
                            out_ref[comp, pl.ds(16 * half, 16), pl.ds(left, 128)] = turned[
                                row : row + 16
                            ]

    return kernel


def neighbours(head, tail, axis):
    count = lax.axis_size(axis)
    even = lax.axis_index(axis) % 2 == 0
    near = [(i, i ^ 1) for i in range(count) if i ^ 1 < count]
    far = [(i + 1, i + 2) for i in range(0, count - 2, 2)]
    far = far + [(b, a) for a, b in far]
    first = lax.ppermute(jnp.where(even, tail, head), axis, near)
    second = lax.ppermute(jnp.where(even, head, tail), axis, far) if far else jnp.zeros_like(first)
    return jnp.where(even, second, first), jnp.where(even, first, second)


def body(
    echo, chirp, beam_one, shift_one, frac_one, base_one, beam_two, shift_two, frac_two, base_two
):
    signal = echo[0]
    beams, _, bins = signal.shape
    span = STEP + chirp.shape[1]
    pulse = lax.axis_index("pulse")

    signal = signal.reshape(4, beams // 4, 2, bins).transpose(0, 2, 1, 3)
    small = (
        chirp, beam_one, shift_one, frac_one, base_one, beam_two, shift_two, frac_two, base_two
    )
    chirp, beam_one, shift_one, frac_one, base_one, beam_two, shift_two, frac_two, base_two = (
        pltpu.with_memory_space_constraint(array, pltpu.HBM) for array in small
    )

    def block_of(array, mask):
        index = pulse ^ mask
        return lax.dynamic_index_in_dim(array, 2 * (index % 2) + index // 2 % 2, 0, keepdims=False)

    def sent(array, mask):
        count = lax.axis_size("pulse")
        return lax.ppermute(array, "pulse", [(i, i ^ mask) for i in range(count)])

    far_main = sent(block_of(signal, 3), 3)
    from_left, from_right = neighbours(
        signal[:, :, :, :span], signal[:, :, :, bins - span :], "range"
    )
    from_left = from_left[:, :, :, span - LEFT :]
    wide = jnp.concatenate([from_left, signal, from_right], axis=3)
    rims = jnp.concatenate([from_left, from_right], axis=3)
    parts = [block_of(wide, 0)] + [sent(block_of(wide, mask), mask) for mask in (1, 2)]
    far_rim = sent(block_of(rims, 3), 3)

    vmem = pl.BlockSpec(memory_space=pltpu.VMEM)
    far = pl.BlockSpec(memory_space=pltpu.HBM)

    def held(space, *arrays):
        return [space(a.shape, a.dtype) for a in arrays] + [
            pltpu.SemaphoreType.DMA((len(arrays),))
        ]

    params = pltpu.CompilerParams(vmem_limit_bytes=24 << 20)
    count = 2 * (ONE + TWO)
    band, taps, turns = pl.pallas_call(
        prep_kernel(bins),
        out_shape=(
            jax.ShapeDtypeStruct((span, 2 * STEP), jnp.bfloat16),
            jax.ShapeDtypeStruct((count, 8, 128), jnp.float32),
            jax.ShapeDtypeStruct((count, 2, ROWS, 128), jnp.float32),
        ),
        in_specs=[far] * 7,
        out_specs=(vmem,) * 3,
        scratch_shapes=held(
            pltpu.VMEM, chirp, shift_one, frac_one, base_one, shift_two, frac_two, base_two
        ),
        compiler_params=params,
        name="prepare",
    )(chirp, shift_one, frac_one, base_one, shift_two, frac_two, base_two)

    scratch = [
        pltpu.VMEM((2, 16, SPANS * WIDE + span - STEP), jnp.bfloat16),
        pltpu.VMEM((WIDE, 128), jnp.float32),
        pltpu.VMEM((16, TALL, 128), jnp.float32),
    ]
    done = pl.pallas_call(
        first_kernel(bins),
        out_shape=jax.ShapeDtypeStruct((ONE, TALL, 128), jnp.float32),
        in_specs=[far] * 2 + [vmem] * 5,
        out_specs=vmem,
        scratch_shapes=scratch + held(pltpu.SMEM, beam_one, shift_one),
        compiler_params=params,
        name="first_pair",
    )(beam_one, shift_one, parts[0], parts[1], band, taps, turns)
    image = pl.pallas_call(
        second_kernel(bins),
        out_shape=jax.ShapeDtypeStruct((2, 2 * 16, bins), jnp.bfloat16),
        in_specs=[far] * 4 + [vmem] * 7,
        out_specs=vmem,
        scratch_shapes=scratch
        + [
            pltpu.VMEM((2 * ONE, TALL, 128), jnp.float32),
            pltpu.VMEM((16, ROWS, 128), jnp.float32),
        ]
        + held(pltpu.SMEM, beam_one, shift_one, beam_two, shift_two),
        compiler_params=params,
        name="second_pair",
    )(
        beam_one, shift_one, beam_two, shift_two, parts[2], far_main, far_rim, band, taps,
        turns, done,
    )
    return image.transpose(1, 0, 2)[None, None]


def solution(mesh):
    in_specs = (P(("scene", "pulse"), "rep", None, "range"),) + (P(),) * 9
    out_specs = P("rep", ("scene", "pulse"), None, None, "range")

    return jax.shard_map(body, mesh=mesh, in_specs=in_specs, out_specs=out_specs, check_vma=False)
```

```python
import jax
import jax.numpy as jnp
from jax import lax
from jax.experimental import pallas as pl
from jax.experimental.layout import Layout, with_layout_constraint
from jax.experimental.pallas import tpu as pltpu
from jax.sharding import PartitionSpec as P

LEFT = 128
STEP = 128
ROWS = 56
COLS = 64
GROUPS = 16
RIM = 32
WIDE = GROUPS * ROWS
SPANS = COLS // GROUPS
CHUNKS = ROWS // 8
BLOCKS = WIDE // STEP
ONE, TWO = 16, 32
TALL = ROWS + 2 * RIM
TOGETHER = 16


def position():
    rep, pulse = lax.axis_index("rep"), lax.axis_index("pulse")
    low, high = pulse % 2, pulse // 2 % 2
    return 4 * rep + 2 * low + high, low, high


def lane_ids(shape):
    return lax.broadcasted_iota(jnp.int32, shape, len(shape) - 1)


def row_ids(shape):
    return lax.broadcasted_iota(jnp.int32, shape, len(shape) - 2)


def exchange(parts):
    parts = list(parts)
    lane = lane_ids(parts[0].shape)
    step = 1
    while step < len(parts):
        low = (lane & step) == 0
        for first in range(len(parts)):
            if first & step:
                continue
            a, b = parts[first], parts[first + step]
            parts[first] = jnp.where(low, a, pltpu.roll(b, step, 1))
            parts[first + step] = jnp.where(low, pltpu.roll(a, 128 - step, 1), b)
        step *= 2
    return parts


def store_rimmed(ref, index, chunk, value):
    row = 8 * chunk
    ref[index, pl.ds(RIM + row, 8), :] = value
    if row >= ROWS - RIM:
        ref[index, pl.ds(row - (ROWS - RIM), 8), :] = pltpu.roll(value, 1, 1)
    if row < RIM:
        ref[index, pl.ds(RIM + ROWS + row, 8), :] = pltpu.roll(value, 127, 1)


def inside_test(bins):
    first_bin = lax.axis_index("range") * bins
    bin_total = bins * lax.axis_size("range")
    shape = (8, 128)
    place = (lane_ids(shape) & (COLS - 1)) * ROWS + row_ids(shape) + (first_bin - LEFT)

    def inside(chunk, value):
        spot = place + 8 * chunk
        return jnp.where((spot >= 0) & (spot < bin_total), value, 0.0)

    return inside


def fetch(sources, targets, sems):
    copies = [
        pltpu.make_async_copy(source, target, sems.at[index])
        for index, (source, target) in enumerate(zip(sources, targets))
    ]
    for copy in copies:
        copy.start()
    for copy in copies:
        copy.wait()


def prep_kernel(bins):
    def kernel(*refs):
        far, (band_ref, taps_ref, turn_ref) = refs[:7], refs[7:10]
        chirp_ref, shift_one, frac_one, base_one, shift_two, frac_two, base_two = refs[10:17]
        fetch(far, refs[10:17], refs[17])
        own, _, _ = position()
        first_bin = lax.axis_index("range") * bins
        bin_total = bins * lax.axis_size("range")
        span = band_ref.shape[0]
        for part in range(2):
            row = chirp_ref[part : part + 1, :].astype(jnp.float32)
            row = jnp.concatenate([row, jnp.zeros((1, STEP), jnp.float32)], axis=1)
            band = pltpu.roll(jnp.broadcast_to(row, (STEP, span)), 0, 1, stride=1, stride_axis=0)
            for block in range(span // 128):
                turned = band[:, 128 * block : 128 * block + 128].T
                band_ref[pl.ds(128 * block, 128), pl.ds(STEP * part, STEP)] = turned.astype(
                    jnp.bfloat16
                )

        shape = (8, 128)
        lane = lane_ids(shape)

        def packed(first, second):
            total = jnp.zeros(shape, jnp.float32)
            at = 0
            for ref, width in ((first, ONE), (second, TWO)):
                offset = own * width
                for child in range(2):
                    row = ref[child : child + 1, 0:128].astype(jnp.float32)
                    for block in range(1, ref.shape[1] // 128):
                        other = ref[child : child + 1, 128 * block : 128 * block + 128]
                        row = jnp.where(offset // 128 == block, other.astype(jnp.float32), row)
                    row = pltpu.roll(
                        jnp.broadcast_to(row, shape), (at + 256 - offset % 128) % 128, 1
                    )
                    total = jnp.where((lane >= at) & (lane < at + width), row, total)
                    at += width
            return total

        frac = packed(frac_one, frac_two)
        base = packed(base_one, base_two)
        slope = 0.5 * (packed(shift_one, shift_two) + frac)
        row = row_ids(shape).astype(jnp.float32)
        spread = (row - 3.0) - frac
        turned = jnp.pi * spread
        still = turned == 0.0
        safe = jnp.where(still, 1.0, turned)
        weights = jnp.where(still, 1.0, jnp.sin(safe) / safe) * (
            0.54 + 0.46 * jnp.cos(jnp.pi * spread / 4.0)
        )
        count = taps_ref.shape[0]
        square = (128, 128)
        base_rows = jnp.broadcast_to(base[0:1], square).T[:count]
        slope_rows = jnp.broadcast_to(slope[0:1], square).T[:count]
        wide = lane_ids((count, 128))
        spot = (wide & (COLS - 1)) * ROWS + (first_bin - LEFT)
        angle = base_rows + slope_rows * (spot.astype(jnp.float32) / bin_total - 0.5)
        cos_col, sin_col = jnp.cos(angle), jnp.sin(angle)
        sign = jnp.where(lane < COLS, -1.0, 1.0)
        fine, coarse = slope * (row / bin_total), slope * (8.0 / bin_total)
        cos_fine, sin_fine = jnp.cos(fine), jnp.sin(fine)
        cos_coarse, sin_coarse = jnp.cos(coarse), jnp.sin(coarse)
        for place in range(count):

            def spread_out(table):
                return jnp.broadcast_to(table[:, place : place + 1], shape)

            taps_ref[place] = spread_out(weights)
            cos_all = jnp.broadcast_to(cos_col[place : place + 1], shape)
            sin_all = jnp.broadcast_to(sin_col[place : place + 1], shape) * sign
            cos_step, sin_step = spread_out(cos_fine), spread_out(sin_fine) * sign
            cos_next, sin_next = spread_out(cos_coarse), spread_out(sin_coarse) * sign
            for chunk in range(CHUNKS):
                cos_all, sin_all = (
                    cos_all * cos_step - sin_all * sin_step,
                    sin_all * cos_step + cos_all * sin_step,
                )
                turn_ref[place, 0, pl.ds(8 * chunk, 8), :] = cos_all
                turn_ref[place, 1, pl.ds(8 * chunk, 8), :] = sin_all
                cos_step, sin_step = cos_next, sin_next

    return kernel


def compress_pair(near, far, bins, band_ref, source, columns, images, inside):
    rest = source.shape[2] - LEFT - bins
    wide = near[0].shape[2] - LEFT - bins

    def piece(held, comp, at, size):
        if len(held) == 1:
            return held[0][comp, :, pl.ds(at, size)]
        main, rim = held
        if at == LEFT:
            return main[comp]
        return rim[comp, :, pl.ds(min(at, LEFT), size)]

    for comp in range(2):
        for at, size in ((0, LEFT), (LEFT, bins), (LEFT + bins, wide)):
            sides = [piece(held, comp, at, size).astype(jnp.float32) for held in (near, far)]
            source[comp, :, pl.ds(at, size)] = jnp.concatenate(sides, axis=0).astype(jnp.bfloat16)
        if rest > wide:
            source[comp, :, pl.ds(LEFT + bins + wide, rest - wide)] = jnp.zeros(
                (16, rest - wide), jnp.bfloat16
            )
    span = band_ref.shape[0]
    windows = jnp.concatenate(
        [
            source[comp, :, pl.ds(WIDE * u + STEP * block, span)]
            for block in range(BLOCKS)
            for comp in range(2)
            for u in range(SPANS)
        ],
        axis=0,
    )
    product = jnp.dot(windows, band_ref[...], preferred_element_type=jnp.float32)
    half = 16 * SPANS
    for block in range(BLOCKS):
        top = product[128 * block : 128 * block + half]
        low = product[128 * block + half : 128 * block + 128]
        result = jnp.concatenate(
            [top[:, :STEP] + low[:, STEP:], low[:, :STEP] - top[:, STEP:]], axis=0
        )
        columns[pl.ds(STEP * block, STEP), :] = result.astype(jnp.bfloat16).T.astype(jnp.float32)
    for chunk in range(0, CHUNKS, 2):
        size = min(2, CHUNKS - chunk) * 8
        parts = [columns[pl.ds(ROWS * g + 8 * chunk, size), :] for g in range(GROUPS)]
        parts = exchange([part.astype(jnp.bfloat16) for part in parts])
        for image, part in enumerate(parts):
            part = part.astype(jnp.float32)
            for extra in range(size // 8):
                value = inside(chunk + extra, part[8 * extra : 8 * extra + 8])
                store_rimmed(images, image, chunk + extra, value)


def contribution(images, tables, parent, child, first_parent, first_image, width, at):
    beam_ref, shift_ref, taps_ref, turn_ref = tables
    place = at + child * width + parent
    image = beam_ref[child, first_parent + parent] + first_image
    start = shift_ref[child, first_parent + parent] + (RIM - 3)
    value = None
    for tap in range(8):
        term = images[image, pl.ds(start + tap, ROWS), :] * taps_ref[place, pl.ds(tap, 1), :]
        value = term if value is None else value + term
    parts = []
    for chunk in range(CHUNKS):
        part = value[8 * chunk : 8 * chunk + 8]
        parts.append(
            part * turn_ref[place, 0, pl.ds(8 * chunk, 8), :]
            + pltpu.roll(part, COLS, 1) * turn_ref[place, 1, pl.ds(8 * chunk, 8), :]
        )
    return parts


def loop_over(count, one):
    def step(index, carry):
        for extra in range(TOGETHER):
            one(TOGETHER * index + extra)
        return carry

    lax.fori_loop(0, count // TOGETHER, step, 0)


def merge_one(images, tables, result, inside):
    own, low, _ = position()

    def one(parent):
        sides = [
            contribution(
                images, tables, parent, child, ONE * own, (child ^ low) * 8 - 8 * own, ONE, 0
            )
            for child in range(2)
        ]
        for chunk, (a, b) in enumerate(zip(*sides)):
            store_rimmed(result, parent, chunk, inside(chunk, a + b))

    loop_over(ONE, one)


def second_side(images, tables, parent, child):
    own, _, _ = position()
    return contribution(images, tables, parent, child, TWO * own, -ONE * own, TWO, 2 * ONE)


def first_kernel(bins):
    def kernel(
        far_beam_one, far_shift_one, far_beam_two, far_shift_two, a0, a1, band_ref, taps_ref,
        turn_ref, out_ref, source, columns, images, level_one, beam_one, shift_one, beam_two,
        shift_two, sems,
    ):
        inside = inside_test(bins)
        fetch(
            (far_beam_one, far_shift_one, far_beam_two, far_shift_two),
            (beam_one, shift_one, beam_two, shift_two), sems,
        )
        compress_pair((a0,), (a1,), bins, band_ref, source, columns, images, inside)
        merge_one(images, (beam_one, shift_one, taps_ref, turn_ref), level_one, inside)
        _, _, high = position()
        tables = (beam_two, shift_two, taps_ref, turn_ref)

        def one(parent):
            for chunk, part in enumerate(second_side(level_one, tables, parent, high)):
                out_ref[parent, pl.ds(8 * chunk, 8), :] = part

        loop_over(TWO, one)

    return kernel


def second_kernel(bins):
    def kernel(
        far_beam_one, far_shift_one, far_beam_two, far_shift_two, a2, a3, r3, band_ref, taps_ref,
        turn_ref, half_ref, out_ref, source, columns, images, level_one, beam_one, shift_one,
        beam_two, shift_two, sems, level_two,
    ):
        inside = inside_test(bins)
        fetch(
            (far_beam_one, far_shift_one, far_beam_two, far_shift_two),
            (beam_one, shift_one, beam_two, shift_two), sems,
        )
        compress_pair((a2,), (a3, r3), bins, band_ref, source, columns, images, inside)
        merge_one(images, (beam_one, shift_one, taps_ref, turn_ref), level_one, inside)
        _, _, high = position()
        tables = (beam_two, shift_two, taps_ref, turn_ref)

        def one(parent):
            for chunk, part in enumerate(second_side(level_one, tables, parent, 1 - high)):
                rows = pl.ds(8 * chunk, 8)
                level_two[parent, rows, :] = part + half_ref[parent, rows, :]

        loop_over(TWO, one)
        for half in range(2):
            for chunk in range(0, CHUNKS, 2):
                size = min(2, CHUNKS - chunk) * 8
                parts = [
                    level_two[16 * half + image, pl.ds(8 * chunk, size), :].astype(jnp.bfloat16)
                    for image in range(GROUPS)
                ]
                for g, part in enumerate(exchange(parts)):
                    columns[pl.ds(ROWS * g + 8 * chunk, size), :] = part.astype(jnp.float32)
            for block in range(BLOCKS):
                turned = columns[pl.ds(STEP * block, STEP), :].astype(jnp.bfloat16).T
                for comp in range(2):
                    for u in range(SPANS):
                        left = WIDE * u + STEP * block - LEFT
                        if 0 <= left < bins:
                            row = (comp * SPANS + u) * 16
                            out_ref[comp, pl.ds(16 * half, 16), pl.ds(left, 128)] = turned[
                                row : row + 16
                            ]

    return kernel


def neighbours(head, tail, axis):
    count = lax.axis_size(axis)
    even = lax.axis_index(axis) % 2 == 0
    order = Layout(tuple(range(head.ndim)))
    near = [(i, i ^ 1) for i in range(count) if i ^ 1 < count]
    far = [(i + 1, i + 2) for i in range(0, count - 2, 2)]
    far = far + [(b, a) for a, b in far]
    first = with_layout_constraint(jnp.where(even, tail, head), order)
    first = with_layout_constraint(lax.ppermute(first, axis, near), order)
    second = lax.ppermute(jnp.where(even, head, tail), axis, far) if far else jnp.zeros_like(first)
    return jnp.where(even, second, first), jnp.where(even, first, second)


def body(
    echo, chirp, beam_one, shift_one, frac_one, base_one, beam_two, shift_two, frac_two, base_two
):
    signal = echo[0]
    beams, _, bins = signal.shape

    def split(array):
        return array.reshape(4, beams // 4, 2, array.shape[2]).transpose(0, 2, 1, 3)

    span = STEP + chirp.shape[1]
    pulse = lax.axis_index("pulse")

    from_left, from_right = (
        split(side) for side in neighbours(signal[:, :, :span], signal[:, :, bins - span :], "range")
    )
    signal = split(signal)
    small = (
        chirp, beam_one, shift_one, frac_one, base_one, beam_two, shift_two, frac_two, base_two
    )
    chirp, beam_one, shift_one, frac_one, base_one, beam_two, shift_two, frac_two, base_two = (
        pltpu.with_memory_space_constraint(array, pltpu.HBM) for array in small
    )

    def block_of(array, mask):
        index = pulse ^ mask
        return lax.dynamic_index_in_dim(array, 2 * (index % 2) + index // 2 % 2, 0, keepdims=False)

    def sent(array, mask):
        count = lax.axis_size("pulse")
        return lax.ppermute(array, "pulse", [(i, i ^ mask) for i in range(count)])

    far_main = sent(block_of(signal, 3), 3)
    from_left = from_left[:, :, :, span - LEFT :]
    wide = jnp.concatenate([from_left, signal, from_right], axis=3)
    rims = jnp.concatenate([from_left, from_right], axis=3)
    parts = [block_of(wide, 0)] + [sent(block_of(wide, mask), mask) for mask in (1, 2)]
    far_rim = sent(block_of(rims, 3), 3)

    vmem = pl.BlockSpec(memory_space=pltpu.VMEM)
    far = pl.BlockSpec(memory_space=pltpu.HBM)

    def held(space, *arrays):
        return [space(a.shape, a.dtype) for a in arrays] + [
            pltpu.SemaphoreType.DMA((len(arrays),))
        ]

    params = pltpu.CompilerParams(vmem_limit_bytes=24 << 20)
    count = 2 * (ONE + TWO)
    band, taps, turns = pl.pallas_call(
        prep_kernel(bins),
        out_shape=(
            jax.ShapeDtypeStruct((span, 2 * STEP), jnp.bfloat16),
            jax.ShapeDtypeStruct((count, 8, 128), jnp.float32),
            jax.ShapeDtypeStruct((count, 2, ROWS, 128), jnp.float32),
        ),
        in_specs=[far] * 7,
        out_specs=(vmem,) * 3,
        scratch_shapes=held(
            pltpu.VMEM, chirp, shift_one, frac_one, base_one, shift_two, frac_two, base_two
        ),
        compiler_params=params,
        name="prepare",
    )(chirp, shift_one, frac_one, base_one, shift_two, frac_two, base_two)

    index_tables = (beam_one, shift_one, beam_two, shift_two)
    scratch = [
        pltpu.VMEM((2, 16, SPANS * WIDE + span - STEP), jnp.bfloat16),
        pltpu.VMEM((WIDE, 128), jnp.float32),
        pltpu.VMEM((16, TALL, 128), jnp.float32),
        pltpu.VMEM((ONE, TALL, 128), jnp.float32),
    ] + held(pltpu.SMEM, *index_tables)
    half = pl.pallas_call(
        first_kernel(bins),
        out_shape=jax.ShapeDtypeStruct((TWO, ROWS, 128), jnp.float32),
        in_specs=[far] * 4 + [vmem] * 5,
        out_specs=vmem,
        scratch_shapes=scratch,
        compiler_params=params,
        name="first_pair",
    )(*index_tables, parts[0], parts[1], band, taps, turns)
    image = pl.pallas_call(
        second_kernel(bins),
        out_shape=jax.ShapeDtypeStruct((2, TWO, bins), jnp.bfloat16),
        in_specs=[far] * 4 + [vmem] * 7,
        out_specs=vmem,
        scratch_shapes=scratch + [pltpu.VMEM((TWO, ROWS, 128), jnp.float32)],
        compiler_params=params,
        name="second_pair",
    )(*index_tables, parts[2], far_main, far_rim, band, taps, turns, half)
    return image.transpose(1, 0, 2)[None, None]


def solution(mesh):
    in_specs = (P(("scene", "pulse"), "rep", None, "range"),) + (P(),) * 9
    out_specs = P("rep", ("scene", "pulse"), None, None, "range")

    return jax.shard_map(body, mesh=mesh, in_specs=in_specs, out_specs=out_specs, check_vma=False)
```

```python
import jax
import jax.numpy as jnp
from jax import lax
from jax.experimental import pallas as pl
from jax.experimental.pallas import tpu as pltpu
from jax.sharding import PartitionSpec as P

LEFT = 128
STEP = 128
ROWS = 56
COLS = 64
GROUPS = 16
RIM = 32
WIDE = GROUPS * ROWS
SPANS = COLS // GROUPS
CHUNKS = ROWS // 8
BLOCKS = WIDE // STEP
ONE, TWO = 16, 32
TALL = ROWS + 2 * RIM
TOGETHER = 16


def position():
    rep, pulse = lax.axis_index("rep"), lax.axis_index("pulse")
    low, high = pulse % 2, pulse // 2 % 2
    return 4 * rep + 2 * low + high, low, high


def lane_ids(shape):
    return lax.broadcasted_iota(jnp.int32, shape, len(shape) - 1)


def row_ids(shape):
    return lax.broadcasted_iota(jnp.int32, shape, len(shape) - 2)


def exchange(parts):
    parts = list(parts)
    lane = lane_ids(parts[0].shape)
    step = 1
    while step < len(parts):
        low = (lane & step) == 0
        for first in range(len(parts)):
            if first & step:
                continue
            a, b = parts[first], parts[first + step]
            parts[first] = jnp.where(low, a, pltpu.roll(b, step, 1))
            parts[first + step] = jnp.where(low, pltpu.roll(a, 128 - step, 1), b)
        step *= 2
    return parts


def store_rimmed(ref, index, chunk, value):
    row = 8 * chunk
    ref[index, pl.ds(RIM + row, 8), :] = value
    if row >= ROWS - RIM:
        ref[index, pl.ds(row - (ROWS - RIM), 8), :] = pltpu.roll(value, 1, 1)
    if row < RIM:
        ref[index, pl.ds(RIM + ROWS + row, 8), :] = pltpu.roll(value, 127, 1)


def inside_test(bins):
    first_bin = lax.axis_index("range") * bins
    bin_total = bins * lax.axis_size("range")
    shape = (8, 128)
    place = (lane_ids(shape) & (COLS - 1)) * ROWS + row_ids(shape) + (first_bin - LEFT)

    def inside(chunk, value):
        spot = place + 8 * chunk
        return jnp.where((spot >= 0) & (spot < bin_total), value, 0.0)

    return inside


def fetch(sources, targets, sems):
    copies = [
        pltpu.make_async_copy(source, target, sems.at[index])
        for index, (source, target) in enumerate(zip(sources, targets))
    ]
    for copy in copies:
        copy.start()
    for copy in copies:
        copy.wait()


def prep_kernel(bins):
    def kernel(*refs):
        far, (band_ref, taps_ref, turn_ref) = refs[:7], refs[7:10]
        chirp_ref, shift_one, frac_one, base_one, shift_two, frac_two, base_two = refs[10:17]
        fetch(far, refs[10:17], refs[17])
        own, _, _ = position()
        first_bin = lax.axis_index("range") * bins
        bin_total = bins * lax.axis_size("range")
        span = band_ref.shape[0]
        for part in range(2):
            row = chirp_ref[part : part + 1, :].astype(jnp.float32)
            row = jnp.concatenate([row, jnp.zeros((1, STEP), jnp.float32)], axis=1)
            band = pltpu.roll(jnp.broadcast_to(row, (STEP, span)), 0, 1, stride=1, stride_axis=0)
            for block in range(span // 128):
                turned = band[:, 128 * block : 128 * block + 128].T
                band_ref[pl.ds(128 * block, 128), pl.ds(STEP * part, STEP)] = turned.astype(
                    jnp.bfloat16
                )

        shape = (8, 128)
        lane = lane_ids(shape)

        def packed(first, second):
            total = jnp.zeros(shape, jnp.float32)
            at = 0
            for ref, width in ((first, ONE), (second, TWO)):
                offset = own * width
                for child in range(2):
                    row = ref[child : child + 1, 0:128].astype(jnp.float32)
                    for block in range(1, ref.shape[1] // 128):
                        other = ref[child : child + 1, 128 * block : 128 * block + 128]
                        row = jnp.where(offset // 128 == block, other.astype(jnp.float32), row)
                    row = pltpu.roll(
                        jnp.broadcast_to(row, shape), (at + 256 - offset % 128) % 128, 1
                    )
                    total = jnp.where((lane >= at) & (lane < at + width), row, total)
                    at += width
            return total

        frac = packed(frac_one, frac_two)
        base = packed(base_one, base_two)
        slope = 0.5 * (packed(shift_one, shift_two) + frac)
        row = row_ids(shape).astype(jnp.float32)
        spread = (row - 3.0) - frac
        turned = jnp.pi * spread
        still = turned == 0.0
        safe = jnp.where(still, 1.0, turned)
        weights = jnp.where(still, 1.0, jnp.sin(safe) / safe) * (
            0.54 + 0.46 * jnp.cos(jnp.pi * spread / 4.0)
        )
        count = taps_ref.shape[0]
        square = (128, 128)
        base_rows = jnp.broadcast_to(base[0:1], square).T[:count]
        slope_rows = jnp.broadcast_to(slope[0:1], square).T[:count]
        wide = lane_ids((count, 128))
        spot = (wide & (COLS - 1)) * ROWS + (first_bin - LEFT)
        angle = base_rows + slope_rows * (spot.astype(jnp.float32) / bin_total - 0.5)
        cos_col, sin_col = jnp.cos(angle), jnp.sin(angle)
        sign = jnp.where(lane < COLS, -1.0, 1.0)
        fine, coarse = slope * (row / bin_total), slope * (8.0 / bin_total)
        cos_fine, sin_fine = jnp.cos(fine), jnp.sin(fine)
        cos_coarse, sin_coarse = jnp.cos(coarse), jnp.sin(coarse)
        for place in range(count):

            def spread_out(table):
                return jnp.broadcast_to(table[:, place : place + 1], shape)

            taps_ref[place] = spread_out(weights)
            cos_all = jnp.broadcast_to(cos_col[place : place + 1], shape)
            sin_all = jnp.broadcast_to(sin_col[place : place + 1], shape) * sign
            cos_step, sin_step = spread_out(cos_fine), spread_out(sin_fine) * sign
            cos_next, sin_next = spread_out(cos_coarse), spread_out(sin_coarse) * sign
            for chunk in range(CHUNKS):
                cos_all, sin_all = (
                    cos_all * cos_step - sin_all * sin_step,
                    sin_all * cos_step + cos_all * sin_step,
                )
                turn_ref[place, 0, pl.ds(8 * chunk, 8), :] = cos_all
                turn_ref[place, 1, pl.ds(8 * chunk, 8), :] = sin_all
                cos_step, sin_step = cos_next, sin_next

    return kernel


def compress_pair(near, far, bins, band_ref, source, columns, images, inside):
    rest = source.shape[2] - LEFT - bins
    wide = near[0].shape[2] - LEFT - bins

    def piece(held, comp, at, size):
        if len(held) == 1:
            return held[0][comp, :, pl.ds(at, size)]
        main, rim = held
        if at == LEFT:
            return main[comp]
        return rim[comp, :, pl.ds(min(at, LEFT), size)]

    for comp in range(2):
        for at, size in ((0, LEFT), (LEFT, bins), (LEFT + bins, wide)):
            sides = [piece(held, comp, at, size).astype(jnp.float32) for held in (near, far)]
            source[comp, :, pl.ds(at, size)] = jnp.concatenate(sides, axis=0).astype(jnp.bfloat16)
        if rest > wide:
            source[comp, :, pl.ds(LEFT + bins + wide, rest - wide)] = jnp.zeros(
                (16, rest - wide), jnp.bfloat16
            )
    span = band_ref.shape[0]
    windows = jnp.concatenate(
        [
            source[comp, :, pl.ds(WIDE * u + STEP * block, span)]
            for block in range(BLOCKS)
            for comp in range(2)
            for u in range(SPANS)
        ],
        axis=0,
    )
    product = jnp.dot(windows, band_ref[...], preferred_element_type=jnp.float32)
    half = 16 * SPANS
    for block in range(BLOCKS):
        top = product[128 * block : 128 * block + half]
        low = product[128 * block + half : 128 * block + 128]
        result = jnp.concatenate(
            [top[:, :STEP] + low[:, STEP:], low[:, :STEP] - top[:, STEP:]], axis=0
        )
        columns[pl.ds(STEP * block, STEP), :] = result.astype(jnp.bfloat16).T.astype(jnp.float32)
    for chunk in range(0, CHUNKS, 2):
        size = min(2, CHUNKS - chunk) * 8
        parts = [columns[pl.ds(ROWS * g + 8 * chunk, size), :] for g in range(GROUPS)]
        parts = exchange([part.astype(jnp.bfloat16) for part in parts])
        for image, part in enumerate(parts):
            part = part.astype(jnp.float32)
            for extra in range(size // 8):
                value = inside(chunk + extra, part[8 * extra : 8 * extra + 8])
                store_rimmed(images, image, chunk + extra, value)


def contribution(images, tables, parent, child, first_parent, first_image, width, at):
    beam_ref, shift_ref, taps_ref, turn_ref = tables
    place = at + child * width + parent
    image = beam_ref[child, first_parent + parent] + first_image
    start = shift_ref[child, first_parent + parent] + (RIM - 3)
    value = None
    for tap in range(8):
        term = images[image, pl.ds(start + tap, ROWS), :] * taps_ref[place, pl.ds(tap, 1), :]
        value = term if value is None else value + term
    parts = []
    for chunk in range(CHUNKS):
        part = value[8 * chunk : 8 * chunk + 8]
        parts.append(
            part * turn_ref[place, 0, pl.ds(8 * chunk, 8), :]
            + pltpu.roll(part, COLS, 1) * turn_ref[place, 1, pl.ds(8 * chunk, 8), :]
        )
    return parts


def loop_over(count, one):
    def step(index, carry):
        for extra in range(TOGETHER):
            one(TOGETHER * index + extra)
        return carry

    lax.fori_loop(0, count // TOGETHER, step, 0)


def merge_one(images, tables, result, inside):
    own, low, _ = position()

    def one(parent):
        sides = [
            contribution(
                images, tables, parent, child, ONE * own, (child ^ low) * 8 - 8 * own, ONE, 0
            )
            for child in range(2)
        ]
        for chunk, (a, b) in enumerate(zip(*sides)):
            store_rimmed(result, parent, chunk, inside(chunk, a + b))

    loop_over(ONE, one)


def second_side(images, tables, parent, child):
    own, _, _ = position()
    return contribution(images, tables, parent, child, TWO * own, -ONE * own, TWO, 2 * ONE)


def first_kernel(bins):
    def kernel(
        far_beam_one, far_shift_one, far_beam_two, far_shift_two, a0, a1, band_ref, taps_ref,
        turn_ref, out_ref, source, columns, images, level_one, beam_one, shift_one, beam_two,
        shift_two, sems,
    ):
        inside = inside_test(bins)
        fetch(
            (far_beam_one, far_shift_one, far_beam_two, far_shift_two),
            (beam_one, shift_one, beam_two, shift_two), sems,
        )
        compress_pair((a0,), (a1,), bins, band_ref, source, columns, images, inside)
        merge_one(images, (beam_one, shift_one, taps_ref, turn_ref), level_one, inside)
        _, _, high = position()
        tables = (beam_two, shift_two, taps_ref, turn_ref)

        def one(parent):
            for chunk, part in enumerate(second_side(level_one, tables, parent, high)):
                out_ref[parent, pl.ds(8 * chunk, 8), :] = part

        loop_over(TWO, one)

    return kernel


def second_kernel(bins):
    def kernel(
        far_beam_one, far_shift_one, far_beam_two, far_shift_two, a2, a3, r3, band_ref, taps_ref,
        turn_ref, half_ref, out_ref, source, columns, images, level_one, beam_one, shift_one,
        beam_two, shift_two, sems, level_two,
    ):
        inside = inside_test(bins)
        fetch(
            (far_beam_one, far_shift_one, far_beam_two, far_shift_two),
            (beam_one, shift_one, beam_two, shift_two), sems,
        )
        compress_pair((a2,), (a3, r3), bins, band_ref, source, columns, images, inside)
        merge_one(images, (beam_one, shift_one, taps_ref, turn_ref), level_one, inside)
        _, _, high = position()
        tables = (beam_two, shift_two, taps_ref, turn_ref)

        def one(parent):
            for chunk, part in enumerate(second_side(level_one, tables, parent, 1 - high)):
                rows = pl.ds(8 * chunk, 8)
                level_two[parent, rows, :] = part + half_ref[parent, rows, :]

        loop_over(TWO, one)
        for half in range(2):
            for chunk in range(0, CHUNKS, 2):
                size = min(2, CHUNKS - chunk) * 8
                parts = [
                    level_two[16 * half + image, pl.ds(8 * chunk, size), :].astype(jnp.bfloat16)
                    for image in range(GROUPS)
                ]
                for g, part in enumerate(exchange(parts)):
                    columns[pl.ds(ROWS * g + 8 * chunk, size), :] = part.astype(jnp.float32)
            for block in range(BLOCKS):
                turned = columns[pl.ds(STEP * block, STEP), :].astype(jnp.bfloat16).T
                for comp in range(2):
                    for u in range(SPANS):
                        left = WIDE * u + STEP * block - LEFT
                        if 0 <= left < bins:
                            row = (comp * SPANS + u) * 16
                            out_ref[comp, pl.ds(16 * half, 16), pl.ds(left, 128)] = turned[
                                row : row + 16
                            ]

    return kernel


def neighbours(head, tail, axis):
    count = lax.axis_size(axis)
    even = lax.axis_index(axis) % 2 == 0
    near = [(i, i ^ 1) for i in range(count) if i ^ 1 < count]
    far = [(i + 1, i + 2) for i in range(0, count - 2, 2)]
    far = far + [(b, a) for a, b in far]
    first = lax.ppermute(jnp.where(even, tail, head), axis, near)
    second = lax.ppermute(jnp.where(even, head, tail), axis, far) if far else jnp.zeros_like(first)
    return jnp.where(even, second, first), jnp.where(even, first, second)


def body(
    echo, chirp, beam_one, shift_one, frac_one, base_one, beam_two, shift_two, frac_two, base_two
):
    signal = echo[0]
    beams, _, bins = signal.shape
    span = STEP + chirp.shape[1]
    pulse = lax.axis_index("pulse")

    signal = signal.reshape(4, beams // 4, 2, bins).transpose(0, 2, 1, 3)
    small = (
        chirp, beam_one, shift_one, frac_one, base_one, beam_two, shift_two, frac_two, base_two
    )
    chirp, beam_one, shift_one, frac_one, base_one, beam_two, shift_two, frac_two, base_two = (
        pltpu.with_memory_space_constraint(array, pltpu.HBM) for array in small
    )

    def block_of(array, mask):
        index = pulse ^ mask
        return lax.dynamic_index_in_dim(array, 2 * (index % 2) + index // 2 % 2, 0, keepdims=False)

    def sent(array, mask):
        count = lax.axis_size("pulse")
        return lax.ppermute(array, "pulse", [(i, i ^ mask) for i in range(count)])

    far_main = sent(block_of(signal, 3), 3)
    from_left, from_right = neighbours(
        signal[:, :, :, :span], signal[:, :, :, bins - span :], "range"
    )
    from_left = from_left[:, :, :, span - LEFT :]
    wide = jnp.concatenate([from_left, signal, from_right], axis=3)
    rims = jnp.concatenate([from_left, from_right], axis=3)
    parts = [block_of(wide, 0)] + [sent(block_of(wide, mask), mask) for mask in (1, 2)]
    far_rim = sent(block_of(rims, 3), 3)

    vmem = pl.BlockSpec(memory_space=pltpu.VMEM)
    far = pl.BlockSpec(memory_space=pltpu.HBM)

    def held(space, *arrays):
        return [space(a.shape, a.dtype) for a in arrays] + [
            pltpu.SemaphoreType.DMA((len(arrays),))
        ]

    params = pltpu.CompilerParams(vmem_limit_bytes=24 << 20)
    count = 2 * (ONE + TWO)
    band, taps, turns = pl.pallas_call(
        prep_kernel(bins),
        out_shape=(
            jax.ShapeDtypeStruct((span, 2 * STEP), jnp.bfloat16),
            jax.ShapeDtypeStruct((count, 8, 128), jnp.float32),
            jax.ShapeDtypeStruct((count, 2, ROWS, 128), jnp.float32),
        ),
        in_specs=[far] * 7,
        out_specs=(vmem,) * 3,
        scratch_shapes=held(
            pltpu.VMEM, chirp, shift_one, frac_one, base_one, shift_two, frac_two, base_two
        ),
        compiler_params=params,
        name="prepare",
    )(chirp, shift_one, frac_one, base_one, shift_two, frac_two, base_two)

    index_tables = (beam_one, shift_one, beam_two, shift_two)
    scratch = [
        pltpu.VMEM((2, 16, SPANS * WIDE + span - STEP), jnp.bfloat16),
        pltpu.VMEM((WIDE, 128), jnp.float32),
        pltpu.VMEM((16, TALL, 128), jnp.float32),
        pltpu.VMEM((ONE, TALL, 128), jnp.float32),
    ] + held(pltpu.SMEM, *index_tables)
    half = pl.pallas_call(
        first_kernel(bins),
        out_shape=jax.ShapeDtypeStruct((TWO, ROWS, 128), jnp.float32),
        in_specs=[far] * 4 + [vmem] * 5,
        out_specs=vmem,
        scratch_shapes=scratch,
        compiler_params=params,
        name="first_pair",
    )(*index_tables, parts[0], parts[1], band, taps, turns)
    image = pl.pallas_call(
        second_kernel(bins),
        out_shape=jax.ShapeDtypeStruct((2, TWO, bins), jnp.bfloat16),
        in_specs=[far] * 4 + [vmem] * 7,
        out_specs=vmem,
        scratch_shapes=scratch + [pltpu.VMEM((TWO, ROWS, 128), jnp.float32)],
        compiler_params=params,
        name="second_pair",
    )(*index_tables, parts[2], far_main, far_rim, band, taps, turns, half)
    return image.transpose(1, 0, 2)[None, None]


def solution(mesh):
    in_specs = (P(("scene", "pulse"), "rep", None, "range"),) + (P(),) * 9
    out_specs = P("rep", ("scene", "pulse"), None, None, "range")

    return jax.shard_map(body, mesh=mesh, in_specs=in_specs, out_specs=out_specs, check_vma=False)
```

```python
import jax
import jax.numpy as jnp
from jax import lax
from jax.experimental import pallas as pl
from jax.experimental.pallas import tpu as pltpu
from jax.sharding import PartitionSpec as P

LEFT = 128
STEP = 128
ROWS = 56
COLS = 64
GROUPS = 16
RIM = 32
WIDE = GROUPS * ROWS
SPANS = COLS // GROUPS
CHUNKS = ROWS // 8
BLOCKS = WIDE // STEP
ONE, TWO = 16, 32
TALL = ROWS + 2 * RIM
TOGETHER = 16


def position():
    rep, pulse = lax.axis_index("rep"), lax.axis_index("pulse")
    low, high = pulse % 2, pulse // 2 % 2
    return 4 * rep + 2 * low + high, low, high


def lane_ids(shape):
    return lax.broadcasted_iota(jnp.int32, shape, len(shape) - 1)


def row_ids(shape):
    return lax.broadcasted_iota(jnp.int32, shape, len(shape) - 2)


def exchange(parts):
    parts = list(parts)
    lane = lane_ids(parts[0].shape)
    step = 1
    while step < len(parts):
        low = (lane & step) == 0
        for first in range(len(parts)):
            if first & step:
                continue
            a, b = parts[first], parts[first + step]
            parts[first] = jnp.where(low, a, pltpu.roll(b, step, 1))
            parts[first + step] = jnp.where(low, pltpu.roll(a, 128 - step, 1), b)
        step *= 2
    return parts


def store_rimmed(ref, index, chunk, value):
    row = 8 * chunk
    ref[index, pl.ds(RIM + row, 8), :] = value
    if row >= ROWS - RIM:
        ref[index, pl.ds(row - (ROWS - RIM), 8), :] = pltpu.roll(value, 1, 1)
    if row < RIM:
        ref[index, pl.ds(RIM + ROWS + row, 8), :] = pltpu.roll(value, 127, 1)


def inside_test(bins):
    first_bin = lax.axis_index("range") * bins
    bin_total = bins * lax.axis_size("range")
    shape = (8, 128)
    place = (lane_ids(shape) & (COLS - 1)) * ROWS + row_ids(shape) + (first_bin - LEFT)

    def inside(chunk, value):
        spot = place + 8 * chunk
        return jnp.where((spot >= 0) & (spot < bin_total), value, 0.0)

    return inside


def fetch(sources, targets, sems):
    copies = [
        pltpu.make_async_copy(source, target, sems.at[index])
        for index, (source, target) in enumerate(zip(sources, targets))
    ]
    for copy in copies:
        copy.start()
    for copy in copies:
        copy.wait()


def prep_kernel(bins):
    def kernel(*refs):
        far, (band_ref, taps_ref, turn_ref) = refs[:7], refs[7:10]
        chirp_ref, shift_one, frac_one, base_one, shift_two, frac_two, base_two = refs[10:17]
        fetch(far, refs[10:17], refs[17])
        own, _, _ = position()
        first_bin = lax.axis_index("range") * bins
        bin_total = bins * lax.axis_size("range")
        span = band_ref.shape[0]
        for part in range(2):
            row = chirp_ref[part : part + 1, :].astype(jnp.float32)
            row = jnp.concatenate([row, jnp.zeros((1, STEP), jnp.float32)], axis=1)
            band = pltpu.roll(jnp.broadcast_to(row, (STEP, span)), 0, 1, stride=1, stride_axis=0)
            for block in range(span // 128):
                turned = band[:, 128 * block : 128 * block + 128].T
                band_ref[pl.ds(128 * block, 128), pl.ds(STEP * part, STEP)] = turned.astype(
                    jnp.bfloat16
                )

        shape = (8, 128)
        lane = lane_ids(shape)

        def packed(first, second):
            total = jnp.zeros(shape, jnp.float32)
            at = 0
            for ref, width in ((first, ONE), (second, TWO)):
                offset = own * width
                for child in range(2):
                    row = ref[child : child + 1, 0:128].astype(jnp.float32)
                    for block in range(1, ref.shape[1] // 128):
                        other = ref[child : child + 1, 128 * block : 128 * block + 128]
                        row = jnp.where(offset // 128 == block, other.astype(jnp.float32), row)
                    row = pltpu.roll(
                        jnp.broadcast_to(row, shape), (at + 256 - offset % 128) % 128, 1
                    )
                    total = jnp.where((lane >= at) & (lane < at + width), row, total)
                    at += width
            return total

        frac = packed(frac_one, frac_two)
        base = packed(base_one, base_two)
        slope = 0.5 * (packed(shift_one, shift_two) + frac)
        row = row_ids(shape).astype(jnp.float32)
        spread = (row - 3.0) - frac
        turned = jnp.pi * spread
        still = turned == 0.0
        safe = jnp.where(still, 1.0, turned)
        weights = jnp.where(still, 1.0, jnp.sin(safe) / safe) * (
            0.54 + 0.46 * jnp.cos(jnp.pi * spread / 4.0)
        )
        count = taps_ref.shape[0]
        square = (128, 128)
        base_rows = jnp.broadcast_to(base[0:1], square).T[:count]
        slope_rows = jnp.broadcast_to(slope[0:1], square).T[:count]
        wide = lane_ids((count, 128))
        spot = (wide & (COLS - 1)) * ROWS + (first_bin - LEFT)
        angle = base_rows + slope_rows * (spot.astype(jnp.float32) / bin_total - 0.5)
        cos_col, sin_col = jnp.cos(angle), jnp.sin(angle)
        sign = jnp.where(lane < COLS, -1.0, 1.0)
        fine, coarse = slope * (row / bin_total), slope * (8.0 / bin_total)
        cos_fine, sin_fine = jnp.cos(fine), jnp.sin(fine)
        cos_coarse, sin_coarse = jnp.cos(coarse), jnp.sin(coarse)
        for place in range(count):

            def spread_out(table):
                return jnp.broadcast_to(table[:, place : place + 1], shape)

            taps_ref[place] = spread_out(weights)
            cos_all = jnp.broadcast_to(cos_col[place : place + 1], shape)
            sin_all = jnp.broadcast_to(sin_col[place : place + 1], shape) * sign
            cos_step, sin_step = spread_out(cos_fine), spread_out(sin_fine) * sign
            cos_next, sin_next = spread_out(cos_coarse), spread_out(sin_coarse) * sign
            for chunk in range(CHUNKS):
                cos_all, sin_all = (
                    cos_all * cos_step - sin_all * sin_step,
                    sin_all * cos_step + cos_all * sin_step,
                )
                turn_ref[place, 0, pl.ds(8 * chunk, 8), :] = cos_all
                turn_ref[place, 1, pl.ds(8 * chunk, 8), :] = sin_all
                cos_step, sin_step = cos_next, sin_next

    return kernel


def compress_pair(near, far, bins, band_ref, source, columns, images, inside):
    rest = source.shape[2] - LEFT - bins
    wide = near[0].shape[2] - LEFT - bins

    def piece(held, comp, at, size):
        if len(held) == 1:
            return held[0][comp, :, pl.ds(at, size)]
        main, rim = held
        if at == LEFT:
            return main[comp]
        return rim[comp, :, pl.ds(min(at, LEFT), size)]

    for comp in range(2):
        for at, size in ((0, LEFT), (LEFT, bins), (LEFT + bins, wide)):
            sides = [piece(held, comp, at, size).astype(jnp.float32) for held in (near, far)]
            source[comp, :, pl.ds(at, size)] = jnp.concatenate(sides, axis=0).astype(jnp.bfloat16)
        if rest > wide:
            source[comp, :, pl.ds(LEFT + bins + wide, rest - wide)] = jnp.zeros(
                (16, rest - wide), jnp.bfloat16
            )
    span = band_ref.shape[0]
    windows = jnp.concatenate(
        [
            source[comp, :, pl.ds(WIDE * u + STEP * block, span)]
            for block in range(BLOCKS)
            for comp in range(2)
            for u in range(SPANS)
        ],
        axis=0,
    )
    product = jnp.dot(windows, band_ref[...], preferred_element_type=jnp.float32)
    half = 16 * SPANS
    for block in range(BLOCKS):
        top = product[128 * block : 128 * block + half]
        low = product[128 * block + half : 128 * block + 128]
        result = jnp.concatenate(
            [top[:, :STEP] + low[:, STEP:], low[:, :STEP] - top[:, STEP:]], axis=0
        )
        columns[pl.ds(STEP * block, STEP), :] = result.astype(jnp.bfloat16).T.astype(jnp.float32)
    for chunk in range(0, CHUNKS, 2):
        size = min(2, CHUNKS - chunk) * 8
        parts = [columns[pl.ds(ROWS * g + 8 * chunk, size), :] for g in range(GROUPS)]
        parts = exchange([part.astype(jnp.bfloat16) for part in parts])
        for image, part in enumerate(parts):
            part = part.astype(jnp.float32)
            for extra in range(size // 8):
                value = inside(chunk + extra, part[8 * extra : 8 * extra + 8])
                store_rimmed(images, image, chunk + extra, value)


def contribution(images, tables, parent, child, first_parent, first_image, width, at):
    beam_ref, shift_ref, taps_ref, turn_ref = tables
    place = at + child * width + parent
    image = beam_ref[child, first_parent + parent] + first_image
    start = shift_ref[child, first_parent + parent] + (RIM - 3)
    value = None
    for tap in range(8):
        term = images[image, pl.ds(start + tap, ROWS), :] * taps_ref[place, pl.ds(tap, 1), :]
        value = term if value is None else value + term
    parts = []
    for chunk in range(CHUNKS):
        part = value[8 * chunk : 8 * chunk + 8]
        parts.append(
            part * turn_ref[place, 0, pl.ds(8 * chunk, 8), :]
            + pltpu.roll(part, COLS, 1) * turn_ref[place, 1, pl.ds(8 * chunk, 8), :]
        )
    return parts


def loop_over(count, one):
    def step(index, carry):
        for extra in range(TOGETHER):
            one(TOGETHER * index + extra)
        return carry

    lax.fori_loop(0, count // TOGETHER, step, 0)


def merge_one(images, tables, result, inside):
    own, low, _ = position()

    def one(parent):
        sides = [
            contribution(
                images, tables, parent, child, ONE * own, (child ^ low) * 8 - 8 * own, ONE, 0
            )
            for child in range(2)
        ]
        for chunk, (a, b) in enumerate(zip(*sides)):
            store_rimmed(result, parent, chunk, inside(chunk, a + b))

    loop_over(ONE, one)


def second_side(images, tables, parent, child):
    own, _, _ = position()
    return contribution(images, tables, parent, child, TWO * own, -ONE * own, TWO, 2 * ONE)


def first_kernel(bins):
    def kernel(
        far_beam_one, far_shift_one, far_beam_two, far_shift_two, a0, a1, r1, band_ref, taps_ref,
        turn_ref, out_ref, source, columns, images, level_one, beam_one, shift_one, beam_two,
        shift_two, sems,
    ):
        inside = inside_test(bins)
        fetch(
            (far_beam_one, far_shift_one, far_beam_two, far_shift_two),
            (beam_one, shift_one, beam_two, shift_two), sems,
        )
        compress_pair((a0,), (a1, r1), bins, band_ref, source, columns, images, inside)
        merge_one(images, (beam_one, shift_one, taps_ref, turn_ref), level_one, inside)
        _, _, high = position()
        tables = (beam_two, shift_two, taps_ref, turn_ref)

        def one(parent):
            for chunk, part in enumerate(second_side(level_one, tables, parent, high)):
                out_ref[parent, pl.ds(8 * chunk, 8), :] = part

        loop_over(TWO, one)

    return kernel


def second_kernel(bins):
    def kernel(
        far_beam_one, far_shift_one, far_beam_two, far_shift_two, a2, a3, r3, band_ref, taps_ref,
        turn_ref, half_ref, out_ref, source, columns, images, level_one, beam_one, shift_one,
        beam_two, shift_two, sems, level_two,
    ):
        inside = inside_test(bins)
        fetch(
            (far_beam_one, far_shift_one, far_beam_two, far_shift_two),
            (beam_one, shift_one, beam_two, shift_two), sems,
        )
        compress_pair((a2,), (a3, r3), bins, band_ref, source, columns, images, inside)
        merge_one(images, (beam_one, shift_one, taps_ref, turn_ref), level_one, inside)
        _, _, high = position()
        tables = (beam_two, shift_two, taps_ref, turn_ref)

        def one(parent):
            for chunk, part in enumerate(second_side(level_one, tables, parent, 1 - high)):
                rows = pl.ds(8 * chunk, 8)
                level_two[parent, rows, :] = part + half_ref[parent, rows, :]

        loop_over(TWO, one)
        for half in range(2):
            for chunk in range(0, CHUNKS, 2):
                size = min(2, CHUNKS - chunk) * 8
                parts = [
                    level_two[16 * half + image, pl.ds(8 * chunk, size), :].astype(jnp.bfloat16)
                    for image in range(GROUPS)
                ]
                for g, part in enumerate(exchange(parts)):
                    columns[pl.ds(ROWS * g + 8 * chunk, size), :] = part.astype(jnp.float32)
            for block in range(BLOCKS):
                turned = columns[pl.ds(STEP * block, STEP), :].astype(jnp.bfloat16).T
                for comp in range(2):
                    for u in range(SPANS):
                        left = WIDE * u + STEP * block - LEFT
                        if 0 <= left < bins:
                            row = (comp * SPANS + u) * 16
                            out_ref[comp, pl.ds(16 * half, 16), pl.ds(left, 128)] = turned[
                                row : row + 16
                            ]

    return kernel


def neighbours(head, tail, axis):
    count = lax.axis_size(axis)
    even = lax.axis_index(axis) % 2 == 0
    near = [(i, i ^ 1) for i in range(count) if i ^ 1 < count]
    far = [(i + 1, i + 2) for i in range(0, count - 2, 2)]
    far = far + [(b, a) for a, b in far]
    first = lax.ppermute(jnp.where(even, tail, head), axis, near)
    second = lax.ppermute(jnp.where(even, head, tail), axis, far) if far else jnp.zeros_like(first)
    return jnp.where(even, second, first), jnp.where(even, first, second)


def body(
    echo, chirp, beam_one, shift_one, frac_one, base_one, beam_two, shift_two, frac_two, base_two
):
    signal = echo[0]
    beams, _, bins = signal.shape
    span = STEP + chirp.shape[1]
    pulse = lax.axis_index("pulse")

    signal = signal.reshape(4, beams // 4, 2, bins).transpose(0, 2, 1, 3)
    small = (
        chirp, beam_one, shift_one, frac_one, base_one, beam_two, shift_two, frac_two, base_two
    )
    chirp, beam_one, shift_one, frac_one, base_one, beam_two, shift_two, frac_two, base_two = (
        pltpu.with_memory_space_constraint(array, pltpu.HBM) for array in small
    )

    def block_of(array, mask):
        index = pulse ^ mask
        return lax.dynamic_index_in_dim(array, 2 * (index % 2) + index // 2 % 2, 0, keepdims=False)

    def sent(array, mask):
        count = lax.axis_size("pulse")
        return lax.ppermute(array, "pulse", [(i, i ^ mask) for i in range(count)])

    far_main = sent(block_of(signal, 3), 3)
    near_main = sent(block_of(signal, 1), 1)
    from_left, from_right = neighbours(
        signal[:, :, :, :span], signal[:, :, :, bins - span :], "range"
    )
    from_left = from_left[:, :, :, span - LEFT :]
    wide = jnp.concatenate([from_left, signal, from_right], axis=3)
    rims = jnp.concatenate([from_left, from_right], axis=3)
    near_rim = sent(block_of(rims, 1), 1)
    middle = sent(block_of(wide, 2), 2)
    far_rim = sent(block_of(rims, 3), 3)

    vmem = pl.BlockSpec(memory_space=pltpu.VMEM)
    far = pl.BlockSpec(memory_space=pltpu.HBM)

    def held(space, *arrays):
        return [space(a.shape, a.dtype) for a in arrays] + [
            pltpu.SemaphoreType.DMA((len(arrays),))
        ]

    params = pltpu.CompilerParams(vmem_limit_bytes=24 << 20)
    count = 2 * (ONE + TWO)
    band, taps, turns = pl.pallas_call(
        prep_kernel(bins),
        out_shape=(
            jax.ShapeDtypeStruct((span, 2 * STEP), jnp.bfloat16),
            jax.ShapeDtypeStruct((count, 8, 128), jnp.float32),
            jax.ShapeDtypeStruct((count, 2, ROWS, 128), jnp.float32),
        ),
        in_specs=[far] * 7,
        out_specs=(vmem,) * 3,
        scratch_shapes=held(
            pltpu.VMEM, chirp, shift_one, frac_one, base_one, shift_two, frac_two, base_two
        ),
        compiler_params=params,
        name="prepare",
    )(chirp, shift_one, frac_one, base_one, shift_two, frac_two, base_two)

    index_tables = (beam_one, shift_one, beam_two, shift_two)
    scratch = [
        pltpu.VMEM((2, 16, SPANS * WIDE + span - STEP), jnp.bfloat16),
        pltpu.VMEM((WIDE, 128), jnp.float32),
        pltpu.VMEM((16, TALL, 128), jnp.float32),
        pltpu.VMEM((ONE, TALL, 128), jnp.float32),
    ] + held(pltpu.SMEM, *index_tables)
    half = pl.pallas_call(
        first_kernel(bins),
        out_shape=jax.ShapeDtypeStruct((TWO, ROWS, 128), jnp.float32),
        in_specs=[far] * 4 + [vmem] * 6,
        out_specs=vmem,
        scratch_shapes=scratch,
        compiler_params=params,
        name="first_pair",
    )(*index_tables, block_of(wide, 0), near_main, near_rim, band, taps, turns)
    image = pl.pallas_call(
        second_kernel(bins),
        out_shape=jax.ShapeDtypeStruct((2, TWO, bins), jnp.bfloat16),
        in_specs=[far] * 4 + [vmem] * 7,
        out_specs=vmem,
        scratch_shapes=scratch + [pltpu.VMEM((TWO, ROWS, 128), jnp.float32)],
        compiler_params=params,
        name="second_pair",
    )(*index_tables, middle, far_main, far_rim, band, taps, turns, half)
    return image.transpose(1, 0, 2)[None, None]


def solution(mesh):
    in_specs = (P(("scene", "pulse"), "rep", None, "range"),) + (P(),) * 9
    out_specs = P("rep", ("scene", "pulse"), None, None, "range")

    return jax.shard_map(body, mesh=mesh, in_specs=in_specs, out_specs=out_specs, check_vma=False)
```

```python
import jax
import jax.numpy as jnp
from jax import lax
from jax.experimental import pallas as pl
from jax.experimental.pallas import tpu as pltpu
from jax.sharding import PartitionSpec as P

LEFT = 128
STEP = 128
ROWS = 56
COLS = 64
GROUPS = 16
RIM = 32
WIDE = GROUPS * ROWS
SPANS = COLS // GROUPS
CHUNKS = ROWS // 8
BLOCKS = WIDE // STEP
ONE, TWO = 16, 32
TALL = ROWS + 2 * RIM
TOGETHER = 16


def position():
    rep, pulse = lax.axis_index("rep"), lax.axis_index("pulse")
    low, high = pulse % 2, pulse // 2 % 2
    return 4 * rep + 2 * low + high, low, high


def lane_ids(shape):
    return lax.broadcasted_iota(jnp.int32, shape, len(shape) - 1)


def row_ids(shape):
    return lax.broadcasted_iota(jnp.int32, shape, len(shape) - 2)


def exchange(parts):
    parts = list(parts)
    lane = lane_ids(parts[0].shape)
    step = 1
    while step < len(parts):
        low = (lane & step) == 0
        for first in range(len(parts)):
            if first & step:
                continue
            a, b = parts[first], parts[first + step]
            parts[first] = jnp.where(low, a, pltpu.roll(b, step, 1))
            parts[first + step] = jnp.where(low, pltpu.roll(a, 128 - step, 1), b)
        step *= 2
    return parts


def store_rimmed(ref, index, chunk, value):
    row = 8 * chunk
    ref[index, pl.ds(RIM + row, 8), :] = value
    if row >= ROWS - RIM:
        ref[index, pl.ds(row - (ROWS - RIM), 8), :] = pltpu.roll(value, 1, 1)
    if row < RIM:
        ref[index, pl.ds(RIM + ROWS + row, 8), :] = pltpu.roll(value, 127, 1)


def inside_test(bins):
    first_bin = lax.axis_index("range") * bins
    bin_total = bins * lax.axis_size("range")
    shape = (8, 128)
    place = (lane_ids(shape) & (COLS - 1)) * ROWS + row_ids(shape) + (first_bin - LEFT)

    def inside(chunk, value):
        spot = place + 8 * chunk
        return jnp.where((spot >= 0) & (spot < bin_total), value, 0.0)

    return inside


def fetch(sources, targets, sems):
    copies = [
        pltpu.make_async_copy(source, target, sems.at[index])
        for index, (source, target) in enumerate(zip(sources, targets))
    ]
    for copy in copies:
        copy.start()
    return copies


def arrived(copies):
    for copy in copies:
        copy.wait()


def prep_kernel(bins):
    def kernel(*refs):
        far, (band_ref, taps_ref, turn_ref) = refs[:7], refs[7:10]
        chirp_ref, shift_one, frac_one, base_one, shift_two, frac_two, base_two = refs[10:17]
        copies = fetch(far, refs[10:17], refs[17])
        own, _, _ = position()
        first_bin = lax.axis_index("range") * bins
        bin_total = bins * lax.axis_size("range")
        span = band_ref.shape[0]
        arrived(copies[:1])
        for part in range(2):
            row = chirp_ref[part : part + 1, :].astype(jnp.float32)
            row = jnp.concatenate([row, jnp.zeros((1, STEP), jnp.float32)], axis=1)
            band = pltpu.roll(jnp.broadcast_to(row, (STEP, span)), 0, 1, stride=1, stride_axis=0)
            for block in range(span // 128):
                turned = band[:, 128 * block : 128 * block + 128].T
                band_ref[pl.ds(128 * block, 128), pl.ds(STEP * part, STEP)] = turned.astype(
                    jnp.bfloat16
                )

        arrived(copies[1:])
        shape = (8, 128)
        lane = lane_ids(shape)

        def packed(first, second):
            total = jnp.zeros(shape, jnp.float32)
            at = 0
            for ref, width in ((first, ONE), (second, TWO)):
                offset = own * width
                for child in range(2):
                    row = ref[child : child + 1, 0:128].astype(jnp.float32)
                    for block in range(1, ref.shape[1] // 128):
                        other = ref[child : child + 1, 128 * block : 128 * block + 128]
                        row = jnp.where(offset // 128 == block, other.astype(jnp.float32), row)
                    row = pltpu.roll(
                        jnp.broadcast_to(row, shape), (at + 256 - offset % 128) % 128, 1
                    )
                    total = jnp.where((lane >= at) & (lane < at + width), row, total)
                    at += width
            return total

        frac = packed(frac_one, frac_two)
        base = packed(base_one, base_two)
        slope = 0.5 * (packed(shift_one, shift_two) + frac)
        row = row_ids(shape).astype(jnp.float32)
        spread = (row - 3.0) - frac
        turned = jnp.pi * spread
        still = turned == 0.0
        safe = jnp.where(still, 1.0, turned)
        weights = jnp.where(still, 1.0, jnp.sin(safe) / safe) * (
            0.54 + 0.46 * jnp.cos(jnp.pi * spread / 4.0)
        )
        count = taps_ref.shape[0]
        square = (128, 128)
        base_rows = jnp.broadcast_to(base[0:1], square).T[:count]
        slope_rows = jnp.broadcast_to(slope[0:1], square).T[:count]
        wide = lane_ids((count, 128))
        spot = (wide & (COLS - 1)) * ROWS + (first_bin - LEFT)
        angle = base_rows + slope_rows * (spot.astype(jnp.float32) / bin_total - 0.5)
        cos_col, sin_col = jnp.cos(angle), jnp.sin(angle)
        sign = jnp.where(lane < COLS, -1.0, 1.0)
        fine, coarse = slope * (row / bin_total), slope * (8.0 / bin_total)
        cos_fine, sin_fine = jnp.cos(fine), jnp.sin(fine)
        cos_coarse, sin_coarse = jnp.cos(coarse), jnp.sin(coarse)
        for place in range(count):

            def spread_out(table):
                return jnp.broadcast_to(table[:, place : place + 1], shape)

            taps_ref[place] = spread_out(weights)
            cos_all = jnp.broadcast_to(cos_col[place : place + 1], shape)
            sin_all = jnp.broadcast_to(sin_col[place : place + 1], shape) * sign
            cos_step, sin_step = spread_out(cos_fine), spread_out(sin_fine) * sign
            cos_next, sin_next = spread_out(cos_coarse), spread_out(sin_coarse) * sign
            for chunk in range(CHUNKS):
                cos_all, sin_all = (
                    cos_all * cos_step - sin_all * sin_step,
                    sin_all * cos_step + cos_all * sin_step,
                )
                turn_ref[place, 0, pl.ds(8 * chunk, 8), :] = cos_all
                turn_ref[place, 1, pl.ds(8 * chunk, 8), :] = sin_all
                cos_step, sin_step = cos_next, sin_next

    return kernel


def compress_pair(near, far, bins, band_ref, source, columns, images, inside):
    rest = source.shape[2] - LEFT - bins
    wide = near[0].shape[2] - LEFT - bins

    def piece(held, comp, at, size):
        if len(held) == 1:
            return held[0][comp, :, pl.ds(at, size)]
        main, rim = held
        if at == LEFT:
            return main[comp]
        return rim[comp, :, pl.ds(min(at, LEFT), size)]

    for comp in range(2):
        for at, size in ((0, LEFT), (LEFT, bins), (LEFT + bins, wide)):
            sides = [piece(held, comp, at, size).astype(jnp.float32) for held in (near, far)]
            source[comp, :, pl.ds(at, size)] = jnp.concatenate(sides, axis=0).astype(jnp.bfloat16)
        if rest > wide:
            source[comp, :, pl.ds(LEFT + bins + wide, rest - wide)] = jnp.zeros(
                (16, rest - wide), jnp.bfloat16
            )
    span = band_ref.shape[0]
    windows = jnp.concatenate(
        [
            source[comp, :, pl.ds(WIDE * u + STEP * block, span)]
            for block in range(BLOCKS)
            for comp in range(2)
            for u in range(SPANS)
        ],
        axis=0,
    )
    product = jnp.dot(windows, band_ref[...], preferred_element_type=jnp.float32)
    half = 16 * SPANS
    for block in range(BLOCKS):
        top = product[128 * block : 128 * block + half]
        low = product[128 * block + half : 128 * block + 128]
        result = jnp.concatenate(
            [top[:, :STEP] + low[:, STEP:], low[:, :STEP] - top[:, STEP:]], axis=0
        )
        columns[pl.ds(STEP * block, STEP), :] = result.astype(jnp.bfloat16).T.astype(jnp.float32)
    for chunk in range(0, CHUNKS, 2):
        size = min(2, CHUNKS - chunk) * 8
        parts = [columns[pl.ds(ROWS * g + 8 * chunk, size), :] for g in range(GROUPS)]
        parts = exchange([part.astype(jnp.bfloat16) for part in parts])
        for image, part in enumerate(parts):
            part = part.astype(jnp.float32)
            for extra in range(size // 8):
                value = inside(chunk + extra, part[8 * extra : 8 * extra + 8])
                store_rimmed(images, image, chunk + extra, value)


def contribution(images, tables, parent, child, first_parent, first_image, width, at):
    beam_ref, shift_ref, taps_ref, turn_ref = tables
    place = at + child * width + parent
    image = beam_ref[child, first_parent + parent] + first_image
    start = shift_ref[child, first_parent + parent] + (RIM - 3)
    value = None
    for tap in range(8):
        term = images[image, pl.ds(start + tap, ROWS), :] * taps_ref[place, pl.ds(tap, 1), :]
        value = term if value is None else value + term
    parts = []
    for chunk in range(CHUNKS):
        part = value[8 * chunk : 8 * chunk + 8]
        parts.append(
            part * turn_ref[place, 0, pl.ds(8 * chunk, 8), :]
            + pltpu.roll(part, COLS, 1) * turn_ref[place, 1, pl.ds(8 * chunk, 8), :]
        )
    return parts


def loop_over(count, one):
    def step(index, carry):
        for extra in range(TOGETHER):
            one(TOGETHER * index + extra)
        return carry

    lax.fori_loop(0, count // TOGETHER, step, 0)


def merge_one(images, tables, result, inside):
    own, low, _ = position()

    def one(parent):
        sides = [
            contribution(
                images, tables, parent, child, ONE * own, (child ^ low) * 8 - 8 * own, ONE, 0
            )
            for child in range(2)
        ]
        for chunk, (a, b) in enumerate(zip(*sides)):
            store_rimmed(result, parent, chunk, inside(chunk, a + b))

    loop_over(ONE, one)


def second_side(images, tables, parent, child):
    own, _, _ = position()
    return contribution(images, tables, parent, child, TWO * own, -ONE * own, TWO, 2 * ONE)


def first_kernel(bins):
    def kernel(
        far_beam_one, far_shift_one, far_beam_two, far_shift_two, a0, a1, band_ref, taps_ref,
        turn_ref, out_ref, source, columns, images, level_one, beam_one, shift_one, beam_two,
        shift_two, sems,
    ):
        inside = inside_test(bins)
        copies = fetch(
            (far_beam_one, far_shift_one, far_beam_two, far_shift_two),
            (beam_one, shift_one, beam_two, shift_two), sems,
        )
        compress_pair((a0,), (a1,), bins, band_ref, source, columns, images, inside)
        arrived(copies)
        merge_one(images, (beam_one, shift_one, taps_ref, turn_ref), level_one, inside)
        _, _, high = position()
        tables = (beam_two, shift_two, taps_ref, turn_ref)

        def one(parent):
            for chunk, part in enumerate(second_side(level_one, tables, parent, high)):
                out_ref[parent, pl.ds(8 * chunk, 8), :] = part

        loop_over(TWO, one)

    return kernel


def second_kernel(bins):
    def kernel(
        far_beam_one, far_shift_one, far_beam_two, far_shift_two, a2, a3, r3, band_ref, taps_ref,
        turn_ref, half_ref, out_ref, source, columns, images, level_one, beam_one, shift_one,
        beam_two, shift_two, sems, level_two,
    ):
        inside = inside_test(bins)
        copies = fetch(
            (far_beam_one, far_shift_one, far_beam_two, far_shift_two),
            (beam_one, shift_one, beam_two, shift_two), sems,
        )
        compress_pair((a2,), (a3, r3), bins, band_ref, source, columns, images, inside)
        arrived(copies)
        merge_one(images, (beam_one, shift_one, taps_ref, turn_ref), level_one, inside)
        _, _, high = position()
        tables = (beam_two, shift_two, taps_ref, turn_ref)

        def one(parent):
            for chunk, part in enumerate(second_side(level_one, tables, parent, 1 - high)):
                rows = pl.ds(8 * chunk, 8)
                level_two[parent, rows, :] = part + half_ref[parent, rows, :]

        loop_over(TWO, one)
        for half in range(2):
            for chunk in range(0, CHUNKS, 2):
                size = min(2, CHUNKS - chunk) * 8
                parts = [
                    level_two[16 * half + image, pl.ds(8 * chunk, size), :].astype(jnp.bfloat16)
                    for image in range(GROUPS)
                ]
                for g, part in enumerate(exchange(parts)):
                    columns[pl.ds(ROWS * g + 8 * chunk, size), :] = part.astype(jnp.float32)
            for block in range(BLOCKS):
                turned = columns[pl.ds(STEP * block, STEP), :].astype(jnp.bfloat16).T
                for comp in range(2):
                    for u in range(SPANS):
                        left = WIDE * u + STEP * block - LEFT
                        if 0 <= left < bins:
                            row = (comp * SPANS + u) * 16
                            out_ref[comp, pl.ds(16 * half, 16), pl.ds(left, 128)] = turned[
                                row : row + 16
                            ]

    return kernel


def neighbours(head, tail, axis):
    count = lax.axis_size(axis)
    even = lax.axis_index(axis) % 2 == 0
    near = [(i, i ^ 1) for i in range(count) if i ^ 1 < count]
    far = [(i + 1, i + 2) for i in range(0, count - 2, 2)]
    far = far + [(b, a) for a, b in far]
    first = lax.ppermute(jnp.where(even, tail, head), axis, near)
    second = lax.ppermute(jnp.where(even, head, tail), axis, far) if far else jnp.zeros_like(first)
    return jnp.where(even, second, first), jnp.where(even, first, second)


def body(
    echo, chirp, beam_one, shift_one, frac_one, base_one, beam_two, shift_two, frac_two, base_two
):
    signal = echo[0]
    beams, _, bins = signal.shape
    span = STEP + chirp.shape[1]
    pulse = lax.axis_index("pulse")

    signal = signal.reshape(4, beams // 4, 2, bins).transpose(0, 2, 1, 3)
    small = (
        chirp, beam_one, shift_one, frac_one, base_one, beam_two, shift_two, frac_two, base_two
    )
    chirp, beam_one, shift_one, frac_one, base_one, beam_two, shift_two, frac_two, base_two = (
        pltpu.with_memory_space_constraint(array, pltpu.HBM) for array in small
    )

    def block_of(array, mask):
        index = pulse ^ mask
        return lax.dynamic_index_in_dim(array, 2 * (index % 2) + index // 2 % 2, 0, keepdims=False)

    def sent(array, mask):
        count = lax.axis_size("pulse")
        return lax.ppermute(array, "pulse", [(i, i ^ mask) for i in range(count)])

    far_main = sent(block_of(signal, 3), 3)
    from_left, from_right = neighbours(
        signal[:, :, :, :span], signal[:, :, :, bins - span :], "range"
    )
    from_left = from_left[:, :, :, span - LEFT :]
    wide = jnp.concatenate([from_left, signal, from_right], axis=3)
    rims = jnp.concatenate([from_left, from_right], axis=3)
    parts = [block_of(wide, 0)] + [sent(block_of(wide, mask), mask) for mask in (1, 2)]
    far_rim = sent(block_of(rims, 3), 3)

    vmem = pl.BlockSpec(memory_space=pltpu.VMEM)
    far = pl.BlockSpec(memory_space=pltpu.HBM)

    def held(space, *arrays):
        return [space(a.shape, a.dtype) for a in arrays] + [
            pltpu.SemaphoreType.DMA((len(arrays),))
        ]

    params = pltpu.CompilerParams(vmem_limit_bytes=24 << 20)
    count = 2 * (ONE + TWO)
    band, taps, turns = pl.pallas_call(
        prep_kernel(bins),
        out_shape=(
            jax.ShapeDtypeStruct((span, 2 * STEP), jnp.bfloat16),
            jax.ShapeDtypeStruct((count, 8, 128), jnp.float32),
            jax.ShapeDtypeStruct((count, 2, ROWS, 128), jnp.float32),
        ),
        in_specs=[far] * 7,
        out_specs=(vmem,) * 3,
        scratch_shapes=held(
            pltpu.VMEM, chirp, shift_one, frac_one, base_one, shift_two, frac_two, base_two
        ),
        compiler_params=params,
        name="prepare",
    )(chirp, shift_one, frac_one, base_one, shift_two, frac_two, base_two)

    index_tables = (beam_one, shift_one, beam_two, shift_two)
    scratch = [
        pltpu.VMEM((2, 16, SPANS * WIDE + span - STEP), jnp.bfloat16),
        pltpu.VMEM((WIDE, 128), jnp.float32),
        pltpu.VMEM((16, TALL, 128), jnp.float32),
        pltpu.VMEM((ONE, TALL, 128), jnp.float32),
    ] + held(pltpu.SMEM, *index_tables)
    half = pl.pallas_call(
        first_kernel(bins),
        out_shape=jax.ShapeDtypeStruct((TWO, ROWS, 128), jnp.float32),
        in_specs=[far] * 4 + [vmem] * 5,
        out_specs=vmem,
        scratch_shapes=scratch,
        compiler_params=params,
        name="first_pair",
    )(*index_tables, parts[0], parts[1], band, taps, turns)
    image = pl.pallas_call(
        second_kernel(bins),
        out_shape=jax.ShapeDtypeStruct((2, TWO, bins), jnp.bfloat16),
        in_specs=[far] * 4 + [vmem] * 7,
        out_specs=vmem,
        scratch_shapes=scratch + [pltpu.VMEM((TWO, ROWS, 128), jnp.float32)],
        compiler_params=params,
        name="second_pair",
    )(*index_tables, parts[2], far_main, far_rim, band, taps, turns, half)
    return image.transpose(1, 0, 2)[None, None]


def solution(mesh):
    in_specs = (P(("scene", "pulse"), "rep", None, "range"),) + (P(),) * 9
    out_specs = P("rep", ("scene", "pulse"), None, None, "range")

    return jax.shard_map(body, mesh=mesh, in_specs=in_specs, out_specs=out_specs, check_vma=False)
```

```python
import jax
import jax.numpy as jnp
from jax import lax
from jax.experimental import pallas as pl
from jax.experimental.pallas import tpu as pltpu
from jax.sharding import PartitionSpec as P

LEFT = 128
STEP = 128
ROWS = 56
COLS = 64
GROUPS = 16
RIM = 32
WIDE = GROUPS * ROWS
SPANS = COLS // GROUPS
CHUNKS = ROWS // 8
BLOCKS = WIDE // STEP
ONE, TWO = 16, 32
TALL = ROWS + 2 * RIM
TOGETHER = 16


def position():
    rep, pulse = lax.axis_index("rep"), lax.axis_index("pulse")
    low, high = pulse % 2, pulse // 2 % 2
    return 4 * rep + 2 * low + high, low, high


def lane_ids(shape):
    return lax.broadcasted_iota(jnp.int32, shape, len(shape) - 1)


def row_ids(shape):
    return lax.broadcasted_iota(jnp.int32, shape, len(shape) - 2)


def exchange(parts):
    parts = list(parts)
    lane = lane_ids(parts[0].shape)
    step = 1
    while step < len(parts):
        low = (lane & step) == 0
        for first in range(len(parts)):
            if first & step:
                continue
            a, b = parts[first], parts[first + step]
            parts[first] = jnp.where(low, a, pltpu.roll(b, step, 1))
            parts[first + step] = jnp.where(low, pltpu.roll(a, 128 - step, 1), b)
        step *= 2
    return parts


def store_rimmed(ref, index, chunk, value):
    row = 8 * chunk
    ref[index, pl.ds(RIM + row, 8), :] = value
    if row >= ROWS - RIM:
        ref[index, pl.ds(row - (ROWS - RIM), 8), :] = pltpu.roll(value, 1, 1)
    if row < RIM:
        ref[index, pl.ds(RIM + ROWS + row, 8), :] = pltpu.roll(value, 127, 1)


def inside_test(bins):
    first_bin = lax.axis_index("range") * bins
    bin_total = bins * lax.axis_size("range")
    shape = (8, 128)
    place = (lane_ids(shape) & (COLS - 1)) * ROWS + row_ids(shape) + (first_bin - LEFT)

    def inside(chunk, value):
        spot = place + 8 * chunk
        return jnp.where((spot >= 0) & (spot < bin_total), value, 0.0)

    return inside


def fetch(sources, targets, sems):
    copies = [
        pltpu.make_async_copy(source, target, sems.at[index])
        for index, (source, target) in enumerate(zip(sources, targets))
    ]
    for copy in copies:
        copy.start()
    return copies


def arrived(copies):
    for copy in copies:
        copy.wait()


def prep_kernel(bins):
    def kernel(*refs):
        far, (band_ref, taps_ref, turn_ref) = refs[:7], refs[7:10]
        chirp_ref, shift_one, frac_one, base_one, shift_two, frac_two, base_two = refs[10:17]
        copies = fetch(far, refs[10:17], refs[17])
        own, _, _ = position()
        first_bin = lax.axis_index("range") * bins
        bin_total = bins * lax.axis_size("range")
        span = band_ref.shape[0]
        arrived(copies[:1])
        for part in range(2):
            row = chirp_ref[part : part + 1, :].astype(jnp.float32)
            row = jnp.concatenate([row, jnp.zeros((1, STEP), jnp.float32)], axis=1)
            band = pltpu.roll(jnp.broadcast_to(row, (STEP, span)), 0, 1, stride=1, stride_axis=0)
            for block in range(span // 128):
                turned = band[:, 128 * block : 128 * block + 128].T
                band_ref[pl.ds(128 * block, 128), pl.ds(STEP * part, STEP)] = turned.astype(
                    jnp.bfloat16
                )

        arrived(copies[1:])
        shape = (8, 128)
        lane = lane_ids(shape)

        def packed(first, second):
            total = jnp.zeros(shape, jnp.float32)
            at = 0
            for ref, width in ((first, ONE), (second, TWO)):
                offset = own * width
                for child in range(2):
                    row = ref[child : child + 1, 0:128].astype(jnp.float32)
                    for block in range(1, ref.shape[1] // 128):
                        other = ref[child : child + 1, 128 * block : 128 * block + 128]
                        row = jnp.where(offset // 128 == block, other.astype(jnp.float32), row)
                    row = pltpu.roll(
                        jnp.broadcast_to(row, shape), (at + 256 - offset % 128) % 128, 1
                    )
                    total = jnp.where((lane >= at) & (lane < at + width), row, total)
                    at += width
            return total

        frac = packed(frac_one, frac_two)
        base = packed(base_one, base_two)
        slope = 0.5 * (packed(shift_one, shift_two) + frac)
        row = row_ids(shape).astype(jnp.float32)
        spread = (row - 3.0) - frac
        turned = jnp.pi * spread
        still = turned == 0.0
        safe = jnp.where(still, 1.0, turned)
        weights = jnp.where(still, 1.0, jnp.sin(safe) / safe) * (
            0.54 + 0.46 * jnp.cos(jnp.pi * spread / 4.0)
        )
        count = taps_ref.shape[0]
        square = (128, 128)
        base_rows = jnp.broadcast_to(base[0:1], square).T[:count]
        slope_rows = jnp.broadcast_to(slope[0:1], square).T[:count]
        wide = lane_ids((count, 128))
        spot = (wide & (COLS - 1)) * ROWS + (first_bin - LEFT)
        angle = base_rows + slope_rows * (spot.astype(jnp.float32) / bin_total - 0.5)
        cos_col, sin_col = jnp.cos(angle), jnp.sin(angle)
        sign = jnp.where(lane < COLS, -1.0, 1.0)
        fine, coarse = slope * (row / bin_total), slope * (8.0 / bin_total)
        cos_fine, sin_fine = jnp.cos(fine), jnp.sin(fine)
        cos_coarse, sin_coarse = jnp.cos(coarse), jnp.sin(coarse)
        for place in range(count):

            def spread_out(table):
                return jnp.broadcast_to(table[:, place : place + 1], shape)

            taps_ref[place] = spread_out(weights)
            cos_all = jnp.broadcast_to(cos_col[place : place + 1], shape)
            sin_all = jnp.broadcast_to(sin_col[place : place + 1], shape) * sign
            cos_step, sin_step = spread_out(cos_fine), spread_out(sin_fine) * sign
            cos_next, sin_next = spread_out(cos_coarse), spread_out(sin_coarse) * sign
            for chunk in range(CHUNKS):
                cos_all, sin_all = (
                    cos_all * cos_step - sin_all * sin_step,
                    sin_all * cos_step + cos_all * sin_step,
                )
                turn_ref[place, 0, pl.ds(8 * chunk, 8), :] = cos_all
                turn_ref[place, 1, pl.ds(8 * chunk, 8), :] = sin_all
                cos_step, sin_step = cos_next, sin_next

    return kernel


def compress_pair(near, far, bins, band_ref, source, columns, images, inside):
    rest = source.shape[2] - LEFT - bins
    wide = near[0].shape[2] - LEFT - bins

    def piece(held, comp, at, size):
        if len(held) == 1:
            return held[0][comp, :, pl.ds(at, size)]
        main, rim = held
        if at == LEFT:
            return main[comp]
        return rim[comp, :, pl.ds(min(at, LEFT), size)]

    for comp in range(2):
        for at, size in ((0, LEFT), (LEFT, bins), (LEFT + bins, wide)):
            sides = [piece(held, comp, at, size).astype(jnp.float32) for held in (near, far)]
            source[comp, :, pl.ds(at, size)] = jnp.concatenate(sides, axis=0).astype(jnp.bfloat16)
        if rest > wide:
            source[comp, :, pl.ds(LEFT + bins + wide, rest - wide)] = jnp.zeros(
                (16, rest - wide), jnp.bfloat16
            )
    span = band_ref.shape[0]
    windows = jnp.concatenate(
        [
            source[comp, :, pl.ds(WIDE * u + STEP * block, span)]
            for block in range(BLOCKS)
            for comp in range(2)
            for u in range(SPANS)
        ],
        axis=0,
    )
    product = jnp.dot(windows, band_ref[...], preferred_element_type=jnp.float32)
    half = 16 * SPANS
    for block in range(BLOCKS):
        top = product[128 * block : 128 * block + half]
        low = product[128 * block + half : 128 * block + 128]
        result = jnp.concatenate(
            [top[:, :STEP] + low[:, STEP:], low[:, :STEP] - top[:, STEP:]], axis=0
        )
        columns[pl.ds(STEP * block, STEP), :] = result.astype(jnp.bfloat16).T.astype(jnp.float32)
    for chunk in range(0, CHUNKS, 2):
        size = min(2, CHUNKS - chunk) * 8
        parts = [columns[pl.ds(ROWS * g + 8 * chunk, size), :] for g in range(GROUPS)]
        parts = exchange([part.astype(jnp.bfloat16) for part in parts])
        for image, part in enumerate(parts):
            part = part.astype(jnp.float32)
            for extra in range(size // 8):
                value = inside(chunk + extra, part[8 * extra : 8 * extra + 8])
                store_rimmed(images, image, chunk + extra, value)


def contribution(images, tables, parent, child, first_parent, first_image, width, at):
    beam_ref, shift_ref, taps_ref, turn_ref = tables
    place = at + child * width + parent
    image = beam_ref[child, first_parent + parent] + first_image
    start = shift_ref[child, first_parent + parent] + (RIM - 3)
    value = None
    for tap in range(8):
        term = images[image, pl.ds(start + tap, ROWS), :] * taps_ref[place, pl.ds(tap, 1), :]
        value = term if value is None else value + term
    parts = []
    for chunk in range(CHUNKS):
        part = value[8 * chunk : 8 * chunk + 8]
        parts.append(
            part * turn_ref[place, 0, pl.ds(8 * chunk, 8), :]
            + pltpu.roll(part, COLS, 1) * turn_ref[place, 1, pl.ds(8 * chunk, 8), :]
        )
    return parts


def loop_over(count, one):
    def step(index, carry):
        for extra in range(TOGETHER):
            one(TOGETHER * index + extra)
        return carry

    lax.fori_loop(0, count // TOGETHER, step, 0)


def merge_one(images, tables, result, inside):
    own, low, _ = position()

    def one(parent):
        sides = [
            contribution(
                images, tables, parent, child, ONE * own, (child ^ low) * 8 - 8 * own, ONE, 0
            )
            for child in range(2)
        ]
        for chunk, (a, b) in enumerate(zip(*sides)):
            store_rimmed(result, parent, chunk, inside(chunk, a + b))

    loop_over(ONE, one)


def second_side(images, tables, parent, child):
    own, _, _ = position()
    return contribution(images, tables, parent, child, TWO * own, -ONE * own, TWO, 2 * ONE)


def first_kernel(bins):
    def kernel(
        far_beam_one, far_shift_one, far_beam_two, far_shift_two, a0, a1, r1, band_ref, taps_ref,
        turn_ref, out_ref, source, columns, images, level_one, beam_one, shift_one, beam_two,
        shift_two, sems,
    ):
        inside = inside_test(bins)
        copies = fetch(
            (far_beam_one, far_shift_one, far_beam_two, far_shift_two),
            (beam_one, shift_one, beam_two, shift_two), sems,
        )
        compress_pair((a0,), (a1, r1), bins, band_ref, source, columns, images, inside)
        arrived(copies)
        merge_one(images, (beam_one, shift_one, taps_ref, turn_ref), level_one, inside)
        _, _, high = position()
        tables = (beam_two, shift_two, taps_ref, turn_ref)

        def one(parent):
            for chunk, part in enumerate(second_side(level_one, tables, parent, high)):
                out_ref[parent, pl.ds(8 * chunk, 8), :] = part

        loop_over(TWO, one)

    return kernel


def second_kernel(bins):
    def kernel(
        far_beam_one, far_shift_one, far_beam_two, far_shift_two, a2, a3, r3, band_ref, taps_ref,
        turn_ref, half_ref, out_ref, source, columns, images, level_one, beam_one, shift_one,
        beam_two, shift_two, sems, level_two,
    ):
        inside = inside_test(bins)
        copies = fetch(
            (far_beam_one, far_shift_one, far_beam_two, far_shift_two),
            (beam_one, shift_one, beam_two, shift_two), sems,
        )
        compress_pair((a2,), (a3, r3), bins, band_ref, source, columns, images, inside)
        arrived(copies)
        merge_one(images, (beam_one, shift_one, taps_ref, turn_ref), level_one, inside)
        _, _, high = position()
        tables = (beam_two, shift_two, taps_ref, turn_ref)

        def one(parent):
            for chunk, part in enumerate(second_side(level_one, tables, parent, 1 - high)):
                rows = pl.ds(8 * chunk, 8)
                level_two[parent, rows, :] = part + half_ref[parent, rows, :]

        loop_over(TWO, one)
        for half in range(2):
            for chunk in range(0, CHUNKS, 2):
                size = min(2, CHUNKS - chunk) * 8
                parts = [
                    level_two[16 * half + image, pl.ds(8 * chunk, size), :].astype(jnp.bfloat16)
                    for image in range(GROUPS)
                ]
                for g, part in enumerate(exchange(parts)):
                    columns[pl.ds(ROWS * g + 8 * chunk, size), :] = part.astype(jnp.float32)
            for block in range(BLOCKS):
                turned = columns[pl.ds(STEP * block, STEP), :].astype(jnp.bfloat16).T
                for comp in range(2):
                    for u in range(SPANS):
                        left = WIDE * u + STEP * block - LEFT
                        if 0 <= left < bins:
                            row = (comp * SPANS + u) * 16
                            out_ref[comp, pl.ds(16 * half, 16), pl.ds(left, 128)] = turned[
                                row : row + 16
                            ]

    return kernel


def neighbours(head, tail, axis):
    count = lax.axis_size(axis)
    even = lax.axis_index(axis) % 2 == 0
    near = [(i, i ^ 1) for i in range(count) if i ^ 1 < count]
    far = [(i + 1, i + 2) for i in range(0, count - 2, 2)]
    far = far + [(b, a) for a, b in far]
    first = lax.ppermute(jnp.where(even, tail, head), axis, near)
    second = lax.ppermute(jnp.where(even, head, tail), axis, far) if far else jnp.zeros_like(first)
    return jnp.where(even, second, first), jnp.where(even, first, second)


def body(
    echo, chirp, beam_one, shift_one, frac_one, base_one, beam_two, shift_two, frac_two, base_two
):
    signal = echo[0]
    beams, _, bins = signal.shape
    span = STEP + chirp.shape[1]
    pulse = lax.axis_index("pulse")

    signal = signal.reshape(4, beams // 4, 2, bins).transpose(0, 2, 1, 3)
    small = (
        chirp, beam_one, shift_one, frac_one, base_one, beam_two, shift_two, frac_two, base_two
    )
    chirp, beam_one, shift_one, frac_one, base_one, beam_two, shift_two, frac_two, base_two = (
        pltpu.with_memory_space_constraint(array, pltpu.HBM) for array in small
    )

    def block_of(array, mask):
        index = pulse ^ mask
        return lax.dynamic_index_in_dim(array, 2 * (index % 2) + index // 2 % 2, 0, keepdims=False)

    def sent(array, mask):
        count = lax.axis_size("pulse")
        return lax.ppermute(array, "pulse", [(i, i ^ mask) for i in range(count)])

    far_main = sent(block_of(signal, 3), 3)
    near_main = sent(block_of(signal, 1), 1)
    from_left, from_right = neighbours(
        signal[:, :, :, :span], signal[:, :, :, bins - span :], "range"
    )
    from_left = from_left[:, :, :, span - LEFT :]
    wide = jnp.concatenate([from_left, signal, from_right], axis=3)
    rims = jnp.concatenate([from_left, from_right], axis=3)
    middle = sent(block_of(wide, 2), 2)
    near_rim = sent(block_of(rims, 1), 1)
    far_rim = sent(block_of(rims, 3), 3)

    vmem = pl.BlockSpec(memory_space=pltpu.VMEM)
    far = pl.BlockSpec(memory_space=pltpu.HBM)

    def held(space, *arrays):
        return [space(a.shape, a.dtype) for a in arrays] + [
            pltpu.SemaphoreType.DMA((len(arrays),))
        ]

    params = pltpu.CompilerParams(vmem_limit_bytes=24 << 20)
    count = 2 * (ONE + TWO)
    band, taps, turns = pl.pallas_call(
        prep_kernel(bins),
        out_shape=(
            jax.ShapeDtypeStruct((span, 2 * STEP), jnp.bfloat16),
            jax.ShapeDtypeStruct((count, 8, 128), jnp.float32),
            jax.ShapeDtypeStruct((count, 2, ROWS, 128), jnp.float32),
        ),
        in_specs=[far] * 7,
        out_specs=(vmem,) * 3,
        scratch_shapes=held(
            pltpu.VMEM, chirp, shift_one, frac_one, base_one, shift_two, frac_two, base_two
        ),
        compiler_params=params,
        name="prepare",
    )(chirp, shift_one, frac_one, base_one, shift_two, frac_two, base_two)

    index_tables = (beam_one, shift_one, beam_two, shift_two)
    scratch = [
        pltpu.VMEM((2, 16, SPANS * WIDE + span - STEP), jnp.bfloat16),
        pltpu.VMEM((WIDE, 128), jnp.float32),
        pltpu.VMEM((16, TALL, 128), jnp.float32),
        pltpu.VMEM((ONE, TALL, 128), jnp.float32),
    ] + held(pltpu.SMEM, *index_tables)
    half = pl.pallas_call(
        first_kernel(bins),
        out_shape=jax.ShapeDtypeStruct((TWO, ROWS, 128), jnp.float32),
        in_specs=[far] * 4 + [vmem] * 6,
        out_specs=vmem,
        scratch_shapes=scratch,
        compiler_params=params,
        name="first_pair",
    )(*index_tables, block_of(wide, 0), near_main, near_rim, band, taps, turns)
    image = pl.pallas_call(
        second_kernel(bins),
        out_shape=jax.ShapeDtypeStruct((2, TWO, bins), jnp.bfloat16),
        in_specs=[far] * 4 + [vmem] * 7,
        out_specs=vmem,
        scratch_shapes=scratch + [pltpu.VMEM((TWO, ROWS, 128), jnp.float32)],
        compiler_params=params,
        name="second_pair",
    )(*index_tables, middle, far_main, far_rim, band, taps, turns, half)
    return image.transpose(1, 0, 2)[None, None]


def solution(mesh):
    in_specs = (P(("scene", "pulse"), "rep", None, "range"),) + (P(),) * 9
    out_specs = P("rep", ("scene", "pulse"), None, None, "range")

    return jax.shard_map(body, mesh=mesh, in_specs=in_specs, out_specs=out_specs, check_vma=False)
```

```python
import jax
import jax.numpy as jnp
from jax import lax
from jax.experimental import pallas as pl
from jax.experimental.pallas import tpu as pltpu
from jax.sharding import PartitionSpec as P

LEFT = 128
STEP = 128
ROWS = 56
COLS = 64
GROUPS = 16
RIM = 32
WIDE = GROUPS * ROWS
SPANS = COLS // GROUPS
CHUNKS = ROWS // 8
BLOCKS = WIDE // STEP
ONE, TWO = 16, 32
TALL = ROWS + 2 * RIM
TOGETHER = 16


def position():
    rep, pulse = lax.axis_index("rep"), lax.axis_index("pulse")
    low, high = pulse % 2, pulse // 2 % 2
    return 4 * rep + 2 * low + high, low, high


def lane_ids(shape):
    return lax.broadcasted_iota(jnp.int32, shape, len(shape) - 1)


def row_ids(shape):
    return lax.broadcasted_iota(jnp.int32, shape, len(shape) - 2)


def exchange(parts):
    parts = list(parts)
    lane = lane_ids(parts[0].shape)
    step = 1
    while step < len(parts):
        low = (lane & step) == 0
        for first in range(len(parts)):
            if first & step:
                continue
            a, b = parts[first], parts[first + step]
            parts[first] = jnp.where(low, a, pltpu.roll(b, step, 1))
            parts[first + step] = jnp.where(low, pltpu.roll(a, 128 - step, 1), b)
        step *= 2
    return parts


def store_rimmed(ref, index, chunk, value):
    row = 8 * chunk
    ref[index, pl.ds(RIM + row, 8), :] = value
    if row >= ROWS - RIM:
        ref[index, pl.ds(row - (ROWS - RIM), 8), :] = pltpu.roll(value, 1, 1)
    if row < RIM:
        ref[index, pl.ds(RIM + ROWS + row, 8), :] = pltpu.roll(value, 127, 1)


def inside_test(bins):
    first_bin = lax.axis_index("range") * bins
    bin_total = bins * lax.axis_size("range")
    shape = (8, 128)
    place = (lane_ids(shape) & (COLS - 1)) * ROWS + row_ids(shape) + (first_bin - LEFT)

    def inside(chunk, value):
        spot = place + 8 * chunk
        return jnp.where((spot >= 0) & (spot < bin_total), value, 0.0)

    return inside


def fetch(sources, targets, sems):
    copies = [
        pltpu.make_async_copy(source, target, sems.at[index])
        for index, (source, target) in enumerate(zip(sources, targets))
    ]
    for copy in copies:
        copy.start()
    return copies


def arrived(copies):
    for copy in copies:
        copy.wait()


def prep_kernel(bins):
    def kernel(*refs):
        far, (band_ref, taps_ref, turn_ref) = refs[:7], refs[7:10]
        chirp_ref, shift_one, frac_one, base_one, shift_two, frac_two, base_two = refs[10:17]
        copies = fetch(far, refs[10:17], refs[17])
        own, _, _ = position()
        first_bin = lax.axis_index("range") * bins
        bin_total = bins * lax.axis_size("range")
        span = band_ref.shape[0]
        arrived(copies[:1])
        for part in range(2):
            row = chirp_ref[part : part + 1, :].astype(jnp.float32)
            row = jnp.concatenate([row, jnp.zeros((1, STEP), jnp.float32)], axis=1)
            band = pltpu.roll(jnp.broadcast_to(row, (STEP, span)), 0, 1, stride=1, stride_axis=0)
            for block in range(span // 128):
                turned = band[:, 128 * block : 128 * block + 128].T
                band_ref[pl.ds(128 * block, 128), pl.ds(STEP * part, STEP)] = turned.astype(
                    jnp.bfloat16
                )

        arrived(copies[1:])
        shape = (8, 128)
        lane = lane_ids(shape)

        def packed(first, second):
            total = jnp.zeros(shape, jnp.float32)
            at = 0
            for ref, width in ((first, ONE), (second, TWO)):
                offset = own * width
                for child in range(2):
                    row = ref[child : child + 1, 0:128].astype(jnp.float32)
                    for block in range(1, ref.shape[1] // 128):
                        other = ref[child : child + 1, 128 * block : 128 * block + 128]
                        row = jnp.where(offset // 128 == block, other.astype(jnp.float32), row)
                    row = pltpu.roll(
                        jnp.broadcast_to(row, shape), (at + 256 - offset % 128) % 128, 1
                    )
                    total = jnp.where((lane >= at) & (lane < at + width), row, total)
                    at += width
            return total

        frac = packed(frac_one, frac_two)
        base = packed(base_one, base_two)
        slope = 0.5 * (packed(shift_one, shift_two) + frac)
        row = row_ids(shape).astype(jnp.float32)
        spread = (row - 3.0) - frac
        turned = jnp.pi * spread
        still = turned == 0.0
        safe = jnp.where(still, 1.0, turned)
        weights = jnp.where(still, 1.0, jnp.sin(safe) / safe) * (
            0.54 + 0.46 * jnp.cos(jnp.pi * spread / 4.0)
        )
        count = taps_ref.shape[0]
        square = (128, 128)
        base_rows = jnp.broadcast_to(base[0:1], square).T[:count]
        slope_rows = jnp.broadcast_to(slope[0:1], square).T[:count]
        wide = lane_ids((count, 128))
        spot = (wide & (COLS - 1)) * ROWS + (first_bin - LEFT)
        angle = base_rows + slope_rows * (spot.astype(jnp.float32) / bin_total - 0.5)
        cos_col, sin_col = jnp.cos(angle), jnp.sin(angle)
        sign = jnp.where(lane < COLS, -1.0, 1.0)
        fine, coarse = slope * (row / bin_total), slope * (8.0 / bin_total)
        cos_fine, sin_fine = jnp.cos(fine), jnp.sin(fine)
        cos_coarse, sin_coarse = jnp.cos(coarse), jnp.sin(coarse)
        for place in range(count):

            def spread_out(table):
                return jnp.broadcast_to(table[:, place : place + 1], shape)

            taps_ref[place] = spread_out(weights)
            cos_all = jnp.broadcast_to(cos_col[place : place + 1], shape)
            sin_all = jnp.broadcast_to(sin_col[place : place + 1], shape) * sign
            cos_step, sin_step = spread_out(cos_fine), spread_out(sin_fine) * sign
            cos_next, sin_next = spread_out(cos_coarse), spread_out(sin_coarse) * sign
            twice = cos_next + cos_next
            before = None
            for chunk in range(CHUNKS):
                if chunk < 2:
                    now = (
                        cos_all * cos_step - sin_all * sin_step,
                        sin_all * cos_step + cos_all * sin_step,
                    )
                else:
                    now = (twice * cos_all - before[0], twice * sin_all - before[1])
                before = (cos_all, sin_all)
                cos_all, sin_all = now
                turn_ref[place, 0, pl.ds(8 * chunk, 8), :] = cos_all
                turn_ref[place, 1, pl.ds(8 * chunk, 8), :] = sin_all
                cos_step, sin_step = cos_next, sin_next

    return kernel


def compress_pair(near, far, bins, band_ref, source, columns, images, inside):
    rest = source.shape[2] - LEFT - bins
    wide = near[0].shape[2] - LEFT - bins

    def piece(held, comp, at, size):
        if len(held) == 1:
            return held[0][comp, :, pl.ds(at, size)]
        main, rim = held
        if at == LEFT:
            return main[comp]
        return rim[comp, :, pl.ds(min(at, LEFT), size)]

    for comp in range(2):
        for at, size in ((0, LEFT), (LEFT, bins), (LEFT + bins, wide)):
            sides = [piece(held, comp, at, size).astype(jnp.float32) for held in (near, far)]
            source[comp, :, pl.ds(at, size)] = jnp.concatenate(sides, axis=0).astype(jnp.bfloat16)
        if rest > wide:
            source[comp, :, pl.ds(LEFT + bins + wide, rest - wide)] = jnp.zeros(
                (16, rest - wide), jnp.bfloat16
            )
    span = band_ref.shape[0]
    windows = jnp.concatenate(
        [
            source[comp, :, pl.ds(WIDE * u + STEP * block, span)]
            for block in range(BLOCKS)
            for comp in range(2)
            for u in range(SPANS)
        ],
        axis=0,
    )
    product = jnp.dot(windows, band_ref[...], preferred_element_type=jnp.float32)
    half = 16 * SPANS
    for block in range(BLOCKS):
        top = product[128 * block : 128 * block + half]
        low = product[128 * block + half : 128 * block + 128]
        result = jnp.concatenate(
            [top[:, :STEP] + low[:, STEP:], low[:, :STEP] - top[:, STEP:]], axis=0
        )
        columns[pl.ds(STEP * block, STEP), :] = result.astype(jnp.bfloat16).T.astype(jnp.float32)
    for chunk in range(0, CHUNKS, 2):
        size = min(2, CHUNKS - chunk) * 8
        parts = [columns[pl.ds(ROWS * g + 8 * chunk, size), :] for g in range(GROUPS)]
        parts = exchange([part.astype(jnp.bfloat16) for part in parts])
        for image, part in enumerate(parts):
            part = part.astype(jnp.float32)
            for extra in range(size // 8):
                value = inside(chunk + extra, part[8 * extra : 8 * extra + 8])
                store_rimmed(images, image, chunk + extra, value)


def contribution(images, tables, parent, child, first_parent, first_image, width, at):
    beam_ref, shift_ref, taps_ref, turn_ref = tables
    place = at + child * width + parent
    image = beam_ref[child, first_parent + parent] + first_image
    start = shift_ref[child, first_parent + parent] + (RIM - 3)
    value = None
    for tap in range(8):
        term = images[image, pl.ds(start + tap, ROWS), :] * taps_ref[place, pl.ds(tap, 1), :]
        value = term if value is None else value + term
    parts = []
    for chunk in range(CHUNKS):
        part = value[8 * chunk : 8 * chunk + 8]
        parts.append(
            part * turn_ref[place, 0, pl.ds(8 * chunk, 8), :]
            + pltpu.roll(part, COLS, 1) * turn_ref[place, 1, pl.ds(8 * chunk, 8), :]
        )
    return parts


def loop_over(count, one):
    def step(index, carry):
        for extra in range(TOGETHER):
            one(TOGETHER * index + extra)
        return carry

    lax.fori_loop(0, count // TOGETHER, step, 0)


def merge_one(images, tables, result, inside):
    own, low, _ = position()

    def one(parent):
        sides = [
            contribution(
                images, tables, parent, child, ONE * own, (child ^ low) * 8 - 8 * own, ONE, 0
            )
            for child in range(2)
        ]
        for chunk, (a, b) in enumerate(zip(*sides)):
            store_rimmed(result, parent, chunk, inside(chunk, a + b))

    loop_over(ONE, one)


def second_side(images, tables, parent, child):
    own, _, _ = position()
    return contribution(images, tables, parent, child, TWO * own, -ONE * own, TWO, 2 * ONE)


def first_kernel(bins):
    def kernel(
        far_beam_one, far_shift_one, far_beam_two, far_shift_two, a0, a1, r1, band_ref, taps_ref,
        turn_ref, out_ref, source, columns, images, level_one, beam_one, shift_one, beam_two,
        shift_two, sems,
    ):
        inside = inside_test(bins)
        copies = fetch(
            (far_beam_one, far_shift_one, far_beam_two, far_shift_two),
            (beam_one, shift_one, beam_two, shift_two), sems,
        )
        compress_pair((a0,), (a1, r1), bins, band_ref, source, columns, images, inside)
        arrived(copies)
        merge_one(images, (beam_one, shift_one, taps_ref, turn_ref), level_one, inside)
        _, _, high = position()
        tables = (beam_two, shift_two, taps_ref, turn_ref)

        def one(parent):
            for chunk, part in enumerate(second_side(level_one, tables, parent, high)):
                out_ref[parent, pl.ds(8 * chunk, 8), :] = part

        loop_over(TWO, one)

    return kernel


def second_kernel(bins):
    def kernel(
        far_beam_one, far_shift_one, far_beam_two, far_shift_two, a2, a3, r3, band_ref, taps_ref,
        turn_ref, half_ref, out_ref, source, columns, images, level_one, beam_one, shift_one,
        beam_two, shift_two, sems, level_two,
    ):
        inside = inside_test(bins)
        copies = fetch(
            (far_beam_one, far_shift_one, far_beam_two, far_shift_two),
            (beam_one, shift_one, beam_two, shift_two), sems,
        )
        compress_pair((a2,), (a3, r3), bins, band_ref, source, columns, images, inside)
        arrived(copies)
        merge_one(images, (beam_one, shift_one, taps_ref, turn_ref), level_one, inside)
        _, _, high = position()
        tables = (beam_two, shift_two, taps_ref, turn_ref)

        def one(parent):
            for chunk, part in enumerate(second_side(level_one, tables, parent, 1 - high)):
                rows = pl.ds(8 * chunk, 8)
                level_two[parent, rows, :] = part + half_ref[parent, rows, :]

        loop_over(TWO, one)
        for half in range(2):
            for chunk in range(0, CHUNKS, 2):
                size = min(2, CHUNKS - chunk) * 8
                parts = [
                    level_two[16 * half + image, pl.ds(8 * chunk, size), :].astype(jnp.bfloat16)
                    for image in range(GROUPS)
                ]
                for g, part in enumerate(exchange(parts)):
                    columns[pl.ds(ROWS * g + 8 * chunk, size), :] = part.astype(jnp.float32)
            for block in range(BLOCKS):
                turned = columns[pl.ds(STEP * block, STEP), :].astype(jnp.bfloat16).T
                for comp in range(2):
                    for u in range(SPANS):
                        left = WIDE * u + STEP * block - LEFT
                        if 0 <= left < bins:
                            row = (comp * SPANS + u) * 16
                            out_ref[comp, pl.ds(16 * half, 16), pl.ds(left, 128)] = turned[
                                row : row + 16
                            ]

    return kernel


def neighbours(head, tail, axis):
    count = lax.axis_size(axis)
    even = lax.axis_index(axis) % 2 == 0
    near = [(i, i ^ 1) for i in range(count) if i ^ 1 < count]
    far = [(i + 1, i + 2) for i in range(0, count - 2, 2)]
    far = far + [(b, a) for a, b in far]
    first = lax.ppermute(jnp.where(even, tail, head), axis, near)
    second = lax.ppermute(jnp.where(even, head, tail), axis, far) if far else jnp.zeros_like(first)
    return jnp.where(even, second, first), jnp.where(even, first, second)


def body(
    echo, chirp, beam_one, shift_one, frac_one, base_one, beam_two, shift_two, frac_two, base_two
):
    signal = echo[0]
    beams, _, bins = signal.shape
    span = STEP + chirp.shape[1]
    pulse = lax.axis_index("pulse")

    signal = signal.reshape(4, beams // 4, 2, bins).transpose(0, 2, 1, 3)
    small = (
        chirp, beam_one, shift_one, frac_one, base_one, beam_two, shift_two, frac_two, base_two
    )
    chirp, beam_one, shift_one, frac_one, base_one, beam_two, shift_two, frac_two, base_two = (
        pltpu.with_memory_space_constraint(array, pltpu.HBM) for array in small
    )

    def block_of(array, mask):
        index = pulse ^ mask
        return lax.dynamic_index_in_dim(array, 2 * (index % 2) + index // 2 % 2, 0, keepdims=False)

    def sent(array, mask):
        count = lax.axis_size("pulse")
        return lax.ppermute(array, "pulse", [(i, i ^ mask) for i in range(count)])

    far_main = sent(block_of(signal, 3), 3)
    near_main = sent(block_of(signal, 1), 1)
    from_left, from_right = neighbours(
        signal[:, :, :, :span], signal[:, :, :, bins - span :], "range"
    )
    from_left = from_left[:, :, :, span - LEFT :]
    wide = jnp.concatenate([from_left, signal, from_right], axis=3)
    rims = jnp.concatenate([from_left, from_right], axis=3)
    middle = sent(block_of(wide, 2), 2)
    near_rim = sent(block_of(rims, 1), 1)
    far_rim = sent(block_of(rims, 3), 3)

    vmem = pl.BlockSpec(memory_space=pltpu.VMEM)
    far = pl.BlockSpec(memory_space=pltpu.HBM)

    def held(space, *arrays):
        return [space(a.shape, a.dtype) for a in arrays] + [
            pltpu.SemaphoreType.DMA((len(arrays),))
        ]

    params = pltpu.CompilerParams(vmem_limit_bytes=24 << 20)
    count = 2 * (ONE + TWO)
    band, taps, turns = pl.pallas_call(
        prep_kernel(bins),
        out_shape=(
            jax.ShapeDtypeStruct((span, 2 * STEP), jnp.bfloat16),
            jax.ShapeDtypeStruct((count, 8, 128), jnp.float32),
            jax.ShapeDtypeStruct((count, 2, ROWS, 128), jnp.float32),
        ),
        in_specs=[far] * 7,
        out_specs=(vmem,) * 3,
        scratch_shapes=held(
            pltpu.VMEM, chirp, shift_one, frac_one, base_one, shift_two, frac_two, base_two
        ),
        compiler_params=params,
        name="prepare",
    )(chirp, shift_one, frac_one, base_one, shift_two, frac_two, base_two)

    index_tables = (beam_one, shift_one, beam_two, shift_two)
    scratch = [
        pltpu.VMEM((2, 16, SPANS * WIDE + span - STEP), jnp.bfloat16),
        pltpu.VMEM((WIDE, 128), jnp.float32),
        pltpu.VMEM((16, TALL, 128), jnp.float32),
        pltpu.VMEM((ONE, TALL, 128), jnp.float32),
    ] + held(pltpu.SMEM, *index_tables)
    half = pl.pallas_call(
        first_kernel(bins),
        out_shape=jax.ShapeDtypeStruct((TWO, ROWS, 128), jnp.float32),
        in_specs=[far] * 4 + [vmem] * 6,
        out_specs=vmem,
        scratch_shapes=scratch,
        compiler_params=params,
        name="first_pair",
    )(*index_tables, block_of(wide, 0), near_main, near_rim, band, taps, turns)
    image = pl.pallas_call(
        second_kernel(bins),
        out_shape=jax.ShapeDtypeStruct((2, TWO, bins), jnp.bfloat16),
        in_specs=[far] * 4 + [vmem] * 7,
        out_specs=vmem,
        scratch_shapes=scratch + [pltpu.VMEM((TWO, ROWS, 128), jnp.float32)],
        compiler_params=params,
        name="second_pair",
    )(*index_tables, middle, far_main, far_rim, band, taps, turns, half)
    return image.transpose(1, 0, 2)[None, None]


def solution(mesh):
    in_specs = (P(("scene", "pulse"), "rep", None, "range"),) + (P(),) * 9
    out_specs = P("rep", ("scene", "pulse"), None, None, "range")

    return jax.shard_map(body, mesh=mesh, in_specs=in_specs, out_specs=out_specs, check_vma=False)
```

```python
import jax
import jax.numpy as jnp
from jax import lax
from jax.experimental import pallas as pl
from jax.experimental.pallas import tpu as pltpu
from jax.sharding import PartitionSpec as P

LEFT = 128
STEP = 128
ROWS = 56
COLS = 64
GROUPS = 16
RIM = 32
WIDE = GROUPS * ROWS
SPANS = COLS // GROUPS
CHUNKS = ROWS // 8
BLOCKS = WIDE // STEP
ONE, TWO = 16, 32
TALL = ROWS + 2 * RIM
TOGETHER = 32


def position():
    rep, pulse = lax.axis_index("rep"), lax.axis_index("pulse")
    low, high = pulse % 2, pulse // 2 % 2
    return 4 * rep + 2 * low + high, low, high


def lane_ids(shape):
    return lax.broadcasted_iota(jnp.int32, shape, len(shape) - 1)


def row_ids(shape):
    return lax.broadcasted_iota(jnp.int32, shape, len(shape) - 2)


def exchange(parts):
    parts = list(parts)
    lane = lane_ids(parts[0].shape)
    step = 1
    while step < len(parts):
        low = (lane & step) == 0
        for first in range(len(parts)):
            if first & step:
                continue
            a, b = parts[first], parts[first + step]
            parts[first] = jnp.where(low, a, pltpu.roll(b, step, 1))
            parts[first + step] = jnp.where(low, pltpu.roll(a, 128 - step, 1), b)
        step *= 2
    return parts


def store_rimmed(ref, index, chunk, value):
    row = 8 * chunk
    ref[index, pl.ds(RIM + row, 8), :] = value
    if row >= ROWS - RIM:
        ref[index, pl.ds(row - (ROWS - RIM), 8), :] = pltpu.roll(value, 1, 1)
    if row < RIM:
        ref[index, pl.ds(RIM + ROWS + row, 8), :] = pltpu.roll(value, 127, 1)


def inside_test(bins):
    first_bin = lax.axis_index("range") * bins
    bin_total = bins * lax.axis_size("range")
    shape = (8, 128)
    place = (lane_ids(shape) & (COLS - 1)) * ROWS + row_ids(shape) + (first_bin - LEFT)

    def inside(chunk, value):
        spot = place + 8 * chunk
        return jnp.where((spot >= 0) & (spot < bin_total), value, 0.0)

    return inside


def fetch(sources, targets, sems):
    copies = [
        pltpu.make_async_copy(source, target, sems.at[index])
        for index, (source, target) in enumerate(zip(sources, targets))
    ]
    for copy in copies:
        copy.start()
    return copies


def arrived(copies):
    for copy in copies:
        copy.wait()


def prep_kernel(bins):
    def kernel(*refs):
        far, (band_ref, taps_ref, turn_ref) = refs[:7], refs[7:10]
        chirp_ref, shift_one, frac_one, base_one, shift_two, frac_two, base_two = refs[10:17]
        copies = fetch(far, refs[10:17], refs[17])
        own, _, _ = position()
        first_bin = lax.axis_index("range") * bins
        bin_total = bins * lax.axis_size("range")
        span = band_ref.shape[0]
        arrived(copies[:1])
        for part in range(2):
            row = chirp_ref[part : part + 1, :].astype(jnp.float32)
            row = jnp.concatenate([row, jnp.zeros((1, STEP), jnp.float32)], axis=1)
            band = pltpu.roll(jnp.broadcast_to(row, (STEP, span)), 0, 1, stride=1, stride_axis=0)
            for block in range(span // 128):
                turned = band[:, 128 * block : 128 * block + 128].T
                band_ref[pl.ds(128 * block, 128), pl.ds(STEP * part, STEP)] = turned.astype(
                    jnp.bfloat16
                )

        arrived(copies[1:])
        shape = (8, 128)
        lane = lane_ids(shape)

        def packed(first, second):
            total = jnp.zeros(shape, jnp.float32)
            at = 0
            for ref, width in ((first, ONE), (second, TWO)):
                offset = own * width
                for child in range(2):
                    row = ref[child : child + 1, 0:128].astype(jnp.float32)
                    for block in range(1, ref.shape[1] // 128):
                        other = ref[child : child + 1, 128 * block : 128 * block + 128]
                        row = jnp.where(offset // 128 == block, other.astype(jnp.float32), row)
                    row = pltpu.roll(
                        jnp.broadcast_to(row, shape), (at + 256 - offset % 128) % 128, 1
                    )
                    total = jnp.where((lane >= at) & (lane < at + width), row, total)
                    at += width
            return total

        frac = packed(frac_one, frac_two)
        base = packed(base_one, base_two)
        slope = 0.5 * (packed(shift_one, shift_two) + frac)
        row = row_ids(shape).astype(jnp.float32)
        spread = (row - 3.0) - frac
        turned = jnp.pi * spread
        still = turned == 0.0
        safe = jnp.where(still, 1.0, turned)
        weights = jnp.where(still, 1.0, jnp.sin(safe) / safe) * (
            0.54 + 0.46 * jnp.cos(jnp.pi * spread / 4.0)
        )
        count = taps_ref.shape[0]
        square = (128, 128)
        base_rows = jnp.broadcast_to(base[0:1], square).T[:count]
        slope_rows = jnp.broadcast_to(slope[0:1], square).T[:count]
        wide = lane_ids((count, 128))
        spot = (wide & (COLS - 1)) * ROWS + (first_bin - LEFT)
        angle = base_rows + slope_rows * (spot.astype(jnp.float32) / bin_total - 0.5)
        cos_col, sin_col = jnp.cos(angle), jnp.sin(angle)
        sign = jnp.where(lane < COLS, -1.0, 1.0)
        fine, coarse = slope * (row / bin_total), slope * (8.0 / bin_total)
        cos_fine, sin_fine = jnp.cos(fine), jnp.sin(fine)
        cos_coarse, sin_coarse = jnp.cos(coarse), jnp.sin(coarse)
        for place in range(count):

            def spread_out(table):
                return jnp.broadcast_to(table[:, place : place + 1], shape)

            taps_ref[place] = spread_out(weights)
            cos_all = jnp.broadcast_to(cos_col[place : place + 1], shape)
            sin_all = jnp.broadcast_to(sin_col[place : place + 1], shape) * sign
            cos_step, sin_step = spread_out(cos_fine), spread_out(sin_fine) * sign
            cos_next, sin_next = spread_out(cos_coarse), spread_out(sin_coarse) * sign
            twice = cos_next + cos_next
            before = None
            for chunk in range(CHUNKS):
                if chunk < 2:
                    now = (
                        cos_all * cos_step - sin_all * sin_step,
                        sin_all * cos_step + cos_all * sin_step,
                    )
                else:
                    now = (twice * cos_all - before[0], twice * sin_all - before[1])
                before = (cos_all, sin_all)
                cos_all, sin_all = now
                turn_ref[place, 0, pl.ds(8 * chunk, 8), :] = cos_all
                turn_ref[place, 1, pl.ds(8 * chunk, 8), :] = sin_all
                cos_step, sin_step = cos_next, sin_next

    return kernel


def compress_pair(near, far, bins, band_ref, source, columns, images, inside):
    rest = source.shape[2] - LEFT - bins
    wide = near[0].shape[2] - LEFT - bins

    def piece(held, comp, at, size):
        if len(held) == 1:
            return held[0][comp, :, pl.ds(at, size)]
        main, rim = held
        if at == LEFT:
            return main[comp]
        return rim[comp, :, pl.ds(min(at, LEFT), size)]

    for comp in range(2):
        for at, size in ((0, LEFT), (LEFT, bins), (LEFT + bins, wide)):
            sides = [piece(held, comp, at, size).astype(jnp.float32) for held in (near, far)]
            source[comp, :, pl.ds(at, size)] = jnp.concatenate(sides, axis=0).astype(jnp.bfloat16)
        if rest > wide:
            source[comp, :, pl.ds(LEFT + bins + wide, rest - wide)] = jnp.zeros(
                (16, rest - wide), jnp.bfloat16
            )
    span = band_ref.shape[0]
    windows = jnp.concatenate(
        [
            source[comp, :, pl.ds(WIDE * u + STEP * block, span)]
            for block in range(BLOCKS)
            for comp in range(2)
            for u in range(SPANS)
        ],
        axis=0,
    )
    product = jnp.dot(windows, band_ref[...], preferred_element_type=jnp.float32)
    half = 16 * SPANS
    for block in range(BLOCKS):
        top = product[128 * block : 128 * block + half]
        low = product[128 * block + half : 128 * block + 128]
        result = jnp.concatenate(
            [top[:, :STEP] + low[:, STEP:], low[:, :STEP] - top[:, STEP:]], axis=0
        )
        columns[pl.ds(STEP * block, STEP), :] = result.astype(jnp.bfloat16).T.astype(jnp.float32)
    for chunk in range(0, CHUNKS, 2):
        size = min(2, CHUNKS - chunk) * 8
        parts = [columns[pl.ds(ROWS * g + 8 * chunk, size), :] for g in range(GROUPS)]
        parts = exchange([part.astype(jnp.bfloat16) for part in parts])
        for image, part in enumerate(parts):
            part = part.astype(jnp.float32)
            for extra in range(size // 8):
                value = inside(chunk + extra, part[8 * extra : 8 * extra + 8])
                store_rimmed(images, image, chunk + extra, value)


def contribution(images, tables, parent, child, first_parent, first_image, width, at):
    beam_ref, shift_ref, taps_ref, turn_ref = tables
    place = at + child * width + parent
    image = beam_ref[child, first_parent + parent] + first_image
    start = shift_ref[child, first_parent + parent] + (RIM - 3)
    value = None
    for tap in range(8):
        term = images[image, pl.ds(start + tap, ROWS), :] * taps_ref[place, pl.ds(tap, 1), :]
        value = term if value is None else value + term
    parts = []
    for chunk in range(CHUNKS):
        part = value[8 * chunk : 8 * chunk + 8]
        parts.append(
            part * turn_ref[place, 0, pl.ds(8 * chunk, 8), :]
            + pltpu.roll(part, COLS, 1) * turn_ref[place, 1, pl.ds(8 * chunk, 8), :]
        )
    return parts


def loop_over(count, one):
    size = min(TOGETHER, count)

    def step(index, carry):
        for extra in range(size):
            one(size * index + extra)
        return carry

    lax.fori_loop(0, count // size, step, 0)


def merge_one(images, tables, result, inside):
    own, low, _ = position()

    def one(parent):
        sides = [
            contribution(
                images, tables, parent, child, ONE * own, (child ^ low) * 8 - 8 * own, ONE, 0
            )
            for child in range(2)
        ]
        for chunk, (a, b) in enumerate(zip(*sides)):
            store_rimmed(result, parent, chunk, inside(chunk, a + b))

    loop_over(ONE, one)


def second_side(images, tables, parent, child):
    own, _, _ = position()
    return contribution(images, tables, parent, child, TWO * own, -ONE * own, TWO, 2 * ONE)


def first_kernel(bins):
    def kernel(
        far_beam_one, far_shift_one, far_beam_two, far_shift_two, a0, a1, r1, band_ref, taps_ref,
        turn_ref, out_ref, source, columns, images, level_one, beam_one, shift_one, beam_two,
        shift_two, sems,
    ):
        inside = inside_test(bins)
        copies = fetch(
            (far_beam_one, far_shift_one, far_beam_two, far_shift_two),
            (beam_one, shift_one, beam_two, shift_two), sems,
        )
        compress_pair((a0,), (a1, r1), bins, band_ref, source, columns, images, inside)
        arrived(copies)
        merge_one(images, (beam_one, shift_one, taps_ref, turn_ref), level_one, inside)
        _, _, high = position()
        tables = (beam_two, shift_two, taps_ref, turn_ref)

        def one(parent):
            for chunk, part in enumerate(second_side(level_one, tables, parent, high)):
                out_ref[parent, pl.ds(8 * chunk, 8), :] = part

        loop_over(TWO, one)

    return kernel


def second_kernel(bins):
    def kernel(
        far_beam_one, far_shift_one, far_beam_two, far_shift_two, a2, a3, r3, band_ref, taps_ref,
        turn_ref, half_ref, out_ref, source, columns, images, level_one, beam_one, shift_one,
        beam_two, shift_two, sems, level_two,
    ):
        inside = inside_test(bins)
        copies = fetch(
            (far_beam_one, far_shift_one, far_beam_two, far_shift_two),
            (beam_one, shift_one, beam_two, shift_two), sems,
        )
        compress_pair((a2,), (a3, r3), bins, band_ref, source, columns, images, inside)
        arrived(copies)
        merge_one(images, (beam_one, shift_one, taps_ref, turn_ref), level_one, inside)
        _, _, high = position()
        tables = (beam_two, shift_two, taps_ref, turn_ref)

        def one(parent):
            for chunk, part in enumerate(second_side(level_one, tables, parent, 1 - high)):
                rows = pl.ds(8 * chunk, 8)
                level_two[parent, rows, :] = part + half_ref[parent, rows, :]

        loop_over(TWO, one)
        for half in range(2):
            for chunk in range(0, CHUNKS, 2):
                size = min(2, CHUNKS - chunk) * 8
                parts = [
                    level_two[16 * half + image, pl.ds(8 * chunk, size), :].astype(jnp.bfloat16)
                    for image in range(GROUPS)
                ]
                for g, part in enumerate(exchange(parts)):
                    columns[pl.ds(ROWS * g + 8 * chunk, size), :] = part.astype(jnp.float32)
            for block in range(BLOCKS):
                turned = columns[pl.ds(STEP * block, STEP), :].astype(jnp.bfloat16).T
                for comp in range(2):
                    for u in range(SPANS):
                        left = WIDE * u + STEP * block - LEFT
                        if 0 <= left < bins:
                            row = (comp * SPANS + u) * 16
                            out_ref[comp, pl.ds(16 * half, 16), pl.ds(left, 128)] = turned[
                                row : row + 16
                            ]

    return kernel


def neighbours(head, tail, axis):
    count = lax.axis_size(axis)
    even = lax.axis_index(axis) % 2 == 0
    near = [(i, i ^ 1) for i in range(count) if i ^ 1 < count]
    far = [(i + 1, i + 2) for i in range(0, count - 2, 2)]
    far = far + [(b, a) for a, b in far]
    first = lax.ppermute(jnp.where(even, tail, head), axis, near)
    second = lax.ppermute(jnp.where(even, head, tail), axis, far) if far else jnp.zeros_like(first)
    return jnp.where(even, second, first), jnp.where(even, first, second)


def body(
    echo, chirp, beam_one, shift_one, frac_one, base_one, beam_two, shift_two, frac_two, base_two
):
    signal = echo[0]
    beams, _, bins = signal.shape
    span = STEP + chirp.shape[1]
    pulse = lax.axis_index("pulse")

    signal = signal.reshape(4, beams // 4, 2, bins).transpose(0, 2, 1, 3)
    small = (
        chirp, beam_one, shift_one, frac_one, base_one, beam_two, shift_two, frac_two, base_two
    )
    chirp, beam_one, shift_one, frac_one, base_one, beam_two, shift_two, frac_two, base_two = (
        pltpu.with_memory_space_constraint(array, pltpu.HBM) for array in small
    )

    def block_of(array, mask):
        index = pulse ^ mask
        return lax.dynamic_index_in_dim(array, 2 * (index % 2) + index // 2 % 2, 0, keepdims=False)

    def sent(array, mask):
        count = lax.axis_size("pulse")
        return lax.ppermute(array, "pulse", [(i, i ^ mask) for i in range(count)])

    far_main = sent(block_of(signal, 3), 3)
    near_main = sent(block_of(signal, 1), 1)
    from_left, from_right = neighbours(
        signal[:, :, :, :span], signal[:, :, :, bins - span :], "range"
    )
    from_left = from_left[:, :, :, span - LEFT :]
    wide = jnp.concatenate([from_left, signal, from_right], axis=3)
    rims = jnp.concatenate([from_left, from_right], axis=3)
    middle = sent(block_of(wide, 2), 2)
    near_rim = sent(block_of(rims, 1), 1)
    far_rim = sent(block_of(rims, 3), 3)

    vmem = pl.BlockSpec(memory_space=pltpu.VMEM)
    far = pl.BlockSpec(memory_space=pltpu.HBM)

    def held(space, *arrays):
        return [space(a.shape, a.dtype) for a in arrays] + [
            pltpu.SemaphoreType.DMA((len(arrays),))
        ]

    params = pltpu.CompilerParams(vmem_limit_bytes=24 << 20)
    count = 2 * (ONE + TWO)
    band, taps, turns = pl.pallas_call(
        prep_kernel(bins),
        out_shape=(
            jax.ShapeDtypeStruct((span, 2 * STEP), jnp.bfloat16),
            jax.ShapeDtypeStruct((count, 8, 128), jnp.float32),
            jax.ShapeDtypeStruct((count, 2, ROWS, 128), jnp.float32),
        ),
        in_specs=[far] * 7,
        out_specs=(vmem,) * 3,
        scratch_shapes=held(
            pltpu.VMEM, chirp, shift_one, frac_one, base_one, shift_two, frac_two, base_two
        ),
        compiler_params=params,
        name="prepare",
    )(chirp, shift_one, frac_one, base_one, shift_two, frac_two, base_two)

    index_tables = (beam_one, shift_one, beam_two, shift_two)
    scratch = [
        pltpu.VMEM((2, 16, SPANS * WIDE + span - STEP), jnp.bfloat16),
        pltpu.VMEM((WIDE, 128), jnp.float32),
        pltpu.VMEM((16, TALL, 128), jnp.float32),
        pltpu.VMEM((ONE, TALL, 128), jnp.float32),
    ] + held(pltpu.SMEM, *index_tables)
    half = pl.pallas_call(
        first_kernel(bins),
        out_shape=jax.ShapeDtypeStruct((TWO, ROWS, 128), jnp.float32),
        in_specs=[far] * 4 + [vmem] * 6,
        out_specs=vmem,
        scratch_shapes=scratch,
        compiler_params=params,
        name="first_pair",
    )(*index_tables, block_of(wide, 0), near_main, near_rim, band, taps, turns)
    image = pl.pallas_call(
        second_kernel(bins),
        out_shape=jax.ShapeDtypeStruct((2, TWO, bins), jnp.bfloat16),
        in_specs=[far] * 4 + [vmem] * 7,
        out_specs=vmem,
        scratch_shapes=scratch + [pltpu.VMEM((TWO, ROWS, 128), jnp.float32)],
        compiler_params=params,
        name="second_pair",
    )(*index_tables, middle, far_main, far_rim, band, taps, turns, half)
    return image.transpose(1, 0, 2)[None, None]


def solution(mesh):
    in_specs = (P(("scene", "pulse"), "rep", None, "range"),) + (P(),) * 9
    out_specs = P("rep", ("scene", "pulse"), None, None, "range")

    return jax.shard_map(body, mesh=mesh, in_specs=in_specs, out_specs=out_specs, check_vma=False)
```
